32 devices in a mesh: dp: 4 (over z), seq: 8 (over y, x, core).
Axes of the slice: x: 2, y: 2, z: 4, core: 2. Of those that a mesh axis runs over, the one named last changes fastest.
Arguments:
- hidden: bfloat16 [4096, 2048], P(('dp', 'seq')), may hold values from -6 to 6
- cotangent: bfloat16 [4096, 2048], P(('dp', 'seq')), may hold values from -6 to 6
- attn_gain: bfloat16 [2048], P(('dp', 'seq')), may hold values from 0.25 to 1.75
- q_weight: bfloat16 [2048, 3072], P(('dp', 'seq')), may hold values from -0.125 to 0.125
- kv_down: bfloat16 [2048, 576], P(('dp', 'seq')), may hold values from -0.125 to 0.125
- kv_gain: bfloat16 [512], P(('dp', 'seq')), may hold values from 0.25 to 1.75
- kv_up: bfloat16 [512, 4096], P(('dp', 'seq')), may hold values from -0.25 to 0.25
- out_weight: bfloat16 [2048, 2048], P(('dp', 'seq')), may hold values from -2 to 2
- ffn_gain: bfloat16 [2048], P(('dp', 'seq')), may hold values from 0.25 to 1.75
- shared_gate_up: bfloat16 [2048, 5632], P(('dp', 'seq')), may hold values from -0.125 to 0.125
- shared_down: bfloat16 [2816, 2048], P(('dp', 'seq')), may hold values from -0.109375 to 0.109375
- expert_gate_up: bfloat16 [2048, 16, 2816], P('dp', 'seq'), may hold values from -0.125 to 0.125
- expert_down: bfloat16 [1408, 16, 2048], P('dp', 'seq'), may hold values from -0.15625 to 0.15625
- expert_ids: int32 [4096, 6], P('dp'), may hold values from 0 to 15, all different within a row; in each aligned block of 128 rows (0 to 127, 128 to 255, ...) at most 96 rows name the same one
- gate_fix: int32 [4096, 6], P(('dp', 'seq')), may hold values from 1024 to 8191
- block_ids: int32 [4, 1024], P('dp'), may hold values from 0 to 7, never falling along the last dimension, each value on 1 to 256 neighbouring positions
Outputs:
- output: bfloat16 [4096, 2048], P(('dp', 'seq'))
- d_hidden: float32 [4096, 2048], P(('dp', 'seq'))
- d_attn_gain: float32 [2048], P(('dp', 'seq'))
- d_q_weight: float32 [2048, 3072], P(('dp', 'seq'))
- d_kv_down: float32 [2048, 576], P(('dp', 'seq'))
- d_kv_gain: float32 [512], P(('dp', 'seq'))
- d_kv_up: float32 [512, 4096], P(('dp', 'seq'))
- d_out_weight: float32 [2048, 2048], P(('dp', 'seq'))
- d_ffn_gain: float32 [2048], P(('dp', 'seq'))
- d_shared_gate_up: float32 [2048, 5632], P(('dp', 'seq'))
- d_shared_down: float32 [2816, 2048], P(('dp', 'seq'))
- d_expert_gate_up: float32 [2048, 16, 2816], P('dp', 'seq')
- d_expert_down: float32 [1408, 16, 2048], P('dp', 'seq')
The draws below stay inside these ranges and needn't reach their ends.
Inputs may be any that keep to these rules, and one draw needn't show every extreme that they name: `expert_ids`: each row names 6 different experts; within each aligned block of 128 rows (the rows of one device) no expert is named by more than 96 rows. `block_ids`: along each sequence the block number never falls, and each block spans 1 to 256 positions.
All inputs are finite; a program needn't handle non-finite values.
Results may differ from the reference program's by a relative error of at most 0.018.
Values may be sent and summed in bfloat16 or wider, within the bound.
No kernel may reach another device: no remote copies, remote signals or barrier semaphores. Data moves between devices by JAX's collectives and lax.ppermute only.
A program may use at most 448 MiB of HBM per device.

```python
import math
import jax
import jax.numpy as jnp
import numpy as np
from jax import lax

D = 2048
H = 16
NOPE = 128
ROPE = 64
VD = 128
KV_RANK = 512
FF = 1408
TOP = 6
SH = 2816
EXP_DEV = 2
EXPERTS = 16
TOK_DEV = 128
SEQ_LEN = 1024
BLOCK = 256
SEQS_ALL = 4
TOKENS = 4096
MOST = 96
BLOCKS_SEQ = 8
N_DP = 4
N_SEQ = 8


def place_ends(drawn, stream_key, smallest, high):
    shape = drawn.shape
    index_at = [jax.random.randint(jax.random.fold_in(stream_key, axis), (), 0, shape[axis]) for axis in range(len(shape))]
    drawn = drawn.at[tuple(index_at)].set(smallest)
    longest = shape.index(max(shape))
    index_at[longest] = (index_at[longest] + 1) % shape[longest]
    return drawn.at[tuple(index_at)].set(high)


def block_scale(rng, shape, cuts, least, largest):
    def one(axis_at, blocks):
        steps = jax.random.uniform(jax.random.fold_in(jax.random.fold_in(rng, 6), axis_at), (blocks,), jnp.float32, least / len(cuts), largest / len(cuts))
        return jnp.repeat(jnp.exp(steps), shape[axis_at] // blocks).reshape((-1,) + (1,) * (len(shape) - axis_at - 1))

    level = one(*cuts[0])
    for cut in cuts[1:]:
        level = level * one(*cut)
    return level


def profile(number_of, total, reach, lean):
    portions = [(1 << 20) // math.isqrt(rank ** lean) + 1 for rank in range(2, number_of + 1)]
    spare, given = total - reach - (number_of - 1), [1] * (number_of - 1)
    while spare > 0:
        free = [i for i in range(number_of - 1) if given[i] < reach]
        whole, left = sum([portions[i] for i in free]), spare
        for i in free:
            extra = min(reach - given[i], max(1, left * portions[i] // whole), spare)
            given[i] = given[i] + extra
            spare = spare - extra
    return np.array([reach] + given)


def uneven(key, count, total, most, lean):
    if count == 2:
        one = jax.random.randint(key, (), max(1, total - most), min(most, total - 1) + 1)
        return jnp.stack([one, total - one])
    lengths = jnp.asarray(profile(count, total, most, lean), jnp.int32)
    pairs = (count - 1) // 2
    source_of, receiver = lengths[1:1 + 2 * pairs:2], lengths[2:2 + 2 * pairs:2]
    slack = jnp.minimum(source_of - 1, most - receiver)
    passed = jax.random.randint(jax.random.fold_in(key, 1), (pairs,), 0, 1 << 20) % (slack + 1)
    lengths = lengths.at[1:1 + 2 * pairs:2].set(source_of - passed).at[2:2 + 2 * pairs:2].set(receiver + passed)
    return lengths[jax.random.permutation(jax.random.fold_in(key, 2), count)]


def deal_out(own_key, own, number, rows, amount, top, bound, lean):
    order = jax.random.permutation(own_key, amount)
    crowded, common = load_shares(amount, rows * top, bound, lean, True), load_shares(amount, rows * top, bound, lean, False)
    places = jnp.arange(amount)

    def named(sizes, offset_by):
        used = int((sizes > 0).sum())
        fixed = max(1, used // 4)
        passed = fixed + (places - fixed + offset_by * (used - fixed)) % max(1, amount - fixed)
        return jnp.zeros((amount,), jnp.int32).at[order[jnp.where(places < fixed, places, passed)]].set(jnp.asarray(sizes, jnp.int32))

    sizes = jnp.where(number % 4 == 0, named(crowded, number // 4), named(common, number - number // 4 - 1))
    mixed = jax.random.permutation(jax.random.fold_in(own, 3), amount)
    source_of, receiver = mixed[0:amount // 2 * 2:2], mixed[1:amount // 2 * 2:2]
    margin = jnp.minimum(sizes[source_of] - 1, bound - sizes[receiver]) // 2
    margin = jnp.where((source_of == order[0]) | (receiver == order[0]) | (sizes[receiver] == 0), 0, jnp.maximum(margin, 0))
    passed = jax.random.randint(jax.random.fold_in(own, 4), (amount // 2,), 0, 1 << 20) % (margin + 1)
    sizes = sizes.at[source_of].add(-passed).at[receiver].add(passed)
    items = jnp.searchsorted(jnp.cumsum(sizes), jnp.arange(rows * top), side="right").astype(jnp.int32)
    listing = items.reshape(top, rows).T
    listing = listing[jax.random.permutation(jax.random.fold_in(own, 1), rows)]
    offset_by = jax.random.randint(jax.random.fold_in(own, 2), (rows, 1), 0, top)
    return jnp.take_along_axis(listing, (jnp.arange(top)[None, :] + offset_by) % top, axis=1)


def load_shares(number_of, total, limit, skew, full):
    weights = [(1 << 20) // math.isqrt(standing ** skew) + 1 for standing in range(1, number_of + 1)]
    largest = limit if full else min(limit, max(-(-total // number_of), total * weights[0] // sum(weights)))
    least = 1 if total - largest >= number_of - 1 else 0
    holding, rest = [largest] + [least] * (number_of - 1), total - largest - least * (number_of - 1)
    while rest > 0:
        movable = [i for i in range(1, number_of) if holding[i] < largest] or [i for i in range(1, number_of) if holding[i] < limit]
        pool, remaining = sum([weights[i] for i in movable]), rest
        for i in movable:
            addition = min(limit - holding[i], max(1, remaining * weights[i] // pool), rest)
            holding[i] = holding[i] + addition
            rest = rest - addition
    return np.array(holding)


def scatter_about(key, shape, deviation, reach, split=(), kind=jnp.bfloat16):
    values = jax.random.normal(key, shape, jnp.float32) * deviation
    if len(split) > 0:
        values = block_scale(key, shape, split, -0.22, 0.18) * values
    return jnp.clip(values, min=-reach, max=reach).astype(kind)


def setup_inputs(seed: int = 0) -> dict:
    keys = jax.random.split(jax.random.key(seed), 17)
    hidden = scatter_about(keys[0], (TOKENS, D), 1.0, 6.0, ((0, 32),))
    cotangent = scatter_about(keys[1], (TOKENS, D), 1.0, 6.0, ((0, 32),))
    attn_gain = jnp.clip(1.0 + 0.15 * jax.random.normal(keys[2], (D,), jnp.float32), 0.25, 1.75).astype(jnp.bfloat16)
    q_weight = scatter_about(keys[3], (D, H * (NOPE + ROPE)), D ** -0.5, 0.125, ((0, 32),))
    kv_down = scatter_about(keys[4], (D, KV_RANK + ROPE), D ** -0.5, 0.125, ((0, 32),))
    kv_gain = jnp.clip(1.0 + 0.15 * jax.random.normal(keys[5], (KV_RANK,), jnp.float32), 0.25, 1.75).astype(jnp.bfloat16)
    kv_up = scatter_about(keys[6], (KV_RANK, H * (NOPE + VD)), KV_RANK ** -0.5, 0.25, ((0, 32),))
    out_weight = scatter_about(keys[7], (H * VD, D), (max(H * VD // 256, 1)) ** -0.5, 2.0, ((0, 32),))
    ffn_gain = jnp.clip(1.0 + 0.15 * jax.random.normal(keys[8], (D,), jnp.float32), 0.25, 1.75).astype(jnp.bfloat16)
    shared_gate_up = scatter_about(keys[9], (D, 2 * SH), D ** -0.5, 0.125, ((0, 32),))
    shared_down = scatter_about(keys[10], (SH, D), SH ** -0.5, 0.109375, ((0, 32),))
    expert_gate_up = scatter_about(keys[11], (D, EXPERTS, 2 * FF), D ** -0.5, 0.125, ((0, 4), (1, 8)))
    expert_down = scatter_about(keys[12], (FF, EXPERTS, D), FF ** -0.5, 0.15625, ((0, 4), (1, 8)))
    expert_ids_keys = jax.random.split(jax.random.fold_in(keys[13], 1), TOKENS // TOK_DEV)
    expert_ids_turns = jax.random.permutation(jax.random.fold_in(keys[13], 3), TOKENS // TOK_DEV)
    expert_ids = jax.vmap(lambda own, number: deal_out(jax.random.fold_in(keys[13], 2), own, number, TOK_DEV, EXPERTS, TOP, MOST, 2))(expert_ids_keys, expert_ids_turns).reshape((TOKENS, TOP))
    gate_fix = place_ends(jax.random.randint(keys[14], (TOKENS, TOP), 1024, 8192), jax.random.fold_in(keys[14], 1), 1024, 8191).astype(jnp.int32)
    block_ids = jax.vmap(lambda own: jnp.searchsorted(jnp.cumsum(uneven(own, BLOCKS_SEQ, SEQ_LEN, BLOCK, 1)), jnp.arange(SEQ_LEN), side="right"))(jax.random.split(keys[15], SEQS_ALL)).reshape((SEQS_ALL, SEQ_LEN)).astype(jnp.int32)
    return {"hidden": hidden, "cotangent": cotangent, "attn_gain": attn_gain, "q_weight": q_weight, "kv_down": kv_down, "kv_gain": kv_gain, "kv_up": kv_up, "out_weight": out_weight, "ffn_gain": ffn_gain, "shared_gate_up": shared_gate_up, "shared_down": shared_down, "expert_gate_up": expert_gate_up, "expert_down": expert_down, "expert_ids": expert_ids, "gate_fix": gate_fix, "block_ids": block_ids}


@jax.custom_vjp
def low(v):
    return lax.optimization_barrier(v.astype(jnp.bfloat16)).astype(jnp.float32)

@jax.custom_vjp
def low_back(v):
    return v

def low_keep(v):
    return (low(v), None)

def low_pass(kept, grad):
    return (grad,)

def back_keep(v):
    return (v, None)

def back_low(kept, grad):
    return (low(grad),)
low.defvjp(low_keep, low_pass)
low_back.defvjp(back_keep, back_low)
EPS = 1e-06
THETA = 10000.0
GATE_UNIT = 16384.0
HIGH = lax.Precision.HIGHEST

def matmul(left_side, right_side):
    return jnp.dot(left_side, right_side, precision=HIGH)

def rms_norm(values, scale_vec):
    return values * lax.rsqrt(lax.optimization_barrier(jnp.mean(values * values, axis=-1, keepdims=True)) + EPS) * scale_vec

def swiglu(joined):
    half_width = joined.shape[-1] // 2
    return jax.nn.silu(joined[..., :half_width]) * joined[..., half_width:]

def rotary_tables(positions):
    half_width = ROPE // 2
    frequency = THETA ** (-jnp.arange(half_width, dtype=jnp.float32) * 2.0 / ROPE)
    angles = positions.astype(jnp.float32)[:, None] * frequency[None, :]
    return (jnp.cos(angles), jnp.sin(angles))

def rotate(values, cosine, sine_table):
    half_width = values.shape[-1] // 2
    leading = values[..., :half_width]
    trailing = values[..., half_width:]
    return jnp.concatenate([leading * cosine - trailing * sine_table, trailing * cosine + leading * sine_table], axis=-1)

def assemble(query_in, rope_in, expand_in, cosine, sine_table):
    tokens = query_in.shape[0]
    query_heads = query_in.reshape(tokens, H, NOPE + ROPE)
    expand_heads = expand_in.reshape(tokens, H, NOPE + VD)
    query_rot = rotate(query_heads[..., NOPE:], cosine[:, None, :], sine_table[:, None, :])
    key_rot = jnp.broadcast_to(rotate(rope_in, cosine, sine_table)[:, None, :], (tokens, H, ROPE))
    return jnp.concatenate([query_heads[..., :NOPE], query_rot, expand_heads[..., :NOPE], key_rot, expand_heads[..., NOPE:]], axis=-1)

def attend(packed, blocks):
    head_width = NOPE + ROPE
    queries = packed[..., :head_width]
    key_rows = packed[..., head_width:2 * head_width]
    values = packed[..., 2 * head_width:]
    scores = jnp.einsum('qhd,khd->hqk', queries, key_rows, precision=HIGH) * head_width ** (-0.5)
    scores = low_back(scores)
    allowed = blocks[None, :] <= blocks[:, None]
    scores = jnp.where(allowed[None, :, :], scores, -1e+30)
    row_max = lax.optimization_barrier(jnp.max(scores, axis=-1, keepdims=True))
    weights = jnp.exp(scores - row_max)
    shares = weights / lax.optimization_barrier(jnp.sum(weights, axis=-1, keepdims=True))
    return jnp.einsum('hqk,khd->qhd', low(shares), values, precision=HIGH)

def route_experts(normed_ffn, expert_pick, gate_values, expert_gate_up, expert_down):
    group_tokens = normed_ffn.shape[0]
    experts = expert_gate_up.shape[1]
    capacity = TOP * TOK_DEV // EXP_DEV
    labels = jnp.arange(experts, dtype=jnp.int32)
    pair_hits = lax.optimization_barrier(jnp.sum((expert_pick[:, :, None] == labels[None, None, :]).astype(jnp.int32), axis=1)).astype(jnp.int32)
    before = (jnp.cumsum(pair_hits, axis=0).astype(jnp.int32) - pair_hits).astype(jnp.int32)
    slot_of = jnp.take_along_axis(before, expert_pick, axis=1).astype(jnp.int32)
    owners = jnp.broadcast_to(jnp.arange(group_tokens, dtype=jnp.int32)[:, None], expert_pick.shape)
    slot_table = jnp.full((experts, capacity), group_tokens, jnp.int32).at[expert_pick, slot_of].set(owners, mode='drop')
    padded = jnp.concatenate([normed_ffn, jnp.zeros((1, normed_ffn.shape[1]), jnp.float32)], axis=0)
    slot_rows = low_back(padded[slot_table])
    gate_up = low_back(jnp.einsum('ecd,def->ecf', slot_rows, expert_gate_up, precision=HIGH))
    hidden_act = low(swiglu(gate_up))
    produced = low_back(low(jnp.einsum('ecf,fed->ecd', hidden_act, expert_down, precision=HIGH)))
    kept_pair = slot_of < capacity
    flat_index = jnp.where(kept_pair, expert_pick * capacity + slot_of, 0).astype(jnp.int32)
    picked = produced.reshape(experts * capacity, -1)[flat_index] * kept_pair[:, :, None].astype(jnp.float32)
    return lax.optimization_barrier(jnp.sum(gate_values[:, :, None] * picked, axis=1))

def group_forward(weights, group_items):
    attn_gain, q_weight, kv_down, kv_gain, kv_up, out_weight, ffn_gain, shared_gate_up, shared_down, expert_gate_up, expert_down = weights
    row_values, expert_pick, gate_values, blocks = group_items
    group_tokens = row_values.shape[0]
    part_length = SEQ_LEN // N_SEQ
    sequences = blocks.shape[0]
    row_number = jnp.arange(group_tokens, dtype=jnp.int32)
    positions = row_number // TOK_DEV * part_length + row_number % part_length
    cosine, sine_table = rotary_tables(positions)
    normed = low(rms_norm(row_values, attn_gain))
    queries = low_back(matmul(normed, q_weight))
    latent_in = low_back(matmul(normed, kv_down))
    latent = low(rms_norm(latent_in[:, :KV_RANK], kv_gain))
    expanded = low_back(matmul(latent, kv_up))
    packed = low_back(low(assemble(queries, latent_in[:, KV_RANK:], expanded, cosine, sine_table)))
    by_seq = packed.reshape(N_SEQ, sequences, part_length, H, -1).transpose(1, 0, 2, 3, 4).reshape(sequences, SEQ_LEN, H, -1)
    attended = lax.map(jax.checkpoint(lambda operands: attend(operands[0], operands[1])), (by_seq, blocks))
    heads_out = attended.reshape(sequences, N_SEQ, part_length, H * VD).transpose(1, 0, 2, 3).reshape(group_tokens, H * VD)
    heads_out = low_back(low(heads_out))
    residual = row_values + low_back(matmul(heads_out, out_weight))
    normed_ffn = low(rms_norm(residual, ffn_gain))
    shared = low_back(matmul(low(swiglu(low_back(matmul(normed_ffn, shared_gate_up)))), shared_down))
    routed = route_experts(normed_ffn, expert_pick, gate_values, expert_gate_up, expert_down)
    return residual + shared + routed

def reference(hidden, cotangent, attn_gain, q_weight, kv_down, kv_gain, kv_up, out_weight, ffn_gain, shared_gate_up, shared_down, expert_gate_up, expert_down, expert_ids, gate_fix, block_ids):
    group_tokens = TOK_DEV * N_SEQ
    params = tuple((weight.astype(jnp.float32) for weight in (attn_gain, q_weight, kv_down, kv_gain, kv_up, out_weight, ffn_gain, shared_gate_up, shared_down, expert_gate_up, expert_down)))
    row_values = hidden.astype(jnp.float32).reshape(N_DP, group_tokens, -1)
    expert_pick = expert_ids.reshape(N_DP, group_tokens, TOP)
    gate_values = gate_fix.astype(jnp.float32).reshape(N_DP, group_tokens, TOP) / GATE_UNIT
    blocks = block_ids.reshape(N_DP, -1, SEQ_LEN)

    def whole(rows_in, *weights):
        group_step = jax.checkpoint(lambda group_items: group_forward(weights, group_items))
        return lax.map(group_step, (rows_in, expert_pick, gate_values, blocks))
    result, pullback = jax.vjp(whole, row_values, *params)
    gradients = pullback(cotangent.astype(jnp.float32).reshape(N_DP, group_tokens, -1))
    output = result.reshape(TOKENS, -1).astype(jnp.bfloat16)
    d_rows = gradients[0].reshape(TOKENS, -1)
    return (output, d_rows, gradients[1], gradients[2], gradients[3], gradients[4], gradients[5], gradients[6], gradients[7], gradients[8], gradients[9], gradients[10], gradients[11])
```

```python
import jax
import jax.numpy as jnp
from jax import lax
from jax.sharding import PartitionSpec as P

H = 16
NOPE = 128
ROPE = 64
VD = 128
KV_RANK = 512
TOP = 6

EPS = 1e-06
THETA = 10000.0
GATE_UNIT = 16384.0

BOTH = ("dp", "seq")
F32 = jnp.float32
BF16 = jnp.bfloat16


def contract(left_side, right_side, left_dim, right_dim):
    return lax.dot_general(
        left_side,
        right_side,
        (((left_dim,), (right_dim,)), ((), ())),
        preferred_element_type=F32,
    )


def matmul(left_side, right_side):
    return contract(left_side, right_side, left_side.ndim - 1, 0)


def lead_dot(left_side, right_side):
    return contract(left_side, right_side, 0, 0)


def tail_dot(left_side, right_side):
    return contract(left_side, right_side, 1, 1)


def rms_scale(values):
    return lax.rsqrt(jnp.mean(values * values, axis=-1, keepdims=True) + EPS)


def rms_back(values, gain, grad):
    scale = rms_scale(values)
    unit = values * scale
    weighted = grad * gain
    centre = jnp.mean(weighted * unit, axis=-1, keepdims=True)
    return scale * (weighted - unit * centre), jnp.sum(grad * unit, axis=0)


def swiglu(gate, up):
    return jax.nn.silu(gate) * up


def swiglu_back(gate, up, grad):
    sig = jax.nn.sigmoid(gate)
    return grad * up * sig * (1.0 + gate * (1.0 - sig)), grad * (gate * sig)


def rotary_tables(positions):
    half_width = ROPE // 2
    frequency = THETA ** (-jnp.arange(half_width, dtype=F32) * 2.0 / ROPE)
    angles = positions.astype(F32)[:, None] * frequency[None, :]
    return jnp.cos(angles), jnp.sin(angles)


def rotate(values, cosine, sine):
    half_width = values.shape[-1] // 2
    lead = values[..., :half_width]
    trail = values[..., half_width:]
    return jnp.concatenate([lead * cosine - trail * sine, trail * cosine + lead * sine], axis=-1)


def rotate_back(grads, cosine, sine):
    return rotate(grads, cosine, -sine)


def scatter_sum(values, axis_name, parts):
    moved = lax.all_to_all(values.astype(BF16), axis_name, split_axis=0, concat_axis=0, tiled=True)
    return jnp.sum(moved.reshape((parts, -1) + values.shape[1:]).astype(F32), axis=0)


def body(
    hidden,
    cotangent,
    attn_gain,
    q_weight,
    kv_down,
    kv_gain,
    kv_up,
    out_weight,
    ffn_gain,
    shared_gate_up,
    shared_down,
    expert_gate_up,
    expert_down,
    expert_ids,
    gate_fix,
    block_ids,
):
    n_dp = lax.axis_size("dp")
    n_seq = lax.axis_size("seq")
    n_all = n_dp * n_seq
    dp_index = lax.axis_index("dp")
    seq_index = lax.axis_index("seq")
    tokens, width = hidden.shape
    sequences, length = block_ids.shape
    part = length // n_seq
    group = n_seq * tokens
    heads = H // n_seq
    per_device = expert_gate_up.shape[1]
    experts = per_device * n_seq
    capacity = TOP * tokens // per_device
    ff_parts = n_dp // per_device
    expert_bit = dp_index % per_device
    down_rows = kv_down.shape[0]
    down_width = kv_down.shape[1]
    q_width = heads * (NOPE + ROPE)
    e_width = heads * (NOPE + VD)

    labels = jnp.arange(experts, dtype=jnp.int32)
    hits = jnp.sum((expert_ids[:, :, None] == labels).astype(jnp.int32), axis=1)
    earlier = jnp.arange(group, dtype=jnp.int32)[:, None] < seq_index * tokens
    before_own = jnp.sum(jnp.where(earlier, hits, 0), axis=0)
    own_hits = lax.dynamic_slice_in_dim(hits, seq_index * tokens, tokens, 0)
    own_picks = lax.dynamic_slice_in_dim(expert_ids, seq_index * tokens, tokens, 0)
    own_slot = before_own[None, :] + jnp.cumsum(own_hits, axis=0) - own_hits
    code = jnp.where((own_hits > 0) & (own_slot < capacity), own_slot + 1, 0)
    gates = jnp.sum(
        gate_fix[:, :, None] * (own_picks[:, :, None] == labels).astype(jnp.int32), axis=1
    )
    pieces = jnp.stack([code // 16, code % 16, gates // 128, gates % 128], axis=0)
    pieces = jnp.transpose(pieces, (2, 0, 1)).reshape(experts, 4 * tokens).astype(BF16)

    def wide_row(vector):
        return jnp.pad(vector, (0, down_width - 4 * tokens - vector.shape[0]))[None]

    extras = jnp.concatenate([wide_row(attn_gain), wide_row(ffn_gain), wide_row(kv_gain)], axis=0)
    extras = jnp.pad(extras, ((0, experts - 3), (0, 0)))
    message = jnp.concatenate(
        [kv_down, jnp.concatenate([pieces, extras], axis=1)], axis=0
    )
    spread = lax.all_gather(message, BOTH, axis=0, tiled=False)
    weight_down = spread[:, :down_rows].reshape(-1, down_width)
    spread_tail = spread[:, down_rows:]
    first = 4 * tokens
    gain_attn = spread_tail[:, 0, first : first + attn_gain.shape[0]].reshape(-1).astype(F32)
    gain_ffn = spread_tail[:, 1, first : first + ffn_gain.shape[0]].reshape(-1).astype(F32)
    gain_kv = spread_tail[:, 2, first : first + kv_gain.shape[0]].reshape(-1).astype(F32)
    own_expert = per_device * seq_index + expert_bit
    routing = lax.dynamic_index_in_dim(spread_tail, own_expert, axis=1, keepdims=False)
    routing = routing[:, :first].reshape(n_all, 4, tokens).astype(jnp.int32)
    slot_code = (routing[:, 0] * 16 + routing[:, 1]).reshape(n_dp, group)
    gate_of = (routing[:, 2] * 128 + routing[:, 3]).astype(F32).reshape(n_dp, group) / GATE_UNIT

    q_rows = lax.all_to_all(q_weight, "seq", split_axis=1, concat_axis=0, tiled=True)
    up_rows = lax.all_to_all(kv_up, "seq", split_axis=1, concat_axis=0, tiled=True)
    up_shape = up_rows.shape
    joined = jnp.concatenate([q_rows, up_rows.reshape(q_rows.shape[0], -1)], axis=1)
    joined = lax.all_gather(joined, "dp", axis=0, tiled=True)
    weight_q = joined[:, :q_width]
    weight_up = joined[:, q_width:].reshape(n_dp * up_shape[0], up_shape[1])
    weight_out = lax.all_gather(out_weight, BOTH, axis=0, tiled=True)

    units = shared_down.shape[0]
    gate_up_parts = shared_gate_up.reshape(-1, 2, n_all, units)
    gate_up_parts = jnp.transpose(gate_up_parts, (2, 0, 1, 3)).reshape(n_all, -1, 2 * units)
    weight_shared_in = lax.all_to_all(
        gate_up_parts, BOTH, split_axis=0, concat_axis=0, tiled=True
    ).reshape(-1, 2 * units)

    ff_width = expert_gate_up.shape[2] // 2
    ff_part = ff_width // ff_parts
    expert_rows = expert_gate_up.shape[0]
    in_parts = expert_gate_up.reshape(expert_rows, per_device, 2, ff_parts, ff_part)
    in_parts = jnp.transpose(in_parts, (3, 1, 0, 2, 4)).reshape(n_dp, expert_rows, 2 * ff_part)
    weight_in = lax.all_to_all(in_parts, "dp", split_axis=0, concat_axis=0, tiled=True)
    weight_in = weight_in.reshape(-1, 2 * ff_part)
    swap = [(i, i ^ 1) for i in range(n_dp)]
    down_kept = lax.dynamic_index_in_dim(expert_down, expert_bit, 1, keepdims=False)
    down_sent = lax.dynamic_index_in_dim(expert_down, 1 - expert_bit, 1, keepdims=False)
    down_got = lax.ppermute(down_sent, "dp", swap)
    is_low = expert_bit == 0
    weight_back = jnp.concatenate(
        [jnp.where(is_low, down_kept, down_got), jnp.where(is_low, down_got, down_kept)], axis=0
    )

    cot_all = lax.all_gather(cotangent, BOTH, axis=0, tiled=True)

    hidden_group = lax.all_gather(hidden, "seq", axis=0, tiled=True)
    rows_group = hidden_group.astype(F32)
    normed_group = (rows_group * rms_scale(rows_group) * gain_attn).astype(BF16)
    group_row = jnp.arange(group, dtype=jnp.int32)
    positions = group_row // tokens * part + group_row % part
    cosine, sine = rotary_tables(positions)

    def to_sequence(values):
        split = values.reshape((n_seq, sequences, part) + values.shape[1:])
        return jnp.swapaxes(split, 0, 1).reshape((sequences, length) + values.shape[1:])

    def to_rows(values):
        split = values.reshape((sequences, n_seq, part) + values.shape[2:])
        return jnp.swapaxes(split, 0, 1).reshape((group,) + values.shape[2:])

    query_raw = matmul(normed_group, weight_q).reshape(group, heads, NOPE + ROPE)
    latent_in = matmul(normed_group, weight_down)
    latent_raw = latent_in[:, :KV_RANK]
    latent = (latent_raw * rms_scale(latent_raw) * gain_kv).astype(BF16)
    expanded = matmul(latent, weight_up).reshape(group, heads, NOPE + VD)
    rope_query = rotate(query_raw[..., NOPE:], cosine[:, None], sine[:, None])
    rope_key = rotate(latent_in[:, KV_RANK:], cosine, sine)
    rope_key = jnp.broadcast_to(rope_key[:, None], (group, heads, ROPE))
    queries = to_sequence(
        jnp.concatenate([query_raw[..., :NOPE], rope_query], axis=-1).astype(BF16)
    )
    keys = to_sequence(
        jnp.concatenate([expanded[..., :NOPE], rope_key], axis=-1).astype(BF16)
    )
    values = to_sequence(expanded[..., NOPE:].astype(BF16))
    score_scale = (NOPE + ROPE) ** (-0.5)
    scores = jnp.einsum("bqhd,bkhd->bhqk", queries, keys, preferred_element_type=F32) * score_scale
    allowed = block_ids[:, None, None, :] <= block_ids[:, None, :, None]
    scores = jnp.where(allowed, scores, -1e30)
    weights = jnp.exp(scores - jnp.max(scores, axis=-1, keepdims=True))
    probs = weights / jnp.sum(weights, axis=-1, keepdims=True)
    shares = probs.astype(BF16)
    attended = jnp.einsum("bhqk,bkhd->bqhd", shares, values, preferred_element_type=F32)
    attended = to_rows(attended.astype(BF16)).reshape(group, heads * VD)
    heads_out = lax.all_to_all(attended, "seq", split_axis=0, concat_axis=1, tiled=True)

    rows = hidden.astype(F32)
    residual = rows + matmul(heads_out, weight_out)
    normed_ffn = (residual * rms_scale(residual) * gain_ffn).astype(BF16)
    ffn_all = lax.all_gather(normed_ffn, BOTH, axis=0, tiled=True)

    shared_in = matmul(ffn_all, weight_shared_in)
    shared_gate, shared_up = shared_in[:, :units], shared_in[:, units:]
    shared_act = swiglu(shared_gate, shared_up).astype(BF16)
    shared_act_grad = tail_dot(cot_all, shared_down)
    grad_shared_down = lead_dot(shared_act, cot_all)
    shared_in_grad = jnp.concatenate(
        swiglu_back(shared_gate, shared_up, shared_act_grad), axis=1
    ).astype(BF16)
    grad_shared_in = lead_dot(ffn_all, shared_in_grad)

    slots = jnp.arange(1, capacity + 1, dtype=jnp.int32)
    placed = (slot_code[:, :, None] == slots).astype(BF16)
    slot_gate = jnp.sum(
        jnp.where(slot_code[:, :, None] == slots, gate_of[:, :, None], 0.0), axis=1
    )[..., None]
    slot_rows = jnp.einsum(
        "gtc,gtd->gcd", placed, ffn_all.reshape(n_dp, group, width), preferred_element_type=F32
    ).astype(BF16)
    slot_cot = jnp.einsum(
        "gtc,gtd->gcd", placed, cot_all.reshape(n_dp, group, width), preferred_element_type=F32
    )
    slot_cot = (slot_cot * slot_gate).astype(BF16)
    slot_rows = slot_rows.reshape(n_dp * capacity, width)
    slot_cot = slot_cot.reshape(n_dp * capacity, width)
    expert_in = matmul(slot_rows, weight_in)
    expert_gate, expert_up = expert_in[:, :ff_part], expert_in[:, ff_part:]
    expert_act = swiglu(expert_gate, expert_up).astype(BF16)
    expert_act_grad = tail_dot(slot_cot, weight_back)
    grad_back = lead_dot(expert_act, slot_cot)
    expert_in_grad = jnp.concatenate(
        swiglu_back(expert_gate, expert_up, expert_act_grad), axis=1
    ).astype(BF16)
    grad_in = lead_dot(slot_rows, expert_in_grad)
    slot_grad = tail_dot(expert_in_grad, weight_in).astype(BF16)
    expert_out = matmul(expert_act, weight_back).reshape(n_dp, capacity, width)
    expert_out = (expert_out * slot_gate).astype(BF16)

    dn_part = jnp.einsum(
        "gtc,gcd->gtd",
        placed,
        slot_grad.reshape(n_dp, capacity, width),
        preferred_element_type=F32,
    ).reshape(n_all * tokens, width) + tail_dot(shared_in_grad, weight_shared_in)
    ffn_grad = lax.psum_scatter(dn_part.astype(BF16), BOTH, scatter_dimension=0, tiled=True)
    ffn_grad = ffn_grad.astype(F32)
    out_part = jnp.einsum(
        "gtc,gcd->gtd", placed, expert_out, preferred_element_type=F32
    ).reshape(n_all * tokens, width) + matmul(shared_act, shared_down)
    out_sum = lax.psum_scatter(out_part.astype(BF16), BOTH, scatter_dimension=0, tiled=True)
    output = (residual + out_sum.astype(F32)).astype(BF16)

    in_back = lax.all_to_all(
        grad_in.astype(BF16).reshape(n_dp, expert_rows, 2 * ff_part),
        "dp",
        split_axis=0,
        concat_axis=0,
        tiled=True,
    ).reshape(ff_parts, per_device, expert_rows, 2, ff_part)
    grad_expert_in = jnp.transpose(in_back, (2, 1, 3, 0, 4)).reshape(expert_gate_up.shape)
    grad_expert_in = grad_expert_in.astype(F32)
    half = expert_down.shape[0]
    low_half, high_half = grad_back[:half], grad_back[half:]
    grad_kept = jnp.where(is_low, low_half, high_half)
    grad_sent = jnp.where(is_low, high_half, low_half).astype(BF16)
    grad_got = lax.ppermute(grad_sent, "dp", swap).astype(F32)
    grad_expert_down = jnp.stack(
        [jnp.where(is_low, grad_kept, grad_got), jnp.where(is_low, grad_got, grad_kept)], axis=1
    )

    shared_back = lax.all_to_all(
        grad_shared_in.astype(BF16).reshape(n_all, -1, 2 * units),
        BOTH,
        split_axis=0,
        concat_axis=0,
        tiled=True,
    ).reshape(n_all, -1, 2, units)
    grad_shared_gate_up = jnp.transpose(shared_back, (1, 2, 0, 3)).reshape(shared_gate_up.shape)
    grad_shared_gate_up = grad_shared_gate_up.astype(F32)

    from_norm, gain_ffn_grad = rms_back(residual, gain_ffn, ffn_grad)
    residual_grad = cotangent.astype(F32) + from_norm
    residual_low = residual_grad.astype(BF16)
    heads_grad = tail_dot(residual_low, weight_out).astype(BF16)
    heads_grad = lax.all_to_all(heads_grad, "seq", split_axis=1, concat_axis=0, tiled=True)
    residual_group = lax.all_gather(residual_low, "seq", axis=0, tiled=True)
    grad_out_heads = lead_dot(attended, residual_group)
    out_shard = scatter_sum(grad_out_heads, "dp", n_dp)
    home = [
        (d * n_seq + s, s * n_dp + d) for d in range(n_dp) for s in range(n_seq)
    ]
    grad_out_weight = lax.ppermute(out_shard, BOTH, home)

    grad_o = to_sequence(heads_grad.reshape(group, heads, VD))
    prob_grad = jnp.einsum("bqhd,bkhd->bhqk", grad_o, values, preferred_element_type=F32)
    centre = jnp.sum(probs * prob_grad, axis=-1, keepdims=True)
    score_grad = (probs * (prob_grad - centre)).astype(BF16)
    query_grad = jnp.einsum("bhqk,bkhd->bqhd", score_grad, keys, preferred_element_type=F32)
    key_grad = jnp.einsum("bhqk,bqhd->bkhd", score_grad, queries, preferred_element_type=F32)
    value_grad = jnp.einsum("bhqk,bqhd->bkhd", shares, grad_o, preferred_element_type=F32)
    query_grad = to_rows((query_grad * score_scale).astype(BF16)).astype(F32)
    key_grad = to_rows((key_grad * score_scale).astype(BF16)).astype(F32)
    value_grad = to_rows(value_grad.astype(BF16))
    query_low = jnp.concatenate(
        [
            query_grad[..., :NOPE],
            rotate_back(query_grad[..., NOPE:], cosine[:, None], sine[:, None]),
        ],
        axis=-1,
    ).astype(BF16).reshape(group, q_width)
    rope_grad = rotate_back(jnp.sum(key_grad[..., NOPE:], axis=1), cosine, sine)
    expand_low = jnp.concatenate(
        [key_grad[..., :NOPE].astype(BF16), value_grad], axis=-1
    ).reshape(group, e_width)

    latent_part = tail_dot(expand_low, weight_up)
    latent_sum = scatter_sum(jnp.concatenate([latent_part, rope_grad], axis=1), "seq", n_seq)
    normed_sum = scatter_sum(tail_dot(query_low, weight_q), "seq", n_seq)
    grad_q = scatter_sum(lead_dot(normed_group, query_low), "dp", n_dp)
    grad_q = lax.all_to_all(grad_q, "seq", split_axis=0, concat_axis=1, tiled=True)
    grad_up = scatter_sum(lead_dot(latent, expand_low), "dp", n_dp)
    grad_up = lax.all_to_all(grad_up, "seq", split_axis=0, concat_axis=1, tiled=True)

    own_latent = lax.dynamic_slice_in_dim(latent_raw, seq_index * tokens, tokens, 0)
    latent_grad, gain_kv_grad = rms_back(own_latent, gain_kv, latent_sum[:, :KV_RANK])
    down_low = jnp.concatenate([latent_grad, latent_sum[:, KV_RANK:]], axis=1).astype(BF16)
    down_group = lax.all_gather(down_low, "seq", axis=0, tiled=True)
    normed_cols = normed_group.reshape(group, n_dp, n_seq, down_rows)
    normed_cols = lax.dynamic_index_in_dim(normed_cols, seq_index, 2, keepdims=False)
    grad_down = lead_dot(normed_cols.reshape(group, n_dp * down_rows), down_group)
    grad_down = scatter_sum(grad_down, "dp", n_dp)

    normed_grad = normed_sum + tail_dot(down_low, weight_down)
    rows_from_norm, gain_attn_grad = rms_back(rows, gain_attn, normed_grad)
    input_grad = residual_grad + rows_from_norm

    gain_grads = jnp.concatenate(
        [
            gain_attn_grad.reshape(n_all, -1),
            gain_ffn_grad.reshape(n_all, -1),
            gain_kv_grad.reshape(n_all, -1),
        ],
        axis=1,
    )
    gain_grads = lax.all_to_all(gain_grads, BOTH, split_axis=0, concat_axis=0, tiled=True)
    gain_grads = jnp.sum(gain_grads, axis=0)
    attn_end = attn_gain.shape[0]
    ffn_end = attn_end + ffn_gain.shape[0]

    return (
        output,
        input_grad,
        gain_grads[:attn_end],
        grad_q,
        grad_down,
        gain_grads[ffn_end:],
        grad_up,
        grad_out_weight,
        gain_grads[attn_end:ffn_end],
        grad_shared_gate_up,
        grad_shared_down,
        grad_expert_in,
        grad_expert_down,
    )


def solution(mesh):
    rows = P(BOTH, None)
    return jax.shard_map(
        body,
        mesh=mesh,
        in_specs=(
            rows,
            rows,
            P(BOTH),
            rows,
            rows,
            P(BOTH),
            rows,
            rows,
            P(BOTH),
            rows,
            rows,
            P("dp", "seq", None),
            P("dp", "seq", None),
            P("dp", None),
            rows,
            P("dp", None),
        ),
        out_specs=(
            rows,
            rows,
            P(BOTH),
            rows,
            rows,
            P(BOTH),
            rows,
            rows,
            P(BOTH),
            rows,
            rows,
            P("dp", "seq", None),
            P("dp", "seq", None),
        ),
        check_vma=False,
    )
```

```python
import jax
import jax.numpy as jnp
import numpy as np
from jax import lax
from jax.sharding import PartitionSpec as P

H = 16
NOPE = 128
ROPE = 64
VD = 128
KV_RANK = 512
TOP = 6

EPS = 1e-06
THETA = 10000.0
GATE_UNIT = 16384.0

BOTH = ("dp", "seq")
F32 = jnp.float32
BF16 = jnp.bfloat16


def contract(left_side, right_side, left_dim, right_dim):
    return lax.dot_general(
        left_side,
        right_side,
        (((left_dim,), (right_dim,)), ((), ())),
        preferred_element_type=F32,
    )


def matmul(left_side, right_side):
    return contract(left_side, right_side, left_side.ndim - 1, 0)


def lead_dot(left_side, right_side):
    return contract(left_side, right_side, 0, 0)


def tail_dot(left_side, right_side):
    return contract(left_side, right_side, 1, 1)


def rms_scale(values):
    return lax.rsqrt(jnp.mean(values * values, axis=-1, keepdims=True) + EPS)


def rms_back(values, gain, grad):
    scale = rms_scale(values)
    unit = values * scale
    weighted = grad * gain
    centre = jnp.mean(weighted * unit, axis=-1, keepdims=True)
    return scale * (weighted - unit * centre), jnp.sum(grad * unit, axis=0)


def swiglu(gate, up):
    return jax.nn.silu(gate) * up


def swiglu_back(gate, up, grad):
    sig = jax.nn.sigmoid(gate)
    return grad * up * sig * (1.0 + gate * (1.0 - sig)), grad * (gate * sig)


def rotary_tables(positions):
    half_width = ROPE // 2
    frequency = THETA ** (-jnp.arange(half_width, dtype=F32) * 2.0 / ROPE)
    angles = positions.astype(F32)[:, None] * frequency[None, :]
    return jnp.cos(angles), jnp.sin(angles)


def rotate(values, cosine, sine):
    half_width = values.shape[-1] // 2
    lead = values[..., :half_width]
    trail = values[..., half_width:]
    return jnp.concatenate([lead * cosine - trail * sine, trail * cosine + lead * sine], axis=-1)


def rotate_back(grads, cosine, sine):
    return rotate(grads, cosine, -sine)


def link_orders(n_seq):
    bits = [1 << j for j in range(1, n_seq.bit_length() - 1)]
    return bits, bits[::-1]


def block_table(n_seq):
    orders = link_orders(n_seq)
    steps = len(orders[0])
    table = np.zeros((n_seq, n_seq), np.int32)
    for s in range(n_seq):
        for m in range(n_seq):
            core = (s & 1) ^ (m >> steps)
            other = (s & ~1) | core
            for j in range(steps):
                if m >> j & 1:
                    other ^= orders[core][j]
            table[s, m] = other
    return table


def seq_step(values, n_seq, step):
    orders = link_orders(n_seq)
    return lax.ppermute(values, "seq", [(s, s ^ orders[s & 1][step]) for s in range(n_seq)])


def core_swap(values, n_seq):
    return lax.ppermute(values, "seq", [(s, s ^ 1) for s in range(n_seq)])


def seq_gather(values, n_seq):
    current = values
    for step in range(len(link_orders(n_seq)[0])):
        current = jnp.concatenate([current, seq_step(current, n_seq, step)], axis=0)
    return jnp.concatenate([current, core_swap(current, n_seq)], axis=0)


def seq_scatter(values, n_seq):
    values = values.astype(BF16)
    half = values.shape[0] // 2
    total = values[:half].astype(F32) + core_swap(values[half:], n_seq).astype(F32)
    for step in reversed(range(len(link_orders(n_seq)[0]))):
        half = total.shape[0] // 2
        sent = seq_step(total[half:].astype(BF16), n_seq, step)
        total = total[:half] + sent.astype(F32)
    return total


def dp_swap(values, n_dp, step):
    return lax.ppermute(values, "dp", [(d, d ^ step) for d in range(n_dp)])


def dp_block(blocks, index):
    return lax.dynamic_index_in_dim(blocks, index, 0, keepdims=False)


def dp_exchange(blocks, n_dp, dp_index):
    moved = [dp_block(blocks, dp_index)]
    for step in range(1, n_dp):
        moved.append(dp_swap(dp_block(blocks, dp_index ^ step), n_dp, step))
    return in_order(moved, n_dp, dp_index)


def in_order(moved, n_dp, dp_index):
    return jnp.take(jnp.stack(moved), jnp.arange(n_dp, dtype=jnp.int32) ^ dp_index, axis=0)


def dp_gather(values, n_dp, dp_index):
    moved = [values] + [dp_swap(values, n_dp, step) for step in range(1, n_dp)]
    return in_order(moved, n_dp, dp_index)


def dp_scatter(values, n_dp, dp_index):
    blocks = values.reshape((n_dp, -1) + values.shape[1:])
    low = blocks.astype(BF16)
    total = dp_block(blocks, dp_index).astype(F32)
    for step in range(1, n_dp):
        total = total + dp_swap(dp_block(low, dp_index ^ step), n_dp, step).astype(F32)
    return total


def body(
    hidden,
    cotangent,
    attn_gain,
    q_weight,
    kv_down,
    kv_gain,
    kv_up,
    out_weight,
    ffn_gain,
    shared_gate_up,
    shared_down,
    expert_gate_up,
    expert_down,
    expert_ids,
    gate_fix,
    block_ids,
):
    n_dp = lax.axis_size("dp")
    n_seq = lax.axis_size("seq")
    n_all = n_dp * n_seq
    dp_index = lax.axis_index("dp")
    seq_index = lax.axis_index("seq")
    tokens, width = hidden.shape
    sequences, length = block_ids.shape
    part = length // n_seq
    group = n_seq * tokens
    heads = H // n_seq
    per_device = expert_gate_up.shape[1]
    experts = per_device * n_seq
    capacity = TOP * tokens // per_device
    ff_parts = n_dp // per_device
    expert_bit = dp_index % per_device
    down_rows = kv_down.shape[0]
    down_width = kv_down.shape[1]
    q_width = heads * (NOPE + ROPE)
    e_width = heads * (NOPE + VD)
    block_at = dp_block(jnp.asarray(block_table(n_seq)), seq_index)
    block_of = dp_block(jnp.asarray(np.argsort(block_table(n_seq), axis=1)), seq_index)

    def relative(values):
        return jnp.take(values, block_at, axis=0)

    def absolute(values):
        return jnp.take(values, block_of, axis=0)

    up_rows = kv_up.reshape(kv_up.shape[0], n_seq, -1, kv_up.shape[0] * e_width // down_rows)
    up_rows = jnp.swapaxes(up_rows, 1, 2).reshape(down_rows, n_seq, -1)
    joined = jnp.concatenate([q_weight.reshape(down_rows, n_seq, q_width), up_rows], axis=2)
    joined_width = joined.shape[2]
    joined = lax.all_to_all(joined, "seq", split_axis=1, concat_axis=0, tiled=True)
    joined = joined.reshape(n_seq * down_rows, joined_width)
    joined = dp_gather(joined, n_dp, dp_index).reshape(-1, joined_width)
    weight_q = joined[:, :q_width]
    weight_up = joined[:, q_width:].reshape(KV_RANK, e_width)

    hidden_group = seq_gather(hidden, n_seq)

    labels = jnp.arange(experts, dtype=jnp.int32)
    hits = jnp.sum((expert_ids[:, :, None] == labels).astype(jnp.int32), axis=1)
    earlier = jnp.arange(group, dtype=jnp.int32)[:, None] < seq_index * tokens
    before_own = jnp.sum(jnp.where(earlier, hits, 0), axis=0)
    own_hits = lax.dynamic_slice_in_dim(hits, seq_index * tokens, tokens, 0)
    own_picks = lax.dynamic_slice_in_dim(expert_ids, seq_index * tokens, tokens, 0)
    own_slot = before_own[None, :] + jnp.cumsum(own_hits, axis=0) - own_hits
    code = jnp.where((own_hits > 0) & (own_slot < capacity), own_slot + 1, 0)
    gates = jnp.sum(
        gate_fix[:, :, None] * (own_picks[:, :, None] == labels).astype(jnp.int32), axis=1
    )
    pieces = jnp.stack([code // 16, code % 16, gates // 128, gates % 128], axis=0)
    pieces = jnp.transpose(pieces, (2, 0, 1)).reshape(experts, 4 * tokens).astype(BF16)

    def wide_row(vector):
        return jnp.pad(vector, (0, down_width - 4 * tokens - vector.shape[0]))[None]

    extras = jnp.concatenate([wide_row(attn_gain), wide_row(ffn_gain), wide_row(kv_gain)], axis=0)
    extras = jnp.pad(extras, ((0, experts - 3), (0, 0)))
    message = jnp.concatenate(
        [kv_down, jnp.concatenate([pieces, extras], axis=1)], axis=0
    )
    spread = lax.all_gather(message, BOTH, axis=0, tiled=False)
    weight_down = spread[:, :down_rows].reshape(-1, down_width)
    spread_tail = spread[:, down_rows:]
    first = 4 * tokens
    gain_attn = spread_tail[:, 0, first : first + attn_gain.shape[0]].reshape(-1).astype(F32)
    gain_ffn = spread_tail[:, 1, first : first + ffn_gain.shape[0]].reshape(-1).astype(F32)
    gain_kv = spread_tail[:, 2, first : first + kv_gain.shape[0]].reshape(-1).astype(F32)
    own_expert = per_device * seq_index + expert_bit
    routing = lax.dynamic_index_in_dim(spread_tail, own_expert, axis=1, keepdims=False)
    routing = routing[:, :first].reshape(n_dp, n_seq, 4, tokens).astype(jnp.int32)
    slot_code = routing[:, :, 0] * 16 + routing[:, :, 1]
    gate_of = (routing[:, :, 2] * 128 + routing[:, :, 3]).astype(F32) / GATE_UNIT

    weight_out = lax.all_gather(out_weight, BOTH, axis=0, tiled=True)

    ff_width = expert_gate_up.shape[2] // 2
    ff_part = ff_width // ff_parts
    expert_rows = expert_gate_up.shape[0]
    in_parts = expert_gate_up.reshape(expert_rows, per_device, 2, ff_parts, ff_part)
    in_parts = jnp.transpose(in_parts, (3, 1, 0, 2, 4)).reshape(n_dp, expert_rows, 2 * ff_part)
    weight_in = dp_exchange(in_parts, n_dp, dp_index).reshape(-1, 2 * ff_part)
    down_kept = lax.dynamic_index_in_dim(expert_down, expert_bit, 1, keepdims=False)
    down_sent = lax.dynamic_index_in_dim(expert_down, 1 - expert_bit, 1, keepdims=False)
    down_got = dp_swap(down_sent, n_dp, 1)
    is_low = expert_bit == 0
    weight_back = jnp.concatenate(
        [jnp.where(is_low, down_kept, down_got), jnp.where(is_low, down_got, down_kept)], axis=0
    )

    units = shared_down.shape[0]
    gate_up_parts = shared_gate_up.reshape(-1, 2, n_all, units)
    gate_up_parts = jnp.transpose(gate_up_parts, (2, 0, 1, 3)).reshape(n_all, -1, 2 * units)
    weight_shared_in = lax.all_to_all(
        gate_up_parts, BOTH, split_axis=0, concat_axis=0, tiled=True
    ).reshape(-1, 2 * units)

    def chunk_gather(values):
        sent = [values] + [dp_swap(values, n_dp, step) for step in range(1, n_dp)]
        return [seq_gather(piece, n_seq) for piece in sent]

    cot_chunks = chunk_gather(cotangent)

    rows_group = hidden_group.astype(F32)
    normed_group = (rows_group * rms_scale(rows_group) * gain_attn).astype(BF16)
    in_part = jnp.arange(tokens, dtype=jnp.int32) % part
    positions = (block_at[:, None] * part + in_part[None, :]).reshape(group)
    cosine, sine = rotary_tables(positions)

    def to_sequence(values):
        split = values.reshape((n_seq, sequences, part) + values.shape[1:])
        return jnp.swapaxes(split, 0, 1).reshape((sequences, length) + values.shape[1:])

    def to_rows(values):
        split = values.reshape((sequences, n_seq, part) + values.shape[2:])
        return jnp.swapaxes(split, 0, 1).reshape((group,) + values.shape[2:])

    query_raw = matmul(normed_group, weight_q).reshape(group, heads, NOPE + ROPE)
    latent_in = matmul(normed_group, weight_down)
    latent_raw = latent_in[:, :KV_RANK]
    latent = (latent_raw * rms_scale(latent_raw) * gain_kv).astype(BF16)
    expanded = matmul(latent, weight_up).reshape(group, heads, NOPE + VD)
    rope_query = rotate(query_raw[..., NOPE:], cosine[:, None], sine[:, None])
    rope_key = rotate(latent_in[:, KV_RANK:], cosine, sine)
    rope_key = jnp.broadcast_to(rope_key[:, None], (group, heads, ROPE))
    queries = to_sequence(
        jnp.concatenate([query_raw[..., :NOPE], rope_query], axis=-1).astype(BF16)
    )
    keys = to_sequence(
        jnp.concatenate([expanded[..., :NOPE], rope_key], axis=-1).astype(BF16)
    )
    values = to_sequence(expanded[..., NOPE:].astype(BF16))
    blocks = jnp.take(block_ids.reshape(sequences, n_seq, part), block_at, axis=1)
    blocks = blocks.reshape(sequences, length)
    score_scale = (NOPE + ROPE) ** (-0.5)
    scores = jnp.einsum("bqhd,bkhd->bhqk", queries, keys, preferred_element_type=F32) * score_scale
    allowed = blocks[:, None, None, :] <= blocks[:, None, :, None]
    scores = jnp.where(allowed, scores, -1e30)
    weights = jnp.exp(scores - jnp.max(scores, axis=-1, keepdims=True))
    probs = weights / jnp.sum(weights, axis=-1, keepdims=True)
    shares = probs.astype(BF16)
    attended = jnp.einsum("bhqk,bkhd->bqhd", shares, values, preferred_element_type=F32)
    attended = to_rows(attended.astype(BF16)).reshape(group, heads * VD)
    heads_out = absolute(attended.reshape(n_seq, tokens, heads * VD))
    heads_out = lax.all_to_all(heads_out, "seq", split_axis=0, concat_axis=2, tiled=True)
    heads_out = heads_out.reshape(tokens, H * VD)

    rows = hidden.astype(F32)
    residual = rows + matmul(heads_out, weight_out)
    normed_ffn = (residual * rms_scale(residual) * gain_ffn).astype(BF16)

    slots = jnp.arange(1, capacity + 1, dtype=jnp.int32)
    ffn_chunks = chunk_gather(normed_ffn)
    ffn_grad = 0.0
    out_chunks = []
    grad_shared_down = 0.0
    grad_shared_in = 0.0
    kept_rows, kept_cots, kept_acts, kept_grads = [], [], [], []
    for step in range(n_dp):
        ffn_rows, cot_rows = ffn_chunks[step], cot_chunks[step]
        codes = relative(dp_block(slot_code, dp_index ^ step)).reshape(group)
        chunk_gate = relative(dp_block(gate_of, dp_index ^ step)).reshape(group)
        here = codes[:, None] == slots
        placed = here.astype(BF16)
        slot_gate = jnp.sum(jnp.where(here, chunk_gate[:, None], 0.0), axis=0)[:, None]

        shared_in = matmul(ffn_rows, weight_shared_in)
        shared_gate, shared_up = shared_in[:, :units], shared_in[:, units:]
        shared_act = swiglu(shared_gate, shared_up).astype(BF16)
        shared_act_grad = tail_dot(cot_rows, shared_down)
        shared_in_grad = jnp.concatenate(
            swiglu_back(shared_gate, shared_up, shared_act_grad), axis=1
        ).astype(BF16)
        grad_shared_down = grad_shared_down + lead_dot(shared_act, cot_rows)
        grad_shared_in = grad_shared_in + lead_dot(ffn_rows, shared_in_grad)

        slot_cot = (lead_dot(placed, cot_rows) * slot_gate).astype(BF16)
        slot_rows = lead_dot(placed, ffn_rows).astype(BF16)
        expert_in = matmul(slot_rows, weight_in)
        expert_gate, expert_up = expert_in[:, :ff_part], expert_in[:, ff_part:]
        expert_act = swiglu(expert_gate, expert_up).astype(BF16)
        expert_act_grad = tail_dot(slot_cot, weight_back)
        expert_in_grad = jnp.concatenate(
            swiglu_back(expert_gate, expert_up, expert_act_grad), axis=1
        ).astype(BF16)
        slot_grad = tail_dot(expert_in_grad, weight_in).astype(BF16)
        dn_part = matmul(
            jnp.concatenate([placed, shared_in_grad], axis=1),
            jnp.concatenate([slot_grad, weight_shared_in.T], axis=0),
        )
        plane_sum = seq_scatter(dn_part, n_seq)
        if step:
            plane_sum = dp_swap(plane_sum.astype(BF16), n_dp, step).astype(F32)
        ffn_grad = ffn_grad + plane_sum

        expert_out = (matmul(expert_act, weight_back) * slot_gate).astype(BF16)
        out_chunks.append(
            matmul(
                jnp.concatenate([placed, shared_act], axis=1),
                jnp.concatenate([expert_out, shared_down], axis=0),
            ).astype(BF16)
        )
        kept_rows.append(slot_rows)
        kept_cots.append(slot_cot)
        kept_acts.append(expert_act)
        kept_grads.append(expert_in_grad)

    grad_in = lead_dot(jnp.concatenate(kept_rows), jnp.concatenate(kept_grads))
    grad_back = lead_dot(jnp.concatenate(kept_acts), jnp.concatenate(kept_cots))

    out_sum = 0.0
    for step in range(n_dp):
        plane_sum = seq_scatter(out_chunks[step], n_seq)
        if step:
            plane_sum = dp_swap(plane_sum.astype(BF16), n_dp, step).astype(F32)
        out_sum = out_sum + plane_sum
    output = (residual + out_sum).astype(BF16)

    in_back = dp_exchange(
        grad_in.astype(BF16).reshape(n_dp, expert_rows, 2 * ff_part), n_dp, dp_index
    ).reshape(ff_parts, per_device, expert_rows, 2, ff_part)
    grad_expert_in = jnp.transpose(in_back, (2, 1, 3, 0, 4)).reshape(expert_gate_up.shape)
    grad_expert_in = grad_expert_in.astype(F32)
    half = expert_down.shape[0]
    low_half, high_half = grad_back[:half], grad_back[half:]
    grad_kept = jnp.where(is_low, low_half, high_half)
    grad_sent = jnp.where(is_low, high_half, low_half).astype(BF16)
    grad_got = dp_swap(grad_sent, n_dp, 1).astype(F32)
    grad_expert_down = jnp.stack(
        [jnp.where(is_low, grad_kept, grad_got), jnp.where(is_low, grad_got, grad_kept)], axis=1
    )

    shared_back = lax.all_to_all(
        grad_shared_in.astype(BF16).reshape(n_all, -1, 2 * units),
        BOTH,
        split_axis=0,
        concat_axis=0,
        tiled=True,
    ).reshape(n_all, -1, 2, units)
    grad_shared_gate_up = jnp.transpose(shared_back, (1, 2, 0, 3)).reshape(shared_gate_up.shape)
    grad_shared_gate_up = grad_shared_gate_up.astype(F32)

    from_norm, gain_ffn_grad = rms_back(residual, gain_ffn, ffn_grad)
    residual_grad = cotangent.astype(F32) + from_norm
    residual_low = residual_grad.astype(BF16)
    heads_grad = tail_dot(residual_low, weight_out).astype(BF16)
    heads_grad = heads_grad.reshape(tokens, n_seq, heads * VD)
    heads_grad = lax.all_to_all(heads_grad, "seq", split_axis=1, concat_axis=0, tiled=True)
    heads_grad = relative(heads_grad.reshape(n_seq, tokens, heads * VD))
    residual_group = seq_gather(residual_low, n_seq)
    grad_out_heads = lead_dot(attended, residual_group)
    out_shard = dp_scatter(grad_out_heads, n_dp, dp_index)
    home = [
        (d * n_seq + s, s * n_dp + d) for d in range(n_dp) for s in range(n_seq)
    ]
    grad_out_weight = lax.ppermute(out_shard, BOTH, home)

    grad_o = to_sequence(heads_grad.reshape(group, heads, VD))
    prob_grad = jnp.einsum("bqhd,bkhd->bhqk", grad_o, values, preferred_element_type=F32)
    centre = jnp.sum(probs * prob_grad, axis=-1, keepdims=True)
    score_grad = (probs * (prob_grad - centre)).astype(BF16)
    query_grad = jnp.einsum("bhqk,bkhd->bqhd", score_grad, keys, preferred_element_type=F32)
    key_grad = jnp.einsum("bhqk,bqhd->bkhd", score_grad, queries, preferred_element_type=F32)
    value_grad = jnp.einsum("bhqk,bqhd->bkhd", shares, grad_o, preferred_element_type=F32)
    query_grad = to_rows((query_grad * score_scale).astype(BF16)).astype(F32)
    key_grad = to_rows((key_grad * score_scale).astype(BF16)).astype(F32)
    value_grad = to_rows(value_grad.astype(BF16))
    query_low = jnp.concatenate(
        [
            query_grad[..., :NOPE],
            rotate_back(query_grad[..., NOPE:], cosine[:, None], sine[:, None]),
        ],
        axis=-1,
    ).astype(BF16).reshape(group, q_width)
    rope_grad = rotate_back(jnp.sum(key_grad[..., NOPE:], axis=1), cosine, sine)
    expand_low = jnp.concatenate(
        [key_grad[..., :NOPE].astype(BF16), value_grad], axis=-1
    ).reshape(group, e_width)

    latent_part = tail_dot(expand_low, weight_up)
    latent_sum = seq_scatter(jnp.concatenate([latent_part, rope_grad], axis=1), n_seq)
    normed_sum = seq_scatter(tail_dot(query_low, weight_q), n_seq)
    grad_q = lead_dot(normed_group, query_low)
    grad_up = lead_dot(latent, expand_low).reshape(width, -1)
    grad_joined = dp_scatter(jnp.concatenate([grad_q, grad_up], axis=1), n_dp, dp_index)
    grad_joined = grad_joined.reshape(n_seq, down_rows, joined_width)
    grad_joined = lax.all_to_all(grad_joined, "seq", split_axis=0, concat_axis=0, tiled=True)
    grad_q = jnp.swapaxes(grad_joined[..., :q_width], 0, 1).reshape(q_weight.shape)
    grad_up = grad_joined[..., q_width:].reshape(n_seq, kv_up.shape[0], e_width)
    grad_up = jnp.swapaxes(grad_up, 0, 1).reshape(kv_up.shape)

    latent_grad, gain_kv_grad = rms_back(latent_raw[:tokens], gain_kv, latent_sum[:, :KV_RANK])
    down_low = jnp.concatenate([latent_grad, latent_sum[:, KV_RANK:]], axis=1).astype(BF16)
    down_group = seq_gather(down_low, n_seq)
    normed_cols = normed_group.reshape(group, n_dp, n_seq, down_rows)
    normed_cols = lax.dynamic_index_in_dim(normed_cols, seq_index, 2, keepdims=False)
    grad_down = lead_dot(normed_cols.reshape(group, n_dp * down_rows), down_group)
    grad_down = dp_scatter(grad_down, n_dp, dp_index)

    normed_grad = normed_sum + tail_dot(down_low, weight_down)
    rows_from_norm, gain_attn_grad = rms_back(rows, gain_attn, normed_grad)
    input_grad = residual_grad + rows_from_norm

    gain_grads = jnp.concatenate(
        [
            gain_attn_grad.reshape(n_all, -1),
            gain_ffn_grad.reshape(n_all, -1),
            gain_kv_grad.reshape(n_all, -1),
        ],
        axis=1,
    )
    gain_grads = lax.all_to_all(gain_grads, BOTH, split_axis=0, concat_axis=0, tiled=True)
    gain_grads = jnp.sum(gain_grads, axis=0)
    attn_end = attn_gain.shape[0]
    ffn_end = attn_end + ffn_gain.shape[0]

    return (
        output,
        input_grad,
        gain_grads[:attn_end],
        grad_q,
        grad_down,
        gain_grads[ffn_end:],
        grad_up,
        grad_out_weight,
        gain_grads[attn_end:ffn_end],
        grad_shared_gate_up,
        grad_shared_down,
        grad_expert_in,
        grad_expert_down,
    )


def solution(mesh):
    rows = P(BOTH, None)
    return jax.shard_map(
        body,
        mesh=mesh,
        in_specs=(
            rows,
            rows,
            P(BOTH),
            rows,
            rows,
            P(BOTH),
            rows,
            rows,
            P(BOTH),
            rows,
            rows,
            P("dp", "seq", None),
            P("dp", "seq", None),
            P("dp", None),
            rows,
            P("dp", None),
        ),
        out_specs=(
            rows,
            rows,
            P(BOTH),
            rows,
            rows,
            P(BOTH),
            rows,
            rows,
            P(BOTH),
            rows,
            rows,
            P("dp", "seq", None),
            P("dp", "seq", None),
        ),
        check_vma=False,
    )
```

```python
import jax
import jax.numpy as jnp
import numpy as np
from jax import lax
from jax.experimental import pallas as pl
from jax.experimental.pallas import tpu as pltpu
from jax.sharding import PartitionSpec as P

H = 16
NOPE = 128
ROPE = 64
VD = 128
KV_RANK = 512
TOP = 6

EPS = 1e-06
THETA = 10000.0
GATE_UNIT = 16384.0

BOTH = ("dp", "seq")
F32 = jnp.float32
BF16 = jnp.bfloat16


def contract(left_side, right_side, left_dim, right_dim):
    return lax.dot_general(
        left_side,
        right_side,
        (((left_dim,), (right_dim,)), ((), ())),
        preferred_element_type=F32,
    )


def matmul(left_side, right_side):
    return contract(left_side, right_side, left_side.ndim - 1, 0)


def lead_dot(left_side, right_side):
    return contract(left_side, right_side, 0, 0)


def tail_dot(left_side, right_side):
    return contract(left_side, right_side, 1, 1)


def rms_scale(values):
    return lax.rsqrt(jnp.mean(values * values, axis=-1, keepdims=True) + EPS)


def rms_back(values, gain, grad):
    scale = rms_scale(values)
    unit = values * scale
    weighted = grad * gain
    centre = jnp.mean(weighted * unit, axis=-1, keepdims=True)
    return scale * (weighted - unit * centre), jnp.sum(grad * unit, axis=0)


def swiglu(gate, up):
    return jax.nn.silu(gate) * up


def swiglu_back(gate, up, grad):
    sig = jax.nn.sigmoid(gate)
    return grad * up * sig * (1.0 + gate * (1.0 - sig)), grad * (gate * sig)


def rotary_tables(positions):
    half_width = ROPE // 2
    frequency = THETA ** (-jnp.arange(half_width, dtype=F32) * 2.0 / ROPE)
    angles = positions.astype(F32)[:, None] * frequency[None, :]
    return jnp.cos(angles), jnp.sin(angles)


def rotate(values, cosine, sine):
    half_width = values.shape[-1] // 2
    lead = values[..., :half_width]
    trail = values[..., half_width:]
    return jnp.concatenate([lead * cosine - trail * sine, trail * cosine + lead * sine], axis=-1)


def rotate_back(grads, cosine, sine):
    return rotate(grads, cosine, -sine)


def link_orders(n_seq):
    bits = [1 << j for j in range(1, n_seq.bit_length() - 1)]
    return bits, bits[::-1]


def block_table(n_seq):
    orders = link_orders(n_seq)
    steps = len(orders[0])
    table = np.zeros((n_seq, n_seq), np.int32)
    for s in range(n_seq):
        for m in range(n_seq):
            core = (s & 1) ^ (m >> steps)
            other = (s & ~1) | core
            for j in range(steps):
                if m >> j & 1:
                    other ^= orders[core][j]
            table[s, m] = other
    return table


def seq_step(values, n_seq, step):
    orders = link_orders(n_seq)
    return lax.ppermute(values, "seq", [(s, s ^ orders[s & 1][step]) for s in range(n_seq)])


def core_swap(values, n_seq):
    return lax.ppermute(values, "seq", [(s, s ^ 1) for s in range(n_seq)])


def seq_gather(values, n_seq):
    current = values
    for step in range(len(link_orders(n_seq)[0])):
        current = jnp.concatenate([current, seq_step(current, n_seq, step)], axis=0)
    return jnp.concatenate([current, core_swap(current, n_seq)], axis=0)


def seq_scatter(values, n_seq):
    stages = []
    half = values.shape[0] // 2
    values = values.astype(BF16)
    total = values[:half].astype(F32) + core_swap(values[half:], n_seq).astype(F32)
    stages.append(total)
    for step in reversed(range(len(link_orders(n_seq)[0]))):
        half = total.shape[0] // 2
        sent = seq_step(total[half:].astype(BF16), n_seq, step)
        total = total[:half] + sent.astype(F32)
        stages.append(total)
    return stages


def hold(value, *until):
    return lax.optimization_barrier((value,) + until)[0]


def dp_swap(values, n_dp, step):
    return lax.ppermute(values, "dp", [(d, d ^ step) for d in range(n_dp)])


def dp_block(blocks, index):
    return lax.dynamic_index_in_dim(blocks, index, 0, keepdims=False)


def dp_exchange(blocks, n_dp, dp_index):
    moved = [dp_block(blocks, dp_index)]
    for step in range(1, n_dp):
        moved.append(dp_swap(dp_block(blocks, dp_index ^ step), n_dp, step))
    return moved


def in_order(moved, n_dp, dp_index):
    result = jnp.zeros((n_dp,) + moved[0].shape, moved[0].dtype)
    for step in range(n_dp):
        result = lax.dynamic_update_index_in_dim(result, moved[step], dp_index ^ step, 0)
    return result


def dp_gather(values, n_dp, dp_index):
    moved = [values] + [dp_swap(values, n_dp, step) for step in range(1, n_dp)]
    return in_order(moved, n_dp, dp_index)


def dp_scatter(values, n_dp, dp_index):
    blocks = values.reshape((n_dp, -1) + values.shape[1:])
    low = blocks.astype(BF16)
    total = dp_block(blocks, dp_index).astype(F32)
    for step in range(1, n_dp):
        total = total + dp_swap(dp_block(low, dp_index ^ step), n_dp, step).astype(F32)
    return total


def assemble_kernel(index_ref, *refs):
    pieces, out_ref = refs[:-1], refs[-1]
    count = len(pieces)
    per_device = out_ref.shape[1]
    part = pieces[0].shape[1] // 2
    values = [piece[...].astype(F32) for piece in pieces]
    for expert in range(per_device):
        gates, ups = [], []
        for ff in range(count // per_device):
            step = index_ref[0] ^ (ff * per_device + expert)
            chosen = values[0]
            for j in range(1, count):
                chosen = jnp.where(step == j, values[j], chosen)
            gates.append(chosen[:, :part])
            ups.append(chosen[:, part:])
        out_ref[:, expert, :] = jnp.concatenate(gates + ups, axis=1)


def assemble(pieces, dp_index, out_shape):
    rows, piece_width = pieces[0].shape
    step_rows = 64
    return pl.pallas_call(
        assemble_kernel,
        out_shape=jax.ShapeDtypeStruct(out_shape, F32),
        grid_spec=pltpu.PrefetchScalarGridSpec(
            num_scalar_prefetch=1,
            grid=(rows // step_rows,),
            in_specs=[pl.BlockSpec((step_rows, piece_width), lambda i, index: (i, 0))] * len(pieces),
            out_specs=pl.BlockSpec((step_rows,) + out_shape[1:], lambda i, index: (i, 0, 0)),
        ),
        compiler_params=pltpu.CompilerParams(vmem_limit_bytes=48 * 2**20),
        name="assemble",
    )(jnp.reshape(dp_index, (1,)).astype(jnp.int32), *pieces)


def body(
    hidden,
    cotangent,
    attn_gain,
    q_weight,
    kv_down,
    kv_gain,
    kv_up,
    out_weight,
    ffn_gain,
    shared_gate_up,
    shared_down,
    expert_gate_up,
    expert_down,
    expert_ids,
    gate_fix,
    block_ids,
):
    n_dp = lax.axis_size("dp")
    n_seq = lax.axis_size("seq")
    n_all = n_dp * n_seq
    dp_index = lax.axis_index("dp")
    seq_index = lax.axis_index("seq")
    tokens, width = hidden.shape
    sequences, length = block_ids.shape
    part = length // n_seq
    group = n_seq * tokens
    heads = H // n_seq
    per_device = expert_gate_up.shape[1]
    experts = per_device * n_seq
    capacity = TOP * tokens // per_device
    ff_parts = n_dp // per_device
    expert_bit = dp_index % per_device
    down_rows = kv_down.shape[0]
    down_width = kv_down.shape[1]
    q_width = heads * (NOPE + ROPE)
    e_width = heads * (NOPE + VD)
    block_at = dp_block(jnp.asarray(block_table(n_seq)), seq_index)
    block_of = dp_block(jnp.asarray(np.argsort(block_table(n_seq), axis=1)), seq_index)

    def relative(values):
        return jnp.take(values, block_at, axis=0, mode="clip")

    def absolute(values):
        return jnp.take(values, block_of, axis=0, mode="clip")

    up_rows = kv_up.reshape(kv_up.shape[0], n_seq, -1, kv_up.shape[0] * e_width // down_rows)
    up_rows = jnp.swapaxes(up_rows, 1, 2).reshape(down_rows, n_seq, -1)
    joined = jnp.concatenate([q_weight.reshape(down_rows, n_seq, q_width), up_rows], axis=2)
    joined_width = joined.shape[2]
    joined = lax.all_to_all(joined, "seq", split_axis=1, concat_axis=0, tiled=True)
    joined = joined.reshape(n_seq * down_rows, joined_width)
    joined = dp_gather(joined, n_dp, dp_index).reshape(-1, joined_width)
    weight_q = joined[:, :q_width]
    weight_up = joined[:, q_width:].reshape(KV_RANK, e_width)

    hidden_group = seq_gather(hidden, n_seq)

    labels = jnp.arange(experts, dtype=jnp.int32)
    hits = jnp.sum((expert_ids[:, :, None] == labels).astype(jnp.int32), axis=1)
    earlier = jnp.arange(group, dtype=jnp.int32)[:, None] < seq_index * tokens
    before_own = jnp.sum(jnp.where(earlier, hits, 0), axis=0)
    own_hits = lax.dynamic_slice_in_dim(hits, seq_index * tokens, tokens, 0)
    own_picks = lax.dynamic_slice_in_dim(expert_ids, seq_index * tokens, tokens, 0)
    own_slot = before_own[None, :] + jnp.cumsum(own_hits, axis=0) - own_hits
    code = jnp.where((own_hits > 0) & (own_slot < capacity), own_slot + 1, 0)
    gates = jnp.sum(
        gate_fix[:, :, None] * (own_picks[:, :, None] == labels).astype(jnp.int32), axis=1
    )
    pieces = jnp.stack([code // 16, code % 16, gates // 128, gates % 128], axis=0)
    pieces = jnp.transpose(pieces, (2, 0, 1)).reshape(experts, 4 * tokens).astype(BF16)

    def wide_row(vector):
        return jnp.pad(vector, (0, down_width - 4 * tokens - vector.shape[0]))[None]

    extras = jnp.concatenate([wide_row(attn_gain), wide_row(ffn_gain), wide_row(kv_gain)], axis=0)
    extras = jnp.pad(extras, ((0, experts - 3), (0, 0)))
    message = jnp.concatenate(
        [kv_down, jnp.concatenate([pieces, extras], axis=1)], axis=0
    )
    spread = lax.all_gather(message, BOTH, axis=0, tiled=False)
    weight_down = spread[:, :down_rows].reshape(-1, down_width)
    spread_tail = spread[:, down_rows:]
    first = 4 * tokens
    gain_attn = spread_tail[:, 0, first : first + attn_gain.shape[0]].reshape(-1).astype(F32)
    gain_ffn = spread_tail[:, 1, first : first + ffn_gain.shape[0]].reshape(-1).astype(F32)
    gain_kv = spread_tail[:, 2, first : first + kv_gain.shape[0]].reshape(-1).astype(F32)
    own_expert = per_device * seq_index + expert_bit
    routing = lax.dynamic_index_in_dim(spread_tail, own_expert, axis=1, keepdims=False)
    routing = routing[:, :first].reshape(n_dp, n_seq, 4, tokens).astype(jnp.int32)
    slot_code = routing[:, :, 0] * 16 + routing[:, :, 1]
    gate_of = (routing[:, :, 2] * 128 + routing[:, :, 3]).astype(F32) / GATE_UNIT

    weight_out = lax.all_gather(hold(out_weight, spread), BOTH, axis=0, tiled=True)
    cot_all = lax.all_gather(hold(cotangent, weight_out), BOTH, axis=0, tiled=True)

    ff_width = expert_gate_up.shape[2] // 2
    ff_part = ff_width // ff_parts
    expert_rows = expert_gate_up.shape[0]
    in_parts = expert_gate_up.reshape(expert_rows, per_device, 2, ff_parts, ff_part)
    in_parts = jnp.transpose(in_parts, (3, 1, 0, 2, 4)).reshape(n_dp, expert_rows, 2 * ff_part)
    in_moved = dp_exchange(hold(in_parts, joined), n_dp, dp_index)
    down_kept = lax.dynamic_index_in_dim(expert_down, expert_bit, 1, keepdims=False)
    down_sent = lax.dynamic_index_in_dim(expert_down, 1 - expert_bit, 1, keepdims=False)
    down_got = dp_swap(hold(down_sent, joined), n_dp, 1)
    is_low = expert_bit == 0

    units = shared_down.shape[0]
    gate_up_parts = shared_gate_up.reshape(-1, 2, n_all, units)
    gate_up_parts = jnp.transpose(gate_up_parts, (2, 0, 1, 3)).reshape(n_all, -1, 2 * units)
    gate_up_parts = hold(gate_up_parts, joined)
    weight_shared_in = lax.all_to_all(
        gate_up_parts, BOTH, split_axis=0, concat_axis=0, tiled=True
    ).reshape(-1, 2 * units)

    def chunk_gather(values):
        sent = [values] + [dp_swap(values, n_dp, step) for step in range(1, n_dp)]
        return [seq_gather(piece, n_seq) for piece in sent]

    rows_group = hidden_group.astype(F32)
    normed_group = (rows_group * rms_scale(rows_group) * gain_attn).astype(BF16)
    in_part = jnp.arange(tokens, dtype=jnp.int32) % part
    positions = (block_at[:, None] * part + in_part[None, :]).reshape(group)
    cosine, sine = rotary_tables(positions)

    def to_sequence(values):
        split = values.reshape((n_seq, sequences, part) + values.shape[1:])
        return jnp.swapaxes(split, 0, 1).reshape((sequences, length) + values.shape[1:])

    def to_rows(values):
        split = values.reshape((sequences, n_seq, part) + values.shape[2:])
        return jnp.swapaxes(split, 0, 1).reshape((group,) + values.shape[2:])

    query_raw = matmul(normed_group, weight_q).reshape(group, heads, NOPE + ROPE)
    latent_in = matmul(normed_group, weight_down)
    latent_raw = latent_in[:, :KV_RANK]
    latent = (latent_raw * rms_scale(latent_raw) * gain_kv).astype(BF16)
    expanded = matmul(latent, weight_up).reshape(group, heads, NOPE + VD)
    rope_query = rotate(query_raw[..., NOPE:], cosine[:, None], sine[:, None])
    rope_key = rotate(latent_in[:, KV_RANK:], cosine, sine)
    rope_key = jnp.broadcast_to(rope_key[:, None], (group, heads, ROPE))
    queries = to_sequence(
        jnp.concatenate([query_raw[..., :NOPE], rope_query], axis=-1).astype(BF16)
    )
    keys = to_sequence(
        jnp.concatenate([expanded[..., :NOPE], rope_key], axis=-1).astype(BF16)
    )
    values = to_sequence(expanded[..., NOPE:].astype(BF16))
    blocks = jnp.take(block_ids.reshape(sequences, n_seq, part), block_at, axis=1, mode="clip")
    blocks = blocks.reshape(sequences, length)
    score_scale = (NOPE + ROPE) ** (-0.5)
    scores = jnp.einsum("bqhd,bkhd->bhqk", queries, keys, preferred_element_type=F32) * score_scale
    allowed = blocks[:, None, None, :] <= blocks[:, None, :, None]
    scores = jnp.where(allowed, scores, -1e30)
    weights = jnp.exp(scores - jnp.max(scores, axis=-1, keepdims=True))
    probs = weights / jnp.sum(weights, axis=-1, keepdims=True)
    shares = probs.astype(BF16)
    attended = jnp.einsum("bhqk,bkhd->bqhd", shares, values, preferred_element_type=F32)
    attended = to_rows(attended.astype(BF16)).reshape(group, heads * VD)
    heads_out = absolute(attended.reshape(n_seq, tokens, heads * VD))
    heads_out = lax.all_to_all(heads_out, "seq", split_axis=0, concat_axis=2, tiled=True)
    heads_out = heads_out.reshape(tokens, H * VD)

    rows = hidden.astype(F32)
    residual = rows + matmul(heads_out, weight_out)
    normed_ffn = (residual * rms_scale(residual) * gain_ffn).astype(BF16)

    slots = jnp.arange(1, capacity + 1, dtype=jnp.int32)
    all_codes = slot_code.reshape(n_dp, group)
    all_here = all_codes[:, :, None] == slots
    slot_gate = jnp.where(all_here, gate_of.reshape(n_dp, group)[:, :, None], 0.0)
    slot_gate = jnp.sum(slot_gate, axis=1)[:, :, None]
    all_placed = lax.optimization_barrier(all_here.astype(BF16))
    cot_rows = cot_all.reshape(n_dp, group, width)
    slot_cot = jnp.einsum("gtc,gtd->gcd", all_placed, cot_rows, preferred_element_type=F32)
    slot_cot = (slot_cot * slot_gate).astype(BF16)
    down_kept, down_got = hold((down_kept, down_got), normed_ffn)
    weight_back = jnp.concatenate(
        [jnp.where(is_low, down_kept, down_got), jnp.where(is_low, down_got, down_kept)], axis=0
    )
    expert_act_grad = contract(slot_cot, weight_back, 2, 1)
    shared_act_grad = contract(cot_rows, shared_down, 2, 1)

    in_moved = hold(in_moved, normed_ffn)
    weight_in = in_order(in_moved, n_dp, dp_index).reshape(-1, 2 * ff_part)
    ffn_chunks = chunk_gather(normed_ffn)
    shared_in_back = weight_shared_in.T
    grad_shared_in = 0.0
    kept_rows, kept_acts, kept_grads = [], [], []
    kept_shared, shared_acts, planes = [], [], []
    dn_part = None
    for step in range(n_dp):
        ffn_rows = ffn_chunks[step]
        codes = relative(dp_block(slot_code, dp_index ^ step)).reshape(group)
        placed = lax.optimization_barrier((codes[:, None] == slots).astype(BF16))

        shared_in = matmul(ffn_rows, weight_shared_in)
        shared_gate, shared_up = shared_in[:, :units], shared_in[:, units:]
        act_grad = dp_block(shared_act_grad, dp_index ^ step)
        act_grad = relative(act_grad.reshape(n_seq, tokens, units)).reshape(group, units)
        shared_in_grad = jnp.concatenate(
            swiglu_back(shared_gate, shared_up, act_grad), axis=1
        ).astype(BF16)
        kept_shared.append(shared_in_grad)
        shared_acts.append(swiglu(shared_gate, shared_up).astype(BF16))

        slot_rows = lead_dot(placed, ffn_rows).astype(BF16)
        expert_in = matmul(slot_rows, weight_in)
        expert_gate, expert_up = expert_in[:, :ff_part], expert_in[:, ff_part:]
        expert_in_grad = jnp.concatenate(
            swiglu_back(expert_gate, expert_up, dp_block(expert_act_grad, dp_index ^ step)), axis=1
        ).astype(BF16)
        slot_grad = tail_dot(expert_in_grad, weight_in).astype(BF16)
        for age in range(1, min(step, 3) + 1):
            placed = hold(placed, planes[step - age][age - 1])
        dn_part = matmul(
            jnp.concatenate([placed, shared_in_grad], axis=1),
            jnp.concatenate([slot_grad, shared_in_back], axis=0),
        ).astype(BF16)
        planes.append(seq_scatter(dn_part, n_seq))

        kept_rows.append(slot_rows)
        kept_acts.append(swiglu(expert_gate, expert_up).astype(BF16))
        kept_grads.append(expert_in_grad)
    ffn_grad = planes[0][-1]
    for step in range(1, n_dp):
        ffn_grad = ffn_grad + dp_swap(planes[step][-1].astype(BF16), n_dp, step).astype(F32)

    kept_rows, kept_acts, kept_grads, shared_acts, ffn_chunks = hold(
        (kept_rows, kept_acts, kept_grads, shared_acts, ffn_chunks), dn_part
    )
    grad_in = lead_dot(jnp.concatenate(kept_rows), jnp.concatenate(kept_grads)).astype(BF16)
    in_back = dp_exchange(grad_in.reshape(n_dp, expert_rows, 2 * ff_part), n_dp, dp_index)
    expert_act = in_order(kept_acts, n_dp, dp_index)
    grad_back = lead_dot(
        expert_act.reshape(n_dp * capacity, ff_part), slot_cot.reshape(n_dp * capacity, width)
    )
    half = expert_down.shape[0]
    low_half, high_half = grad_back[:half], grad_back[half:]
    grad_kept = jnp.where(is_low, low_half, high_half)
    grad_sent = jnp.where(is_low, high_half, low_half).astype(BF16)
    grad_got = dp_swap(grad_sent, n_dp, 1)
    shared_act = in_order(
        [absolute(act.reshape(n_seq, tokens, units)) for act in shared_acts], n_dp, dp_index
    ).reshape(n_dp, group, units)
    expert_out = (contract(expert_act, weight_back, 2, 0) * slot_gate).astype(BF16)
    out_part = jnp.einsum(
        "gtk,gkd->gtd",
        jnp.concatenate([all_placed, shared_act], axis=2),
        jnp.concatenate(
            [expert_out, jnp.broadcast_to(shared_down, (n_dp, units, width))], axis=1
        ),
        preferred_element_type=F32,
    ).astype(BF16)
    out_sum = lax.psum_scatter(
        out_part.reshape(n_all * tokens, width), BOTH, scatter_dimension=0, tiled=True
    )
    output = (residual + out_sum.astype(F32)).astype(BF16)
    grad_shared_down = lead_dot(shared_act.reshape(n_all * tokens, units), cot_all)
    for step in range(n_dp):
        grad_shared_in = grad_shared_in + lead_dot(ffn_chunks[step], kept_shared[step])

    from_norm, gain_ffn_grad = rms_back(residual, gain_ffn, ffn_grad)
    residual_grad = cotangent.astype(F32) + from_norm
    residual_low = residual_grad.astype(BF16)
    heads_grad = tail_dot(residual_low, weight_out).astype(BF16)
    heads_grad = heads_grad.reshape(tokens, n_seq, heads * VD)
    heads_grad = lax.all_to_all(heads_grad, "seq", split_axis=1, concat_axis=0, tiled=True)
    residual_group = seq_gather(hold(residual_low, heads_grad), n_seq)
    grad_shared_in = hold(grad_shared_in.astype(BF16), heads_grad)
    shared_back = lax.all_to_all(
        grad_shared_in.reshape(n_all, -1, 2 * units), BOTH, split_axis=0, concat_axis=0, tiled=True
    )
    heads_grad = relative(heads_grad.reshape(n_seq, tokens, heads * VD))
    grad_out_heads = lead_dot(attended, residual_group)
    out_shard = dp_scatter(grad_out_heads, n_dp, dp_index)
    home = [
        (d * n_seq + s, s * n_dp + d) for d in range(n_dp) for s in range(n_seq)
    ]
    grad_out_weight = lax.ppermute(out_shard, BOTH, home)

    grad_o = to_sequence(heads_grad.reshape(group, heads, VD))
    prob_grad = jnp.einsum("bqhd,bkhd->bhqk", grad_o, values, preferred_element_type=F32)
    centre = jnp.sum(probs * prob_grad, axis=-1, keepdims=True)
    score_grad = (probs * (prob_grad - centre)).astype(BF16)
    query_grad = jnp.einsum("bhqk,bkhd->bqhd", score_grad, keys, preferred_element_type=F32)
    key_grad = jnp.einsum("bhqk,bqhd->bkhd", score_grad, queries, preferred_element_type=F32)
    value_grad = jnp.einsum("bhqk,bqhd->bkhd", shares, grad_o, preferred_element_type=F32)
    query_grad = to_rows((query_grad * score_scale).astype(BF16)).astype(F32)
    key_grad = to_rows((key_grad * score_scale).astype(BF16)).astype(F32)
    value_grad = to_rows(value_grad.astype(BF16))
    query_low = jnp.concatenate(
        [
            query_grad[..., :NOPE],
            rotate_back(query_grad[..., NOPE:], cosine[:, None], sine[:, None]),
        ],
        axis=-1,
    ).astype(BF16).reshape(group, q_width)
    rope_grad = rotate_back(jnp.sum(key_grad[..., NOPE:], axis=1), cosine, sine)
    expand_low = jnp.concatenate(
        [key_grad[..., :NOPE].astype(BF16), value_grad], axis=-1
    ).reshape(group, e_width)

    latent_part = tail_dot(expand_low, weight_up)
    latent_sum = seq_scatter(jnp.concatenate([latent_part, rope_grad], axis=1), n_seq)[-1]
    normed_sum = seq_scatter(tail_dot(query_low, weight_q), n_seq)[-1]
    grad_q = lead_dot(normed_group, query_low)
    grad_up = lead_dot(latent, expand_low).reshape(width, -1)
    grad_joined = dp_scatter(jnp.concatenate([grad_q, grad_up], axis=1), n_dp, dp_index)
    grad_joined = grad_joined.reshape(n_seq, down_rows, joined_width)
    grad_joined = lax.all_to_all(grad_joined, "seq", split_axis=0, concat_axis=0, tiled=True)
    grad_q = jnp.swapaxes(grad_joined[..., :q_width], 0, 1).reshape(q_weight.shape)
    grad_up = grad_joined[..., q_width:].reshape(n_seq, kv_up.shape[0], e_width)
    grad_up = jnp.swapaxes(grad_up, 0, 1).reshape(kv_up.shape)

    latent_grad, gain_kv_grad = rms_back(latent_raw[:tokens], gain_kv, latent_sum[:, :KV_RANK])
    down_low = jnp.concatenate([latent_grad, latent_sum[:, KV_RANK:]], axis=1).astype(BF16)
    down_group = seq_gather(down_low, n_seq)
    normed_cols = normed_group.reshape(group, n_dp, n_seq, down_rows)
    normed_cols = lax.dynamic_index_in_dim(normed_cols, seq_index, 2, keepdims=False)
    grad_down = lead_dot(normed_cols.reshape(group, n_dp * down_rows), down_group)
    grad_down = dp_scatter(grad_down, n_dp, dp_index)

    in_back, grad_got, shared_back = hold((in_back, grad_got, shared_back), down_low)
    grad_expert_in = assemble(in_back, dp_index, expert_gate_up.shape)
    grad_got = grad_got.astype(F32)
    grad_expert_down = jnp.stack(
        [jnp.where(is_low, grad_kept, grad_got), jnp.where(is_low, grad_got, grad_kept)], axis=1
    )
    shared_back = shared_back.reshape(n_all, -1, 2, units).astype(F32)
    grad_shared_gate_up = jnp.transpose(shared_back, (1, 2, 0, 3)).reshape(shared_gate_up.shape)

    normed_grad = normed_sum + tail_dot(down_low, weight_down)
    rows_from_norm, gain_attn_grad = rms_back(rows, gain_attn, normed_grad)
    input_grad = residual_grad + rows_from_norm

    gain_grads = jnp.concatenate(
        [
            gain_attn_grad.reshape(n_all, -1),
            gain_ffn_grad.reshape(n_all, -1),
            gain_kv_grad.reshape(n_all, -1),
        ],
        axis=1,
    )
    gain_grads = lax.all_to_all(gain_grads, BOTH, split_axis=0, concat_axis=0, tiled=True)
    gain_grads = jnp.sum(gain_grads, axis=0)
    attn_end = attn_gain.shape[0]
    ffn_end = attn_end + ffn_gain.shape[0]

    return (
        output,
        input_grad,
        gain_grads[:attn_end],
        grad_q,
        grad_down,
        gain_grads[ffn_end:],
        grad_up,
        grad_out_weight,
        gain_grads[attn_end:ffn_end],
        grad_shared_gate_up,
        grad_shared_down,
        grad_expert_in,
        grad_expert_down,
    )


def solution(mesh):
    rows = P(BOTH, None)
    return jax.shard_map(
        body,
        mesh=mesh,
        in_specs=(
            rows,
            rows,
            P(BOTH),
            rows,
            rows,
            P(BOTH),
            rows,
            rows,
            P(BOTH),
            rows,
            rows,
            P("dp", "seq", None),
            P("dp", "seq", None),
            P("dp", None),
            rows,
            P("dp", None),
        ),
        out_specs=(
            rows,
            rows,
            P(BOTH),
            rows,
            rows,
            P(BOTH),
            rows,
            rows,
            P(BOTH),
            rows,
            rows,
            P("dp", "seq", None),
            P("dp", "seq", None),
        ),
        check_vma=False,
    )
```

```python
import jax
import jax.numpy as jnp
import numpy as np
from jax import lax
from jax.experimental import pallas as pl
from jax.experimental.pallas import tpu as pltpu
from jax.sharding import PartitionSpec as P

H = 16
NOPE = 128
ROPE = 64
VD = 128
KV_RANK = 512
TOP = 6

EPS = 1e-06
THETA = 10000.0
GATE_UNIT = 16384.0

BOTH = ("dp", "seq")
F32 = jnp.float32
BF16 = jnp.bfloat16


def contract(left_side, right_side, left_dim, right_dim):
    return lax.dot_general(
        left_side,
        right_side,
        (((left_dim,), (right_dim,)), ((), ())),
        preferred_element_type=F32,
    )


def matmul(left_side, right_side):
    return contract(left_side, right_side, left_side.ndim - 1, 0)


def lead_dot(left_side, right_side):
    return contract(left_side, right_side, 0, 0)


def tail_dot(left_side, right_side):
    return contract(left_side, right_side, 1, 1)


def rms_scale(values):
    return lax.rsqrt(jnp.mean(values * values, axis=-1, keepdims=True) + EPS)


def rms_back(values, gain, grad):
    scale = rms_scale(values)
    unit = values * scale
    weighted = grad * gain
    centre = jnp.mean(weighted * unit, axis=-1, keepdims=True)
    return scale * (weighted - unit * centre), jnp.sum(grad * unit, axis=0)


def swiglu(gate, up):
    return jax.nn.silu(gate) * up


def swiglu_back(gate, up, grad):
    sig = jax.nn.sigmoid(gate)
    return grad * up * sig * (1.0 + gate * (1.0 - sig)), grad * (gate * sig)


def rotary_tables(positions):
    half_width = ROPE // 2
    frequency = THETA ** (-jnp.arange(half_width, dtype=F32) * 2.0 / ROPE)
    angles = positions.astype(F32)[:, None] * frequency[None, :]
    return jnp.cos(angles), jnp.sin(angles)


def rotate(values, cosine, sine):
    half_width = values.shape[-1] // 2
    lead = values[..., :half_width]
    trail = values[..., half_width:]
    return jnp.concatenate([lead * cosine - trail * sine, trail * cosine + lead * sine], axis=-1)


def rotate_back(grads, cosine, sine):
    return rotate(grads, cosine, -sine)


def link_orders(n_seq):
    bits = [1 << j for j in range(1, n_seq.bit_length() - 1)]
    return bits, bits[::-1]


def block_table(n_seq):
    orders = link_orders(n_seq)
    steps = len(orders[0])
    table = np.zeros((n_seq, n_seq), np.int32)
    for s in range(n_seq):
        for m in range(n_seq):
            core = (s & 1) ^ (m >> steps)
            other = (s & ~1) | core
            for j in range(steps):
                if m >> j & 1:
                    other ^= orders[core][j]
            table[s, m] = other
    return table


def seq_step(values, n_seq, step):
    orders = link_orders(n_seq)
    return lax.ppermute(values, "seq", [(s, s ^ orders[s & 1][step]) for s in range(n_seq)])


def core_swap(values, n_seq):
    return lax.ppermute(values, "seq", [(s, s ^ 1) for s in range(n_seq)])


def seq_gather(values, n_seq):
    current = values
    for step in range(len(link_orders(n_seq)[0])):
        current = jnp.concatenate([current, seq_step(current, n_seq, step)], axis=0)
    return jnp.concatenate([current, core_swap(current, n_seq)], axis=0)


def seq_scatter(values, n_seq):
    stages = []
    half = values.shape[0] // 2
    values = values.astype(BF16)
    total = values[:half].astype(F32) + core_swap(values[half:], n_seq).astype(F32)
    stages.append(total)
    for step in reversed(range(len(link_orders(n_seq)[0]))):
        half = total.shape[0] // 2
        sent = seq_step(total[half:].astype(BF16), n_seq, step)
        total = total[:half] + sent.astype(F32)
        stages.append(total)
    return stages


def hold(value, *until):
    return lax.optimization_barrier((value,) + until)[0]


def dp_swap(values, n_dp, step):
    return lax.ppermute(values, "dp", [(d, d ^ step) for d in range(n_dp)])


def dp_block(blocks, index):
    return lax.dynamic_index_in_dim(blocks, index, 0, keepdims=False)


def dp_exchange(blocks, n_dp, dp_index, steps, until):
    blocks = hold(blocks, until)
    return {
        step: dp_swap(dp_block(blocks, dp_index ^ step), n_dp, step) for step in steps
    }


def in_order(moved, n_dp, dp_index):
    result = jnp.zeros((n_dp,) + moved[0].shape, moved[0].dtype)
    for step in range(n_dp):
        result = lax.dynamic_update_index_in_dim(result, moved[step], dp_index ^ step, 0)
    return result


def dp_gather(values, n_dp, dp_index):
    moved = [values] + [dp_swap(values, n_dp, step) for step in range(1, n_dp)]
    return in_order(moved, n_dp, dp_index)


def dp_scatter(values, n_dp, dp_index):
    blocks = values.reshape((n_dp, -1) + values.shape[1:])
    low = blocks.astype(BF16)
    total = dp_block(blocks, dp_index).astype(F32)
    for step in range(1, n_dp):
        total = total + dp_swap(dp_block(low, dp_index ^ step), n_dp, step).astype(F32)
    return total


def assemble_kernel(index_ref, *refs):
    pieces, out_ref = refs[:-1], refs[-1]
    count = len(pieces)
    per_device = out_ref.shape[1]
    part = pieces[0].shape[1] // 2
    values = [piece[...].astype(F32) for piece in pieces]
    for expert in range(per_device):
        gates, ups = [], []
        for ff in range(count // per_device):
            step = index_ref[0] ^ (ff * per_device + expert)
            chosen = values[0]
            for j in range(1, count):
                chosen = jnp.where(step == j, values[j], chosen)
            gates.append(chosen[:, :part])
            ups.append(chosen[:, part:])
        out_ref[:, expert, :] = jnp.concatenate(gates + ups, axis=1)


def assemble(pieces, dp_index, out_shape):
    rows, piece_width = pieces[0].shape
    step_rows = 64
    return pl.pallas_call(
        assemble_kernel,
        out_shape=jax.ShapeDtypeStruct(out_shape, F32),
        grid_spec=pltpu.PrefetchScalarGridSpec(
            num_scalar_prefetch=1,
            grid=(rows // step_rows,),
            in_specs=[pl.BlockSpec((step_rows, piece_width), lambda i, index: (i, 0))] * len(pieces),
            out_specs=pl.BlockSpec((step_rows,) + out_shape[1:], lambda i, index: (i, 0, 0)),
        ),
        compiler_params=pltpu.CompilerParams(vmem_limit_bytes=48 * 2**20),
        name="assemble",
    )(jnp.reshape(dp_index, (1,)).astype(jnp.int32), *pieces)


def body(
    hidden,
    cotangent,
    attn_gain,
    q_weight,
    kv_down,
    kv_gain,
    kv_up,
    out_weight,
    ffn_gain,
    shared_gate_up,
    shared_down,
    expert_gate_up,
    expert_down,
    expert_ids,
    gate_fix,
    block_ids,
):
    n_dp = lax.axis_size("dp")
    n_seq = lax.axis_size("seq")
    n_all = n_dp * n_seq
    dp_index = lax.axis_index("dp")
    seq_index = lax.axis_index("seq")
    tokens, width = hidden.shape
    sequences, length = block_ids.shape
    part = length // n_seq
    group = n_seq * tokens
    heads = H // n_seq
    per_device = expert_gate_up.shape[1]
    experts = per_device * n_seq
    capacity = TOP * tokens // per_device
    ff_parts = n_dp // per_device
    expert_bit = dp_index % per_device
    down_rows = kv_down.shape[0]
    down_width = kv_down.shape[1]
    q_width = heads * (NOPE + ROPE)
    e_width = heads * (NOPE + VD)
    block_at = dp_block(jnp.asarray(block_table(n_seq)), seq_index)
    block_of = dp_block(jnp.asarray(np.argsort(block_table(n_seq), axis=1)), seq_index)

    def relative(values):
        return jnp.take(values, block_at, axis=0, mode="clip")

    def absolute(values):
        return jnp.take(values, block_of, axis=0, mode="clip")

    up_rows = kv_up.reshape(kv_up.shape[0], n_seq, -1, kv_up.shape[0] * e_width // down_rows)
    up_rows = jnp.swapaxes(up_rows, 1, 2).reshape(down_rows, n_seq, -1)
    joined = jnp.concatenate([q_weight.reshape(down_rows, n_seq, q_width), up_rows], axis=2)
    joined_width = joined.shape[2]
    joined = lax.all_to_all(joined, "seq", split_axis=1, concat_axis=0, tiled=True)
    joined_here = joined
    joined = joined.reshape(n_seq * down_rows, joined_width)
    joined = dp_gather(joined, n_dp, dp_index).reshape(-1, joined_width)
    weight_q = joined[:, :q_width]
    weight_up = joined[:, q_width:].reshape(KV_RANK, e_width)

    hidden_group = seq_gather(hidden, n_seq)

    labels = jnp.arange(experts, dtype=jnp.int32)
    hits = jnp.sum((expert_ids[:, :, None] == labels).astype(jnp.int32), axis=1)
    earlier = jnp.arange(group, dtype=jnp.int32)[:, None] < seq_index * tokens
    before_own = jnp.sum(jnp.where(earlier, hits, 0), axis=0)
    own_hits = lax.dynamic_slice_in_dim(hits, seq_index * tokens, tokens, 0)
    own_picks = lax.dynamic_slice_in_dim(expert_ids, seq_index * tokens, tokens, 0)
    own_slot = before_own[None, :] + jnp.cumsum(own_hits, axis=0) - own_hits
    code = jnp.where((own_hits > 0) & (own_slot < capacity), own_slot + 1, 0)
    gates = jnp.sum(
        gate_fix[:, :, None] * (own_picks[:, :, None] == labels).astype(jnp.int32), axis=1
    )
    pieces = jnp.stack([code // 16, code % 16, gates // 128, gates % 128], axis=0)
    pieces = jnp.transpose(pieces, (2, 0, 1)).reshape(experts, 4 * tokens).astype(BF16)

    def wide_row(vector):
        return jnp.pad(vector, (0, down_width - 4 * tokens - vector.shape[0]))[None]

    extras = jnp.concatenate([wide_row(attn_gain), wide_row(ffn_gain), wide_row(kv_gain)], axis=0)
    extras = jnp.pad(extras, ((0, experts - 3), (0, 0)))
    message = jnp.concatenate(
        [kv_down, jnp.concatenate([pieces, extras], axis=1)], axis=0
    )
    spread = lax.all_gather(message, BOTH, axis=0, tiled=False)
    weight_down = spread[:, :down_rows].reshape(-1, down_width)
    spread_tail = spread[:, down_rows:]
    first = 4 * tokens
    gain_attn = spread_tail[:, 0, first : first + attn_gain.shape[0]].reshape(-1).astype(F32)
    gain_ffn = spread_tail[:, 1, first : first + ffn_gain.shape[0]].reshape(-1).astype(F32)
    gain_kv = spread_tail[:, 2, first : first + kv_gain.shape[0]].reshape(-1).astype(F32)
    own_expert = per_device * seq_index + expert_bit
    routing = lax.dynamic_index_in_dim(spread_tail, own_expert, axis=1, keepdims=False)
    routing = routing[:, :first].reshape(n_dp, n_seq, 4, tokens).astype(jnp.int32)
    slot_code = routing[:, :, 0] * 16 + routing[:, :, 1]
    gate_of = (routing[:, :, 2] * 128 + routing[:, :, 3]).astype(F32) / GATE_UNIT

    weight_out = lax.all_gather(hold(out_weight, joined_here), BOTH, axis=0, tiled=True)
    cot_all = lax.all_gather(hold(cotangent, joined, hidden_group), BOTH, axis=0, tiled=True)

    ff_width = expert_gate_up.shape[2] // 2
    ff_part = ff_width // ff_parts
    expert_rows = expert_gate_up.shape[0]
    in_parts = expert_gate_up.reshape(expert_rows, per_device, 2, ff_parts, ff_part)
    in_parts = jnp.transpose(in_parts, (3, 1, 0, 2, 4)).reshape(n_dp, expert_rows, 2 * ff_part)
    even_steps, odd_steps = range(2, n_dp, 2), range(1, n_dp, 2)
    in_even = dp_exchange(in_parts, n_dp, dp_index, even_steps, joined)
    in_odd = dp_exchange(in_parts, n_dp, dp_index, odd_steps, in_even)
    in_moved = in_even | in_odd
    in_moved[0] = dp_block(in_parts, dp_index)
    down_kept = lax.dynamic_index_in_dim(expert_down, expert_bit, 1, keepdims=False)
    down_sent = lax.dynamic_index_in_dim(expert_down, 1 - expert_bit, 1, keepdims=False)
    down_got = dp_swap(hold(down_sent, joined), n_dp, 1)
    is_low = expert_bit == 0

    units = shared_down.shape[0]
    gate_up_parts = shared_gate_up.reshape(-1, 2, n_all, units)
    gate_up_parts = jnp.transpose(gate_up_parts, (2, 0, 1, 3)).reshape(n_all, -1, 2 * units)
    gate_up_parts = hold(gate_up_parts, joined_here)
    weight_shared_in = lax.all_to_all(
        gate_up_parts, BOTH, split_axis=0, concat_axis=0, tiled=True
    ).reshape(-1, 2 * units)

    def chunk_gather(values):
        far = hold(values, in_odd)
        sent = [values] + [dp_swap(far, n_dp, step) for step in range(1, n_dp)]
        return [seq_gather(piece, n_seq) for piece in sent]

    rows_group = hidden_group.astype(F32)
    normed_group = (rows_group * rms_scale(rows_group) * gain_attn).astype(BF16)
    in_part = jnp.arange(tokens, dtype=jnp.int32) % part
    positions = (block_at[:, None] * part + in_part[None, :]).reshape(group)
    cosine, sine = rotary_tables(positions)

    def to_sequence(values):
        split = values.reshape((n_seq, sequences, part) + values.shape[1:])
        return jnp.swapaxes(split, 0, 1).reshape((sequences, length) + values.shape[1:])

    def to_rows(values):
        split = values.reshape((sequences, n_seq, part) + values.shape[2:])
        return jnp.swapaxes(split, 0, 1).reshape((group,) + values.shape[2:])

    query_raw = matmul(normed_group, weight_q).reshape(group, heads, NOPE + ROPE)
    latent_in = matmul(normed_group, weight_down)
    latent_raw = latent_in[:, :KV_RANK]
    latent = (latent_raw * rms_scale(latent_raw) * gain_kv).astype(BF16)
    expanded = matmul(latent, weight_up).reshape(group, heads, NOPE + VD)
    rope_query = rotate(query_raw[..., NOPE:], cosine[:, None], sine[:, None])
    rope_key = rotate(latent_in[:, KV_RANK:], cosine, sine)
    rope_key = jnp.broadcast_to(rope_key[:, None], (group, heads, ROPE))
    queries = to_sequence(
        jnp.concatenate([query_raw[..., :NOPE], rope_query], axis=-1).astype(BF16)
    )
    keys = to_sequence(
        jnp.concatenate([expanded[..., :NOPE], rope_key], axis=-1).astype(BF16)
    )
    values = to_sequence(expanded[..., NOPE:].astype(BF16))
    blocks = jnp.take(block_ids.reshape(sequences, n_seq, part), block_at, axis=1, mode="clip")
    blocks = blocks.reshape(sequences, length)
    score_scale = (NOPE + ROPE) ** (-0.5)
    scores = jnp.einsum("bqhd,bkhd->bhqk", queries, keys, preferred_element_type=F32) * score_scale
    allowed = blocks[:, None, None, :] <= blocks[:, None, :, None]
    scores = jnp.where(allowed, scores, -1e30)
    weights = jnp.exp(scores - jnp.max(scores, axis=-1, keepdims=True))
    probs = weights / jnp.sum(weights, axis=-1, keepdims=True)
    shares = probs.astype(BF16)
    attended = jnp.einsum("bhqk,bkhd->bqhd", shares, values, preferred_element_type=F32)
    attended = to_rows(attended.astype(BF16)).reshape(group, heads * VD)
    attended = hold(attended, in_even, down_got)
    heads_out = absolute(attended.reshape(n_seq, tokens, heads * VD))
    heads_out = lax.all_to_all(heads_out, "seq", split_axis=0, concat_axis=2, tiled=True)
    heads_out = heads_out.reshape(tokens, H * VD)

    rows = hidden.astype(F32)
    residual = rows + matmul(heads_out, weight_out)
    normed_ffn = (residual * rms_scale(residual) * gain_ffn).astype(BF16)

    slots = jnp.arange(1, capacity + 1, dtype=jnp.int32)
    all_codes = slot_code.reshape(n_dp, group)
    all_here = all_codes[:, :, None] == slots
    slot_gate = jnp.where(all_here, gate_of.reshape(n_dp, group)[:, :, None], 0.0)
    slot_gate = jnp.sum(slot_gate, axis=1)[:, :, None]
    all_placed = lax.optimization_barrier(all_here.astype(BF16))
    cot_rows = cot_all.reshape(n_dp, group, width)
    slot_cot = jnp.stack(
        [
            (lead_dot(all_placed[g], cot_rows[g]) * slot_gate[g]).astype(BF16)
            for g in range(n_dp)
        ]
    )
    down_kept, down_got = hold((down_kept, down_got), normed_ffn)
    weight_back = jnp.concatenate(
        [jnp.where(is_low, down_kept, down_got), jnp.where(is_low, down_got, down_kept)], axis=0
    )
    shared_act_grad = contract(cot_rows, shared_down, 2, 1)

    ffn_chunks = chunk_gather(normed_ffn)
    shared_in_back = weight_shared_in.T
    grad_shared_in = 0.0
    kept_rows, kept_cots, kept_acts, kept_grads = [], [], [], []
    kept_shared, shared_acts, spreads = [], [], []
    for step in range(n_dp):
        ffn_rows = ffn_chunks[step]
        codes = relative(dp_block(slot_code, dp_index ^ step)).reshape(group)
        placed = lax.optimization_barrier((codes[:, None] == slots).astype(BF16))

        shared_in = matmul(ffn_rows, weight_shared_in)
        shared_gate, shared_up = shared_in[:, :units], shared_in[:, units:]
        act_grad = dp_block(shared_act_grad, dp_index ^ step)
        act_grad = relative(act_grad.reshape(n_seq, tokens, units)).reshape(group, units)
        shared_in_grad = jnp.concatenate(
            swiglu_back(shared_gate, shared_up, act_grad), axis=1
        ).astype(BF16)
        kept_shared.append(shared_in_grad)
        shared_acts.append(swiglu(shared_gate, shared_up).astype(BF16))

        kept_rows.append(lead_dot(placed, ffn_rows).astype(BF16))
        spreads.append((placed, shared_in_grad))

    in_moved = hold([in_moved[step] for step in range(n_dp)], kept_rows[0])
    weight_in = in_order(in_moved, n_dp, dp_index).reshape(-1, 2 * ff_part)
    for step in range(n_dp):
        expert_in = matmul(kept_rows[step], weight_in)
        expert_gate, expert_up = expert_in[:, :ff_part], expert_in[:, ff_part:]
        chunk_cot = dp_block(slot_cot, dp_index ^ step)
        expert_in_grad = jnp.concatenate(
            swiglu_back(expert_gate, expert_up, tail_dot(chunk_cot, weight_back)), axis=1
        ).astype(BF16)
        slot_grad = tail_dot(expert_in_grad, weight_in).astype(BF16)
        spreads[step] += (slot_grad,)
        kept_cots.append(chunk_cot)
        kept_acts.append(swiglu(expert_gate, expert_up).astype(BF16))
        kept_grads.append(expert_in_grad)

    planes, sums = [], []
    for step in list(range(1, n_dp)) + [0]:
        placed, shared_in_grad, slot_grad = spreads[step]
        for age in range(1, min(len(planes), 3) + 1):
            placed = hold(placed, planes[-age][age - 1])
        dn_part = matmul(
            jnp.concatenate([placed, shared_in_grad], axis=1),
            jnp.concatenate([slot_grad, shared_in_back], axis=0),
        ).astype(BF16)
        planes.append(seq_scatter(dn_part, n_seq))
        if step:
            sums.append(dp_swap(planes[-1][-1].astype(BF16), n_dp, step).astype(F32))
        else:
            sums.append(planes[-1][-1])
    ffn_grad = sum(sums[1:], sums[0])

    kept_rows, kept_cots, kept_acts, kept_grads, shared_acts, ffn_chunks = hold(
        (kept_rows, kept_cots, kept_acts, kept_grads, shared_acts, ffn_chunks), dn_part
    )
    grad_in = lead_dot(jnp.concatenate(kept_rows), jnp.concatenate(kept_grads)).astype(BF16)
    back_parts = grad_in.reshape(n_dp, expert_rows, 2 * ff_part)
    back_even = dp_exchange(back_parts, n_dp, dp_index, even_steps, ffn_grad)
    expert_act = in_order(kept_acts, n_dp, dp_index)
    grad_back = lead_dot(jnp.concatenate(kept_acts), jnp.concatenate(kept_cots))
    half = expert_down.shape[0]
    low_half, high_half = grad_back[:half], grad_back[half:]
    grad_kept = jnp.where(is_low, low_half, high_half)
    grad_sent = jnp.where(is_low, high_half, low_half).astype(BF16)
    grad_got = dp_swap(hold(grad_sent, ffn_grad), n_dp, 1)
    shared_act = in_order(
        [absolute(act.reshape(n_seq, tokens, units)) for act in shared_acts], n_dp, dp_index
    ).reshape(n_dp, group, units)
    expert_out = (contract(expert_act, weight_back, 2, 0) * slot_gate).astype(BF16)
    out_part = jnp.einsum(
        "gtk,gkd->gtd",
        jnp.concatenate([all_placed, shared_act], axis=2),
        jnp.concatenate(
            [expert_out, jnp.broadcast_to(shared_down, (n_dp, units, width))], axis=1
        ),
        preferred_element_type=F32,
    ).astype(BF16)
    out_sum = lax.psum_scatter(
        hold(out_part.reshape(n_all * tokens, width), ffn_grad),
        BOTH,
        scatter_dimension=0,
        tiled=True,
    )
    output = (residual + out_sum.astype(F32)).astype(BF16)
    grad_shared_down = lead_dot(shared_act.reshape(n_all * tokens, units), cot_all)
    for step in range(n_dp):
        grad_shared_in = grad_shared_in + lead_dot(ffn_chunks[step], kept_shared[step])

    from_norm, gain_ffn_grad = rms_back(residual, gain_ffn, ffn_grad)
    residual_grad = cotangent.astype(F32) + from_norm
    residual_low = residual_grad.astype(BF16)
    heads_grad = tail_dot(residual_low, weight_out).astype(BF16)
    heads_grad = heads_grad.reshape(tokens, n_seq, heads * VD)
    heads_grad = lax.all_to_all(heads_grad, "seq", split_axis=1, concat_axis=0, tiled=True)
    residual_group = seq_gather(hold(residual_low, heads_grad), n_seq)
    grad_shared_in = hold(grad_shared_in.astype(BF16), heads_grad)
    shared_back = lax.all_to_all(
        grad_shared_in.reshape(n_all, -1, 2 * units), BOTH, split_axis=0, concat_axis=0, tiled=True
    )
    heads_grad = relative(heads_grad.reshape(n_seq, tokens, heads * VD))
    grad_out_heads = lead_dot(attended, residual_group)
    out_shard = dp_scatter(grad_out_heads, n_dp, dp_index)
    home = [
        (d * n_seq + s, s * n_dp + d) for d in range(n_dp) for s in range(n_seq)
    ]
    grad_out_weight = lax.ppermute(out_shard, BOTH, home)

    grad_o = to_sequence(heads_grad.reshape(group, heads, VD))
    prob_grad = jnp.einsum("bqhd,bkhd->bhqk", grad_o, values, preferred_element_type=F32)
    centre = jnp.sum(probs * prob_grad, axis=-1, keepdims=True)
    score_grad = (probs * (prob_grad - centre)).astype(BF16)
    query_grad = jnp.einsum("bhqk,bkhd->bqhd", score_grad, keys, preferred_element_type=F32)
    key_grad = jnp.einsum("bhqk,bqhd->bkhd", score_grad, queries, preferred_element_type=F32)
    value_grad = jnp.einsum("bhqk,bqhd->bkhd", shares, grad_o, preferred_element_type=F32)
    query_grad = to_rows((query_grad * score_scale).astype(BF16)).astype(F32)
    key_grad = to_rows((key_grad * score_scale).astype(BF16)).astype(F32)
    value_grad = to_rows(value_grad.astype(BF16))
    query_low = jnp.concatenate(
        [
            query_grad[..., :NOPE],
            rotate_back(query_grad[..., NOPE:], cosine[:, None], sine[:, None]),
        ],
        axis=-1,
    ).astype(BF16).reshape(group, q_width)
    rope_grad = rotate_back(jnp.sum(key_grad[..., NOPE:], axis=1), cosine, sine)
    expand_low = jnp.concatenate(
        [key_grad[..., :NOPE].astype(BF16), value_grad], axis=-1
    ).reshape(group, e_width)

    expand_low = hold(expand_low, grad_got, back_even)
    latent_part = tail_dot(expand_low, weight_up)
    latent_sum = seq_scatter(jnp.concatenate([latent_part, rope_grad], axis=1), n_seq)[-1]
    normed_sum = seq_scatter(tail_dot(query_low, weight_q), n_seq)[-1]
    grad_q = lead_dot(normed_group, query_low)
    grad_up = lead_dot(latent, expand_low).reshape(width, -1)
    grad_joined = dp_scatter(jnp.concatenate([grad_q, grad_up], axis=1), n_dp, dp_index)
    back_odd = dp_exchange(back_parts, n_dp, dp_index, odd_steps, grad_joined)
    grad_joined = grad_joined.reshape(n_seq, down_rows, joined_width)
    grad_joined = lax.all_to_all(grad_joined, "seq", split_axis=0, concat_axis=0, tiled=True)
    grad_q = jnp.swapaxes(grad_joined[..., :q_width], 0, 1).reshape(q_weight.shape)
    grad_up = grad_joined[..., q_width:].reshape(n_seq, kv_up.shape[0], e_width)
    grad_up = jnp.swapaxes(grad_up, 0, 1).reshape(kv_up.shape)

    latent_grad, gain_kv_grad = rms_back(latent_raw[:tokens], gain_kv, latent_sum[:, :KV_RANK])
    down_low = jnp.concatenate([latent_grad, latent_sum[:, KV_RANK:]], axis=1).astype(BF16)
    down_group = seq_gather(down_low, n_seq)
    normed_cols = normed_group.reshape(group, n_dp, n_seq, down_rows)
    normed_cols = lax.dynamic_index_in_dim(normed_cols, seq_index, 2, keepdims=False)
    grad_down = lead_dot(normed_cols.reshape(group, n_dp * down_rows), down_group)
    grad_down = dp_scatter(grad_down, n_dp, dp_index)

    in_back = back_even | back_odd
    in_back[0] = dp_block(back_parts, dp_index)
    in_back, grad_got, shared_back = hold((in_back, grad_got, shared_back), down_low)
    in_back = [in_back[step] for step in range(n_dp)]
    grad_expert_in = assemble(in_back, dp_index, expert_gate_up.shape)
    grad_got = grad_got.astype(F32)
    grad_expert_down = jnp.stack(
        [jnp.where(is_low, grad_kept, grad_got), jnp.where(is_low, grad_got, grad_kept)], axis=1
    )
    shared_back = shared_back.reshape(n_all, -1, 2, units).astype(F32)
    grad_shared_gate_up = jnp.transpose(shared_back, (1, 2, 0, 3)).reshape(shared_gate_up.shape)

    normed_grad = normed_sum + tail_dot(down_low, weight_down)
    rows_from_norm, gain_attn_grad = rms_back(rows, gain_attn, normed_grad)
    input_grad = residual_grad + rows_from_norm

    gain_grads = jnp.concatenate(
        [
            gain_attn_grad.reshape(n_all, -1),
            gain_ffn_grad.reshape(n_all, -1),
            gain_kv_grad.reshape(n_all, -1),
        ],
        axis=1,
    )
    gain_grads = lax.all_to_all(gain_grads, BOTH, split_axis=0, concat_axis=0, tiled=True)
    gain_grads = jnp.sum(gain_grads, axis=0)
    attn_end = attn_gain.shape[0]
    ffn_end = attn_end + ffn_gain.shape[0]

    return (
        output,
        input_grad,
        gain_grads[:attn_end],
        grad_q,
        grad_down,
        gain_grads[ffn_end:],
        grad_up,
        grad_out_weight,
        gain_grads[attn_end:ffn_end],
        grad_shared_gate_up,
        grad_shared_down,
        grad_expert_in,
        grad_expert_down,
    )


def solution(mesh):
    rows = P(BOTH, None)
    return jax.shard_map(
        body,
        mesh=mesh,
        in_specs=(
            rows,
            rows,
            P(BOTH),
            rows,
            rows,
            P(BOTH),
            rows,
            rows,
            P(BOTH),
            rows,
            rows,
            P("dp", "seq", None),
            P("dp", "seq", None),
            P("dp", None),
            rows,
            P("dp", None),
        ),
        out_specs=(
            rows,
            rows,
            P(BOTH),
            rows,
            rows,
            P(BOTH),
            rows,
            rows,
            P(BOTH),
            rows,
            rows,
            P("dp", "seq", None),
            P("dp", "seq", None),
        ),
        check_vma=False,
    )
```

```python
import jax
import jax.numpy as jnp
import numpy as np
from jax import lax
from jax.experimental import pallas as pl
from jax.experimental.pallas import tpu as pltpu
from jax.sharding import PartitionSpec as P

H = 16
NOPE = 128
ROPE = 64
VD = 128
KV_RANK = 512
TOP = 6

EPS = 1e-06
THETA = 10000.0
GATE_UNIT = 16384.0

BOTH = ("dp", "seq")
F32 = jnp.float32
BF16 = jnp.bfloat16


def contract(left_side, right_side, left_dim, right_dim):
    return lax.dot_general(
        left_side,
        right_side,
        (((left_dim,), (right_dim,)), ((), ())),
        preferred_element_type=F32,
    )


def matmul(left_side, right_side):
    return contract(left_side, right_side, left_side.ndim - 1, 0)


def lead_dot(left_side, right_side):
    return contract(left_side, right_side, 0, 0)


def tail_dot(left_side, right_side):
    return contract(left_side, right_side, 1, 1)


def rms_scale(values):
    return lax.rsqrt(jnp.mean(values * values, axis=-1, keepdims=True) + EPS)


def rms_back(values, gain, grad):
    scale = rms_scale(values)
    unit = values * scale
    weighted = grad * gain
    centre = jnp.mean(weighted * unit, axis=-1, keepdims=True)
    return scale * (weighted - unit * centre), jnp.sum(grad * unit, axis=0)


def swiglu(gate, up):
    return jax.nn.silu(gate) * up


def swiglu_back(gate, up, grad):
    sig = jax.nn.sigmoid(gate)
    return grad * up * sig * (1.0 + gate * (1.0 - sig)), grad * (gate * sig)


def rotary_tables(positions):
    half_width = ROPE // 2
    frequency = THETA ** (-jnp.arange(half_width, dtype=F32) * 2.0 / ROPE)
    angles = positions.astype(F32)[:, None] * frequency[None, :]
    return jnp.cos(angles), jnp.sin(angles)


def rotate(values, cosine, sine):
    half_width = values.shape[-1] // 2
    lead = values[..., :half_width]
    trail = values[..., half_width:]
    return jnp.concatenate([lead * cosine - trail * sine, trail * cosine + lead * sine], axis=-1)


def rotate_back(grads, cosine, sine):
    return rotate(grads, cosine, -sine)


def link_orders(n_seq):
    bits = [1 << j for j in range(1, n_seq.bit_length() - 1)]
    return bits, bits[::-1]


def block_table(n_seq):
    orders = link_orders(n_seq)
    steps = len(orders[0])
    table = np.zeros((n_seq, n_seq), np.int32)
    for s in range(n_seq):
        for m in range(n_seq):
            core = (s & 1) ^ (m >> steps)
            other = (s & ~1) | core
            for j in range(steps):
                if m >> j & 1:
                    other ^= orders[core][j]
            table[s, m] = other
    return table


def seq_step(values, n_seq, step):
    orders = link_orders(n_seq)
    return lax.ppermute(values, "seq", [(s, s ^ orders[s & 1][step]) for s in range(n_seq)])


def core_swap(values, n_seq):
    return lax.ppermute(values, "seq", [(s, s ^ 1) for s in range(n_seq)])


def seq_gather(values, n_seq):
    current = values
    for step in range(len(link_orders(n_seq)[0])):
        current = jnp.concatenate([current, seq_step(current, n_seq, step)], axis=0)
    return jnp.concatenate([current, core_swap(current, n_seq)], axis=0)


def seq_scatter(make_half, n_seq):
    sent = core_swap(make_half(1).astype(BF16), n_seq)
    kept = make_half(0)
    stages = []
    for step in reversed(range(len(link_orders(n_seq)[0]))):
        half = sent.shape[0] // 2
        onward = (kept[half:].astype(F32) + sent[half:].astype(F32)).astype(BF16)
        kept = kept[:half].astype(F32) + sent[:half].astype(F32)
        stages.append(kept)
        sent = seq_step(onward, n_seq, step)
    stages.append(kept + sent.astype(F32))
    return stages


def half_of(values, part):
    half = values.shape[0] // 2
    return values[part * half : (part + 1) * half]


def hold(value, *until):
    return lax.optimization_barrier((value,) + until)[0]


def dp_swap(values, n_dp, step):
    return lax.ppermute(values, "dp", [(d, d ^ step) for d in range(n_dp)])


def dp_block(blocks, index):
    return lax.dynamic_index_in_dim(blocks, index, 0, keepdims=False)


def dp_exchange(blocks, n_dp, dp_index, steps, until):
    blocks = hold(blocks, until)
    return {
        step: dp_swap(dp_block(blocks, dp_index ^ step), n_dp, step) for step in steps
    }


def in_order(moved, n_dp, dp_index):
    result = jnp.zeros((n_dp,) + moved[0].shape, moved[0].dtype)
    for step in range(n_dp):
        result = lax.dynamic_update_index_in_dim(result, moved[step], dp_index ^ step, 0)
    return result


def dp_scatter(values, n_dp, dp_index):
    blocks = values.reshape((n_dp, -1) + values.shape[1:])
    low = blocks.astype(BF16)
    total = dp_block(blocks, dp_index).astype(F32)
    for step in range(1, n_dp):
        total = total + dp_swap(dp_block(low, dp_index ^ step), n_dp, step).astype(F32)
    return total


def assemble_kernel(index_ref, *refs):
    pieces, out_ref = refs[:-1], refs[-1]
    count = len(pieces)
    per_device = out_ref.shape[1]
    part = pieces[0].shape[1] // 2
    values = [piece[...].astype(F32) for piece in pieces]
    for expert in range(per_device):
        gates, ups = [], []
        for ff in range(count // per_device):
            step = index_ref[0] ^ (ff * per_device + expert)
            chosen = values[0]
            for j in range(1, count):
                chosen = jnp.where(step == j, values[j], chosen)
            gates.append(chosen[:, :part])
            ups.append(chosen[:, part:])
        out_ref[:, expert, :] = jnp.concatenate(gates + ups, axis=1)


def assemble(pieces, dp_index, out_shape):
    rows, piece_width = pieces[0].shape
    step_rows = 64
    return pl.pallas_call(
        assemble_kernel,
        out_shape=jax.ShapeDtypeStruct(out_shape, F32),
        grid_spec=pltpu.PrefetchScalarGridSpec(
            num_scalar_prefetch=1,
            grid=(rows // step_rows,),
            in_specs=[pl.BlockSpec((step_rows, piece_width), lambda i, index: (i, 0))] * len(pieces),
            out_specs=pl.BlockSpec((step_rows,) + out_shape[1:], lambda i, index: (i, 0, 0)),
        ),
        compiler_params=pltpu.CompilerParams(vmem_limit_bytes=48 * 2**20),
        name="assemble",
    )(jnp.reshape(dp_index, (1,)).astype(jnp.int32), *pieces)


def body(
    hidden,
    cotangent,
    attn_gain,
    q_weight,
    kv_down,
    kv_gain,
    kv_up,
    out_weight,
    ffn_gain,
    shared_gate_up,
    shared_down,
    expert_gate_up,
    expert_down,
    expert_ids,
    gate_fix,
    block_ids,
):
    n_dp = lax.axis_size("dp")
    n_seq = lax.axis_size("seq")
    n_all = n_dp * n_seq
    dp_index = lax.axis_index("dp")
    seq_index = lax.axis_index("seq")
    tokens, width = hidden.shape
    sequences, length = block_ids.shape
    part = length // n_seq
    group = n_seq * tokens
    heads = H // n_seq
    per_device = expert_gate_up.shape[1]
    experts = per_device * n_seq
    capacity = TOP * tokens // per_device
    ff_parts = n_dp // per_device
    expert_bit = dp_index % per_device
    down_rows = kv_down.shape[0]
    down_width = kv_down.shape[1]
    q_width = heads * (NOPE + ROPE)
    e_width = heads * (NOPE + VD)
    block_at = dp_block(jnp.asarray(block_table(n_seq)), seq_index)
    block_of = dp_block(jnp.asarray(np.argsort(block_table(n_seq), axis=1)), seq_index)

    def relative(values):
        return jnp.take(values, block_at, axis=0, mode="clip")

    def absolute(values):
        return jnp.take(values, block_of, axis=0, mode="clip")

    ff_width = expert_gate_up.shape[2] // 2
    ff_part = ff_width // ff_parts
    expert_rows = expert_gate_up.shape[0]
    in_parts = expert_gate_up.reshape(expert_rows, per_device, 2, ff_parts, ff_part)
    in_parts = jnp.transpose(in_parts, (3, 1, 0, 2, 4)).reshape(n_dp, expert_rows, 2 * ff_part)
    down_kept = lax.dynamic_index_in_dim(expert_down, expert_bit, 1, keepdims=False)
    down_sent = lax.dynamic_index_in_dim(expert_down, 1 - expert_bit, 1, keepdims=False)
    is_low = expert_bit == 0

    units = shared_down.shape[0]
    shared_cols = shared_gate_up.reshape(down_rows, 2, n_dp, n_seq, units)
    shared_cols = jnp.transpose(shared_cols, (0, 3, 2, 1, 4)).reshape(down_rows, n_seq, -1)

    up_rows = kv_up.reshape(kv_up.shape[0], n_seq, -1, kv_up.shape[0] * e_width // down_rows)
    up_rows = jnp.swapaxes(up_rows, 1, 2).reshape(down_rows, n_seq, -1)
    joined_width = q_width + up_rows.shape[2]
    joined = jnp.concatenate(
        [q_weight.reshape(down_rows, n_seq, q_width), up_rows, shared_cols], axis=2
    )
    joined = lax.all_to_all(joined, "seq", split_axis=1, concat_axis=0, tiled=True)
    joined = joined.reshape(n_seq * down_rows, -1)
    shared_parts = joined[:, joined_width:].reshape(-1, n_dp, 2 * units)
    shared_parts = jnp.swapaxes(shared_parts, 0, 1)
    joined = joined[:, :joined_width]
    joined = [joined] + [dp_swap(joined, n_dp, step) for step in range(1, n_dp)]
    joined = hold(joined, in_parts, down_kept, down_sent)
    joined = in_order(joined, n_dp, dp_index).reshape(-1, joined_width)
    weight_q = joined[:, :q_width]
    weight_up = joined[:, q_width:].reshape(KV_RANK, e_width)

    hidden_group = seq_gather(hidden, n_seq)
    ready = joined
    in_parts = jnp.concatenate([in_parts, shared_parts], axis=2)
    even_steps, odd_steps = range(2, n_dp, 2), range(1, n_dp, 2)
    in_even = dp_exchange(in_parts, n_dp, dp_index, even_steps, ready)
    down_got = dp_swap(hold(down_sent, ready), n_dp, 1)
    in_odd = dp_exchange(in_parts, n_dp, dp_index, odd_steps, in_even)
    in_moved = in_even | in_odd
    in_moved[0] = dp_block(in_parts, dp_index)

    labels = jnp.arange(experts, dtype=jnp.int32)
    hits = jnp.sum((expert_ids[:, :, None] == labels).astype(jnp.int32), axis=1)
    earlier = jnp.arange(group, dtype=jnp.int32)[:, None] < seq_index * tokens
    before_own = jnp.sum(jnp.where(earlier, hits, 0), axis=0)
    own_hits = lax.dynamic_slice_in_dim(hits, seq_index * tokens, tokens, 0)
    own_picks = lax.dynamic_slice_in_dim(expert_ids, seq_index * tokens, tokens, 0)
    own_slot = before_own[None, :] + jnp.cumsum(own_hits, axis=0) - own_hits
    code = jnp.where((own_hits > 0) & (own_slot < capacity), own_slot + 1, 0)
    gates = jnp.sum(
        gate_fix[:, :, None] * (own_picks[:, :, None] == labels).astype(jnp.int32), axis=1
    )
    pieces = jnp.stack([code // 16, code % 16, gates // 128, gates % 128], axis=0)
    pieces = jnp.transpose(pieces, (2, 0, 1)).reshape(experts, 4 * tokens).astype(BF16)

    def wide_row(vector):
        return jnp.pad(vector, (0, down_width - 4 * tokens - vector.shape[0]))[None]

    extras = jnp.concatenate([wide_row(attn_gain), wide_row(ffn_gain), wide_row(kv_gain)], axis=0)
    extras = jnp.pad(extras, ((0, experts - 3), (0, 0)))
    message = jnp.concatenate(
        [kv_down, jnp.concatenate([pieces, extras], axis=1)], axis=0
    )
    spread = lax.all_gather(message, BOTH, axis=0, tiled=False)
    weight_down = spread[:, :down_rows].reshape(-1, down_width)
    spread_tail = spread[:, down_rows:]
    first = 4 * tokens
    gain_attn = spread_tail[:, 0, first : first + attn_gain.shape[0]].reshape(-1).astype(F32)
    gain_ffn = spread_tail[:, 1, first : first + ffn_gain.shape[0]].reshape(-1).astype(F32)
    gain_kv = spread_tail[:, 2, first : first + kv_gain.shape[0]].reshape(-1).astype(F32)
    own_expert = per_device * seq_index + expert_bit
    routing = lax.dynamic_index_in_dim(spread_tail, own_expert, axis=1, keepdims=False)
    routing = routing[:, :first].reshape(n_dp, n_seq, 4, tokens).astype(jnp.int32)
    slot_code = routing[:, :, 0] * 16 + routing[:, :, 1]
    gate_of = (routing[:, :, 2] * 128 + routing[:, :, 3]).astype(F32) / GATE_UNIT

    weight_out = lax.all_gather(hold(out_weight, joined, hidden_group), BOTH, axis=0, tiled=True)
    cot_all = lax.all_gather(hold(cotangent, joined, hidden_group, spread), BOTH, axis=0, tiled=True)

    def chunk_gather(values):
        far = hold(values, in_odd)
        sent = [values] + [dp_swap(far, n_dp, step) for step in range(1, n_dp)]
        return [seq_gather(piece, n_seq) for piece in sent]

    rows_group = hidden_group.astype(F32)
    normed_group = (rows_group * rms_scale(rows_group) * gain_attn).astype(BF16)
    in_part = jnp.arange(tokens, dtype=jnp.int32) % part
    positions = (block_at[:, None] * part + in_part[None, :]).reshape(group)
    cosine, sine = rotary_tables(positions)

    def to_sequence(values):
        split = values.reshape((n_seq, sequences, part) + values.shape[1:])
        return jnp.swapaxes(split, 0, 1).reshape((sequences, length) + values.shape[1:])

    def to_rows(values):
        split = values.reshape((sequences, n_seq, part) + values.shape[2:])
        return jnp.swapaxes(split, 0, 1).reshape((group,) + values.shape[2:])

    query_raw = matmul(normed_group, weight_q).reshape(group, heads, NOPE + ROPE)
    latent_in = matmul(normed_group, weight_down)
    latent_raw = latent_in[:, :KV_RANK]
    latent = (latent_raw * rms_scale(latent_raw) * gain_kv).astype(BF16)
    expanded = matmul(latent, weight_up).reshape(group, heads, NOPE + VD)
    rope_query = rotate(query_raw[..., NOPE:], cosine[:, None], sine[:, None])
    rope_key = rotate(latent_in[:, KV_RANK:], cosine, sine)
    rope_key = jnp.broadcast_to(rope_key[:, None], (group, heads, ROPE))
    queries = to_sequence(
        jnp.concatenate([query_raw[..., :NOPE], rope_query], axis=-1).astype(BF16)
    )
    keys = to_sequence(
        jnp.concatenate([expanded[..., :NOPE], rope_key], axis=-1).astype(BF16)
    )
    values = to_sequence(expanded[..., NOPE:].astype(BF16))
    blocks = jnp.take(block_ids.reshape(sequences, n_seq, part), block_at, axis=1, mode="clip")
    blocks = blocks.reshape(sequences, length)
    score_scale = (NOPE + ROPE) ** (-0.5)
    scores = jnp.einsum("bqhd,bkhd->bhqk", queries, keys, preferred_element_type=F32) * score_scale
    allowed = blocks[:, None, None, :] <= blocks[:, None, :, None]
    scores = jnp.where(allowed, scores, -1e30)
    weights = jnp.exp(scores - jnp.max(scores, axis=-1, keepdims=True))
    probs = weights / jnp.sum(weights, axis=-1, keepdims=True)
    shares = probs.astype(BF16)
    attended = jnp.einsum("bhqk,bkhd->bqhd", shares, values, preferred_element_type=F32)
    attended = to_rows(attended.astype(BF16)).reshape(group, heads * VD)
    attended = hold(attended, in_even, down_got)
    heads_out = absolute(attended.reshape(n_seq, tokens, heads * VD))
    heads_out = lax.all_to_all(heads_out, "seq", split_axis=0, concat_axis=2, tiled=True)
    heads_out = heads_out.reshape(tokens, H * VD)

    rows = hidden.astype(F32)
    residual = rows + matmul(heads_out, weight_out)
    normed_ffn = (residual * rms_scale(residual) * gain_ffn).astype(BF16)

    slots = jnp.arange(1, capacity + 1, dtype=jnp.int32)
    all_codes = slot_code.reshape(n_dp, group)
    all_here = all_codes[:, :, None] == slots
    slot_gate = jnp.where(all_here, gate_of.reshape(n_dp, group)[:, :, None], 0.0)
    slot_gate = jnp.sum(slot_gate, axis=1)[:, :, None]
    all_placed = lax.optimization_barrier(all_here.astype(BF16))
    cot_rows = cot_all.reshape(n_dp, group, width)
    slot_cot = jnp.stack(
        [
            (lead_dot(all_placed[g], cot_rows[g]) * slot_gate[g]).astype(BF16)
            for g in range(n_dp)
        ]
    )
    down_kept, down_got = hold((down_kept, down_got), normed_ffn)
    weight_back = jnp.concatenate(
        [jnp.where(is_low, down_kept, down_got), jnp.where(is_low, down_got, down_kept)], axis=0
    )
    shared_act_grad = contract(cot_rows, shared_down, 2, 1)

    ffn_chunks = chunk_gather(normed_ffn)
    chunk_places, kept_rows = [], []
    for step in range(n_dp):
        codes = relative(dp_block(slot_code, dp_index ^ step)).reshape(group)
        placed = lax.optimization_barrier((codes[:, None] == slots).astype(BF16))
        if step == 1:
            placed = hold(placed, slot_cot, shared_act_grad)
        chunk_places.append(placed)
        kept_rows.append(lead_dot(placed, ffn_chunks[step]).astype(BF16))

    in_moved = hold([in_moved[step] for step in range(n_dp)], kept_rows[0])
    weight_in = in_order([piece[:, : 2 * ff_part] for piece in in_moved], n_dp, dp_index)
    weight_in = weight_in.reshape(-1, 2 * ff_part)
    weight_shared_in = in_order([piece[:, 2 * ff_part :] for piece in in_moved], n_dp, dp_index)
    weight_shared_in = weight_shared_in.reshape(-1, 2 * units)
    shared_in_back = weight_shared_in.T
    grad_shared_in = 0.0
    kept_cots, kept_acts, kept_grads = [], [], []
    kept_shared, shared_acts, spreads = [], [], []
    for step in range(n_dp):
        ffn_rows = ffn_chunks[step]
        shared_in = matmul(ffn_rows, weight_shared_in)
        shared_gate, shared_up = shared_in[:, :units], shared_in[:, units:]
        act_grad = dp_block(shared_act_grad, dp_index ^ step)
        act_grad = relative(act_grad.reshape(n_seq, tokens, units)).reshape(group, units)
        shared_in_grad = jnp.concatenate(
            swiglu_back(shared_gate, shared_up, act_grad), axis=1
        ).astype(BF16)
        kept_shared.append(shared_in_grad)
        shared_acts.append(swiglu(shared_gate, shared_up).astype(BF16))

        spreads.append((chunk_places[step], shared_in_grad))

    for step in range(n_dp):
        expert_in = matmul(kept_rows[step], weight_in)
        expert_gate, expert_up = expert_in[:, :ff_part], expert_in[:, ff_part:]
        chunk_cot = dp_block(slot_cot, dp_index ^ step)
        expert_in_grad = jnp.concatenate(
            swiglu_back(expert_gate, expert_up, tail_dot(chunk_cot, weight_back)), axis=1
        ).astype(BF16)
        slot_grad = tail_dot(expert_in_grad, weight_in).astype(BF16)
        spreads[step] += (slot_grad,)
        kept_cots.append(chunk_cot)
        kept_acts.append(swiglu(expert_gate, expert_up).astype(BF16))
        kept_grads.append(expert_in_grad)

    planes, sums = [], []
    for step in list(range(1, n_dp)) + [0]:
        placed, shared_in_grad, slot_grad = spreads[step]
        for age in range(1, min(len(planes), 3) + 1):
            placed = hold(placed, planes[-age][age - 1])
        left_side = jnp.concatenate([placed, shared_in_grad], axis=1)
        right_side = jnp.concatenate([slot_grad, shared_in_back], axis=0)
        planes.append(seq_scatter(lambda part: matmul(half_of(left_side, part), right_side), n_seq))
        if step:
            sums.append(dp_swap(planes[-1][-1].astype(BF16), n_dp, step).astype(F32))
        else:
            sums.append(planes[-1][-1])
    ffn_grad = sum(sums[1:], sums[0])

    from_norm, gain_ffn_grad = rms_back(residual, gain_ffn, ffn_grad)
    residual_grad = cotangent.astype(F32) + from_norm
    residual_low = residual_grad.astype(BF16)
    heads_grad = tail_dot(residual_low, weight_out).astype(BF16)
    heads_grad_own = heads_grad
    heads_grad = heads_grad.reshape(tokens, n_seq, heads * VD)
    heads_grad = lax.all_to_all(heads_grad, "seq", split_axis=1, concat_axis=0, tiled=True)

    out_acts, shared_acts = hold((kept_acts, shared_acts), planes[-1][0])
    kept_rows, kept_cots, kept_acts, kept_grads, ffn_chunks = hold(
        (kept_rows, kept_cots, kept_acts, kept_grads, ffn_chunks), heads_grad_own
    )
    grad_in = lead_dot(jnp.concatenate(kept_rows), jnp.concatenate(kept_grads)).astype(BF16)
    back_parts = grad_in.reshape(n_dp, expert_rows, 2 * ff_part)
    back_even = dp_exchange(back_parts, n_dp, dp_index, even_steps, ffn_grad)
    expert_act = in_order(out_acts, n_dp, dp_index)
    grad_back = lead_dot(jnp.concatenate(kept_acts), jnp.concatenate(kept_cots))
    half = expert_down.shape[0]
    low_half, high_half = grad_back[:half], grad_back[half:]
    grad_kept = jnp.where(is_low, low_half, high_half)
    grad_sent = jnp.where(is_low, high_half, low_half).astype(BF16)
    grad_got = dp_swap(hold(grad_sent, ffn_grad), n_dp, 1)
    shared_act = in_order(
        [absolute(act.reshape(n_seq, tokens, units)) for act in shared_acts], n_dp, dp_index
    ).reshape(n_dp, group, units)
    expert_out = (contract(expert_act, weight_back, 2, 0) * slot_gate).astype(BF16)
    out_part = jnp.einsum(
        "gtk,gkd->gtd",
        jnp.concatenate([all_placed, shared_act], axis=2),
        jnp.concatenate(
            [expert_out, jnp.broadcast_to(shared_down, (n_dp, units, width))], axis=1
        ),
        preferred_element_type=F32,
    ).astype(BF16)
    out_sum = lax.psum_scatter(
        hold(out_part.reshape(n_all * tokens, width), ffn_grad),
        BOTH,
        scatter_dimension=0,
        tiled=True,
    )
    output = (residual + out_sum.astype(F32)).astype(BF16)
    shared_late = hold(shared_act, heads_grad_own).reshape(n_all * tokens, units)
    grad_shared_down = lead_dot(shared_late, cot_all)
    for step in range(n_dp):
        grad_shared_in = grad_shared_in + lead_dot(ffn_chunks[step], kept_shared[step])

    residual_group = seq_gather(hold(residual_low, heads_grad), n_seq)
    grad_shared_in = hold(grad_shared_in.astype(BF16), heads_grad)
    shared_back = lax.all_to_all(
        grad_shared_in.reshape(n_all, -1, 2 * units), BOTH, split_axis=0, concat_axis=0, tiled=True
    )
    heads_grad = relative(heads_grad.reshape(n_seq, tokens, heads * VD))
    grad_out_heads = lead_dot(attended, residual_group)
    out_shard = dp_scatter(grad_out_heads, n_dp, dp_index)
    home = [
        (d * n_seq + s, s * n_dp + d) for d in range(n_dp) for s in range(n_seq)
    ]
    grad_out_weight = lax.ppermute(out_shard, BOTH, home)

    grad_o = to_sequence(heads_grad.reshape(group, heads, VD))
    prob_grad = jnp.einsum("bqhd,bkhd->bhqk", grad_o, values, preferred_element_type=F32)
    centre = jnp.sum(probs * prob_grad, axis=-1, keepdims=True)
    score_grad = (probs * (prob_grad - centre)).astype(BF16)
    query_grad = jnp.einsum("bhqk,bkhd->bqhd", score_grad, keys, preferred_element_type=F32)
    key_grad = jnp.einsum("bhqk,bqhd->bkhd", score_grad, queries, preferred_element_type=F32)
    value_grad = jnp.einsum("bhqk,bqhd->bkhd", shares, grad_o, preferred_element_type=F32)
    query_grad = to_rows((query_grad * score_scale).astype(BF16)).astype(F32)
    key_grad = to_rows((key_grad * score_scale).astype(BF16)).astype(F32)
    value_grad = to_rows(value_grad.astype(BF16))
    query_low = jnp.concatenate(
        [
            query_grad[..., :NOPE],
            rotate_back(query_grad[..., NOPE:], cosine[:, None], sine[:, None]),
        ],
        axis=-1,
    ).astype(BF16).reshape(group, q_width)
    rope_grad = rotate_back(jnp.sum(key_grad[..., NOPE:], axis=1), cosine, sine)
    expand_low = jnp.concatenate(
        [key_grad[..., :NOPE].astype(BF16), value_grad], axis=-1
    ).reshape(group, e_width)

    expand_low, rope_grad = hold((expand_low, rope_grad), shared_back)
    latent_sum = seq_scatter(
        lambda part: jnp.concatenate(
            [tail_dot(half_of(expand_low, part), weight_up), half_of(rope_grad, part)], axis=1
        ),
        n_seq,
    )[-1]
    normed_low = [tail_dot(half_of(query_low, part), weight_q).astype(BF16) for part in (0, 1)]
    normed_sum = seq_scatter(lambda part: normed_low[part], n_seq)[-1]
    unit_rows = rows_group * rms_scale(rows_group)
    gain_attn_grad = sum(
        jnp.sum(normed_low[part].astype(F32) * half_of(unit_rows, part), axis=0) for part in (0, 1)
    )
    grad_q = lead_dot(normed_group, query_low)
    grad_up = lead_dot(latent, expand_low).reshape(width, -1)
    grad_joined = hold(jnp.concatenate([grad_q, grad_up], axis=1), back_even, grad_got)
    grad_joined = dp_scatter(grad_joined, n_dp, dp_index)
    back_odd = dp_exchange(back_parts, n_dp, dp_index, odd_steps, grad_joined)
    grad_joined = grad_joined.reshape(n_seq, down_rows, joined_width)
    grad_joined = lax.all_to_all(grad_joined, "seq", split_axis=0, concat_axis=0, tiled=True)
    grad_q = jnp.swapaxes(grad_joined[..., :q_width], 0, 1).reshape(q_weight.shape)
    grad_up = grad_joined[..., q_width:].reshape(n_seq, kv_up.shape[0], e_width)
    grad_up = jnp.swapaxes(grad_up, 0, 1).reshape(kv_up.shape)

    latent_grad, gain_kv_grad = rms_back(latent_raw[:tokens], gain_kv, latent_sum[:, :KV_RANK])
    down_low = jnp.concatenate([latent_grad, latent_sum[:, KV_RANK:]], axis=1).astype(BF16)
    down_group = seq_gather(down_low, n_seq)
    normed_cols = normed_group.reshape(group, n_dp, n_seq, down_rows)
    normed_cols = lax.dynamic_index_in_dim(normed_cols, seq_index, 2, keepdims=False)
    grad_down = lead_dot(normed_cols.reshape(group, n_dp * down_rows), down_group)
    grad_down = dp_scatter(grad_down, n_dp, dp_index)

    in_back = back_even | back_odd
    in_back[0] = dp_block(back_parts, dp_index)
    in_back, grad_got, shared_back = hold((in_back, grad_got, shared_back), down_low)
    in_back = [in_back[step] for step in range(n_dp)]
    grad_expert_in = assemble(in_back, dp_index, expert_gate_up.shape)
    grad_got = grad_got.astype(F32)
    grad_expert_down = jnp.stack(
        [jnp.where(is_low, grad_kept, grad_got), jnp.where(is_low, grad_got, grad_kept)], axis=1
    )
    shared_back = shared_back.reshape(n_all, -1, 2, units).astype(F32)
    grad_shared_gate_up = jnp.transpose(shared_back, (1, 2, 0, 3)).reshape(shared_gate_up.shape)

    down_grad = tail_dot(down_low, weight_down)
    rows_from_norm, _ = rms_back(rows, gain_attn, normed_sum + down_grad)
    input_grad = residual_grad + rows_from_norm

    gain_attn_grad = gain_attn_grad + jnp.sum(down_grad * rows * rms_scale(rows), axis=0)
    gain_grads = jnp.concatenate(
        [
            gain_attn_grad.reshape(n_all, -1),
            gain_ffn_grad.reshape(n_all, -1),
            gain_kv_grad.reshape(n_all, -1),
        ],
        axis=1,
    )
    gain_grads = lax.all_to_all(gain_grads, BOTH, split_axis=0, concat_axis=0, tiled=True)
    gain_grads = jnp.sum(gain_grads, axis=0)
    attn_end = attn_gain.shape[0]
    ffn_end = attn_end + ffn_gain.shape[0]

    return (
        output,
        input_grad,
        gain_grads[:attn_end],
        grad_q,
        grad_down,
        gain_grads[ffn_end:],
        grad_up,
        grad_out_weight,
        gain_grads[attn_end:ffn_end],
        grad_shared_gate_up,
        grad_shared_down,
        grad_expert_in,
        grad_expert_down,
    )


def solution(mesh):
    rows = P(BOTH, None)
    return jax.shard_map(
        body,
        mesh=mesh,
        in_specs=(
            rows,
            rows,
            P(BOTH),
            rows,
            rows,
            P(BOTH),
            rows,
            rows,
            P(BOTH),
            rows,
            rows,
            P("dp", "seq", None),
            P("dp", "seq", None),
            P("dp", None),
            rows,
            P("dp", None),
        ),
        out_specs=(
            rows,
            rows,
            P(BOTH),
            rows,
            rows,
            P(BOTH),
            rows,
            rows,
            P(BOTH),
            rows,
            rows,
            P("dp", "seq", None),
            P("dp", "seq", None),
        ),
        check_vma=False,
    )
```

```python
import jax
import jax.numpy as jnp
import numpy as np
from jax import lax
from jax.experimental import pallas as pl
from jax.experimental.pallas import tpu as pltpu
from jax.sharding import PartitionSpec as P

H = 16
NOPE = 128
ROPE = 64
VD = 128
KV_RANK = 512
TOP = 6

EPS = 1e-06
THETA = 10000.0
GATE_UNIT = 16384.0

BOTH = ("dp", "seq")
F32 = jnp.float32
BF16 = jnp.bfloat16


def contract(left_side, right_side, left_dim, right_dim):
    return lax.dot_general(
        left_side,
        right_side,
        (((left_dim,), (right_dim,)), ((), ())),
        preferred_element_type=F32,
    )


def matmul(left_side, right_side):
    return contract(left_side, right_side, left_side.ndim - 1, 0)


def lead_dot(left_side, right_side):
    return contract(left_side, right_side, 0, 0)


def tail_dot(left_side, right_side):
    return contract(left_side, right_side, 1, 1)


def rms_scale(values):
    return lax.rsqrt(jnp.mean(values * values, axis=-1, keepdims=True) + EPS)


def rms_back(values, gain, grad):
    scale = rms_scale(values)
    unit = values * scale
    weighted = grad * gain
    centre = jnp.mean(weighted * unit, axis=-1, keepdims=True)
    return scale * (weighted - unit * centre), jnp.sum(grad * unit, axis=0)


def swiglu(gate, up):
    return jax.nn.silu(gate) * up


def swiglu_back(gate, up, grad):
    sig = jax.nn.sigmoid(gate)
    return grad * up * sig * (1.0 + gate * (1.0 - sig)), grad * (gate * sig)


def rotary_tables(positions):
    half_width = ROPE // 2
    frequency = THETA ** (-jnp.arange(half_width, dtype=F32) * 2.0 / ROPE)
    angles = positions.astype(F32)[:, None] * frequency[None, :]
    return jnp.cos(angles), jnp.sin(angles)


def rotate(values, cosine, sine):
    half_width = values.shape[-1] // 2
    lead = values[..., :half_width]
    trail = values[..., half_width:]
    return jnp.concatenate([lead * cosine - trail * sine, trail * cosine + lead * sine], axis=-1)


def rotate_back(grads, cosine, sine):
    return rotate(grads, cosine, -sine)


def link_orders(n_seq):
    bits = [1 << j for j in range(1, n_seq.bit_length() - 1)]
    return bits, bits[::-1]


def block_table(n_seq):
    orders = link_orders(n_seq)
    steps = len(orders[0])
    table = np.zeros((n_seq, n_seq), np.int32)
    for s in range(n_seq):
        for m in range(n_seq):
            core = (s & 1) ^ (m >> steps)
            other = (s & ~1) | core
            for j in range(steps):
                if m >> j & 1:
                    other ^= orders[core][j]
            table[s, m] = other
    return table


def seq_step(values, n_seq, step):
    orders = link_orders(n_seq)
    return lax.ppermute(values, "seq", [(s, s ^ orders[s & 1][step]) for s in range(n_seq)])


def core_swap(values, n_seq):
    return lax.ppermute(values, "seq", [(s, s ^ 1) for s in range(n_seq)])


def seq_gather(values, n_seq):
    current = values
    for step in range(len(link_orders(n_seq)[0])):
        current = jnp.concatenate([current, seq_step(current, n_seq, step)], axis=0)
    return jnp.concatenate([current, core_swap(current, n_seq)], axis=0)


def seq_scatter(make_half, n_seq):
    sent = core_swap(make_half(1).astype(BF16), n_seq)
    kept = make_half(0)
    stages = []
    for step in reversed(range(len(link_orders(n_seq)[0]))):
        half = sent.shape[0] // 2
        onward = (kept[half:].astype(F32) + sent[half:].astype(F32)).astype(BF16)
        kept = kept[:half].astype(F32) + sent[:half].astype(F32)
        stages.append(kept)
        sent = seq_step(onward, n_seq, step)
    stages.append(kept + sent.astype(F32))
    return stages


def half_of(values, part):
    half = values.shape[0] // 2
    return values[part * half : (part + 1) * half]


def hold(value, *until):
    return lax.optimization_barrier((value,) + until)[0]


def dp_swap(values, n_dp, step):
    return lax.ppermute(values, "dp", [(d, d ^ step) for d in range(n_dp)])


def dp_block(blocks, index):
    return lax.dynamic_index_in_dim(blocks, index, 0, keepdims=False)


def dp_exchange(blocks, n_dp, dp_index, steps, until):
    blocks = hold(blocks, until)
    return {
        step: dp_swap(dp_block(blocks, dp_index ^ step), n_dp, step) for step in steps
    }


def in_order(moved, n_dp, dp_index):
    result = jnp.zeros((n_dp,) + moved[0].shape, moved[0].dtype)
    for step in range(n_dp):
        result = lax.dynamic_update_index_in_dim(result, moved[step], dp_index ^ step, 0)
    return result


def dp_scatter(values, n_dp, dp_index):
    blocks = values.reshape((n_dp, -1) + values.shape[1:])
    low = blocks.astype(BF16)
    total = dp_block(blocks, dp_index).astype(F32)
    for step in range(1, n_dp):
        total = total + dp_swap(dp_block(low, dp_index ^ step), n_dp, step).astype(F32)
    return total


def assemble_kernel(index_ref, *refs):
    pieces, out_ref = refs[:-1], refs[-1]
    count = len(pieces)
    per_device = out_ref.shape[1]
    part = pieces[0].shape[1] // 2
    values = [piece[...].astype(F32) for piece in pieces]
    for expert in range(per_device):
        gates, ups = [], []
        for ff in range(count // per_device):
            step = index_ref[0] ^ (ff * per_device + expert)
            chosen = values[0]
            for j in range(1, count):
                chosen = jnp.where(step == j, values[j], chosen)
            gates.append(chosen[:, :part])
            ups.append(chosen[:, part:])
        out_ref[:, expert, :] = jnp.concatenate(gates + ups, axis=1)


def assemble(pieces, dp_index, out_shape):
    rows, piece_width = pieces[0].shape
    step_rows = 64
    return pl.pallas_call(
        assemble_kernel,
        out_shape=jax.ShapeDtypeStruct(out_shape, F32),
        grid_spec=pltpu.PrefetchScalarGridSpec(
            num_scalar_prefetch=1,
            grid=(rows // step_rows,),
            in_specs=[pl.BlockSpec((step_rows, piece_width), lambda i, index: (i, 0))] * len(pieces),
            out_specs=pl.BlockSpec((step_rows,) + out_shape[1:], lambda i, index: (i, 0, 0)),
        ),
        compiler_params=pltpu.CompilerParams(vmem_limit_bytes=48 * 2**20),
        name="assemble",
    )(jnp.reshape(dp_index, (1,)).astype(jnp.int32), *pieces)


def body(
    hidden,
    cotangent,
    attn_gain,
    q_weight,
    kv_down,
    kv_gain,
    kv_up,
    out_weight,
    ffn_gain,
    shared_gate_up,
    shared_down,
    expert_gate_up,
    expert_down,
    expert_ids,
    gate_fix,
    block_ids,
):
    n_dp = lax.axis_size("dp")
    n_seq = lax.axis_size("seq")
    n_all = n_dp * n_seq
    dp_index = lax.axis_index("dp")
    seq_index = lax.axis_index("seq")
    tokens, width = hidden.shape
    sequences, length = block_ids.shape
    part = length // n_seq
    group = n_seq * tokens
    heads = H // n_seq
    per_device = expert_gate_up.shape[1]
    experts = per_device * n_seq
    capacity = TOP * tokens // per_device
    ff_parts = n_dp // per_device
    expert_bit = dp_index % per_device
    down_rows = kv_down.shape[0]
    down_width = kv_down.shape[1]
    q_width = heads * (NOPE + ROPE)
    e_width = heads * (NOPE + VD)
    block_at = dp_block(jnp.asarray(block_table(n_seq)), seq_index)
    block_of = dp_block(jnp.asarray(np.argsort(block_table(n_seq), axis=1)), seq_index)

    def relative(values):
        return jnp.take(values, block_at, axis=0, mode="clip")

    def absolute(values):
        return jnp.take(values, block_of, axis=0, mode="clip")

    ff_width = expert_gate_up.shape[2] // 2
    ff_part = ff_width // ff_parts
    expert_rows = expert_gate_up.shape[0]
    in_parts = expert_gate_up.reshape(expert_rows, per_device, 2, ff_parts, ff_part)
    in_parts = jnp.transpose(in_parts, (3, 1, 0, 2, 4)).reshape(n_dp, expert_rows, 2 * ff_part)
    down_kept = lax.dynamic_index_in_dim(expert_down, expert_bit, 1, keepdims=False)
    down_sent = lax.dynamic_index_in_dim(expert_down, 1 - expert_bit, 1, keepdims=False)
    is_low = expert_bit == 0

    units = shared_down.shape[0]
    shared_cols = shared_gate_up.reshape(down_rows, 2, n_dp, n_seq, units)
    shared_cols = jnp.transpose(shared_cols, (0, 3, 2, 1, 4)).reshape(down_rows, n_seq, -1)

    up_rows = kv_up.reshape(kv_up.shape[0], n_seq, -1, kv_up.shape[0] * e_width // down_rows)
    up_rows = jnp.swapaxes(up_rows, 1, 2).reshape(down_rows, n_seq, -1)
    joined_width = q_width + up_rows.shape[2]
    joined = jnp.concatenate(
        [q_weight.reshape(down_rows, n_seq, q_width), up_rows, shared_cols], axis=2
    )
    joined = lax.all_to_all(joined, "seq", split_axis=1, concat_axis=0, tiled=True)
    joined = joined.reshape(n_seq * down_rows, -1)
    shared_parts = joined[:, joined_width:].reshape(-1, n_dp, 2 * units)
    shared_parts = jnp.swapaxes(shared_parts, 0, 1)
    joined = joined[:, :joined_width]
    joined = [joined] + [dp_swap(joined, n_dp, step) for step in range(1, n_dp)]
    joined = hold(joined, in_parts, down_kept, down_sent)
    joined = in_order(joined, n_dp, dp_index).reshape(-1, joined_width)
    weight_q = joined[:, :q_width]
    weight_up = joined[:, q_width:].reshape(KV_RANK, e_width)

    hidden_group = seq_gather(hidden, n_seq)
    ready = joined
    in_parts = jnp.concatenate([in_parts, shared_parts], axis=2)
    even_steps, odd_steps = range(2, n_dp, 2), range(1, n_dp, 2)
    in_even = dp_exchange(in_parts, n_dp, dp_index, even_steps, ready)
    down_got = dp_swap(hold(down_sent, ready), n_dp, 1)

    labels = jnp.arange(experts, dtype=jnp.int32)
    hits = jnp.sum((expert_ids[:, :, None] == labels).astype(jnp.int32), axis=1)
    earlier = jnp.arange(group, dtype=jnp.int32)[:, None] < seq_index * tokens
    before_own = jnp.sum(jnp.where(earlier, hits, 0), axis=0)
    own_hits = lax.dynamic_slice_in_dim(hits, seq_index * tokens, tokens, 0)
    own_picks = lax.dynamic_slice_in_dim(expert_ids, seq_index * tokens, tokens, 0)
    own_slot = before_own[None, :] + jnp.cumsum(own_hits, axis=0) - own_hits
    code = jnp.where((own_hits > 0) & (own_slot < capacity), own_slot + 1, 0)
    gates = jnp.sum(
        gate_fix[:, :, None] * (own_picks[:, :, None] == labels).astype(jnp.int32), axis=1
    )
    pieces = jnp.stack([code // 16, code % 16, gates // 128, gates % 128], axis=0)
    pieces = jnp.transpose(pieces, (2, 0, 1)).reshape(experts, 4 * tokens).astype(BF16)

    def wide_row(vector):
        return jnp.pad(vector, (0, down_width - 4 * tokens - vector.shape[0]))[None]

    extras = jnp.concatenate([wide_row(attn_gain), wide_row(ffn_gain), wide_row(kv_gain)], axis=0)
    extras = jnp.pad(extras, ((0, experts - 3), (0, 0)))
    message = jnp.concatenate(
        [kv_down, jnp.concatenate([pieces, extras], axis=1)], axis=0
    )
    spread = lax.all_gather(message, BOTH, axis=0, tiled=False)
    weight_down = spread[:, :down_rows].reshape(-1, down_width)
    spread_tail = spread[:, down_rows:]
    first = 4 * tokens
    gain_attn = spread_tail[:, 0, first : first + attn_gain.shape[0]].reshape(-1).astype(F32)
    gain_ffn = spread_tail[:, 1, first : first + ffn_gain.shape[0]].reshape(-1).astype(F32)
    gain_kv = spread_tail[:, 2, first : first + kv_gain.shape[0]].reshape(-1).astype(F32)
    own_expert = per_device * seq_index + expert_bit
    routing = lax.dynamic_index_in_dim(spread_tail, own_expert, axis=1, keepdims=False)
    routing = routing[:, :first].reshape(n_dp, n_seq, 4, tokens).astype(jnp.int32)
    slot_code = routing[:, :, 0] * 16 + routing[:, :, 1]
    gate_of = (routing[:, :, 2] * 128 + routing[:, :, 3]).astype(F32) / GATE_UNIT

    weight_out = lax.all_gather(hold(out_weight, joined, hidden_group), BOTH, axis=0, tiled=True)
    cot_all = lax.all_gather(hold(cotangent, joined, hidden_group, spread), BOTH, axis=0, tiled=True)

    rows_group = hidden_group.astype(F32)
    normed_group = (rows_group * rms_scale(rows_group) * gain_attn).astype(BF16)
    in_part = jnp.arange(tokens, dtype=jnp.int32) % part
    positions = (block_at[:, None] * part + in_part[None, :]).reshape(group)
    cosine, sine = rotary_tables(positions)

    def to_sequence(values):
        split = values.reshape((n_seq, sequences, part) + values.shape[1:])
        return jnp.swapaxes(split, 0, 1).reshape((sequences, length) + values.shape[1:])

    def to_rows(values):
        split = values.reshape((sequences, n_seq, part) + values.shape[2:])
        return jnp.swapaxes(split, 0, 1).reshape((group,) + values.shape[2:])

    query_raw = matmul(normed_group, weight_q).reshape(group, heads, NOPE + ROPE)
    latent_in = matmul(normed_group, weight_down)
    latent_raw = latent_in[:, :KV_RANK]
    latent = (latent_raw * rms_scale(latent_raw) * gain_kv).astype(BF16)
    expanded = matmul(latent, weight_up).reshape(group, heads, NOPE + VD)
    rope_query = rotate(query_raw[..., NOPE:], cosine[:, None], sine[:, None])
    rope_key = rotate(latent_in[:, KV_RANK:], cosine, sine)
    rope_key = jnp.broadcast_to(rope_key[:, None], (group, heads, ROPE))
    queries = to_sequence(
        jnp.concatenate([query_raw[..., :NOPE], rope_query], axis=-1).astype(BF16)
    )
    keys = to_sequence(
        jnp.concatenate([expanded[..., :NOPE], rope_key], axis=-1).astype(BF16)
    )
    values = to_sequence(expanded[..., NOPE:].astype(BF16))
    blocks = jnp.take(block_ids.reshape(sequences, n_seq, part), block_at, axis=1, mode="clip")
    blocks = blocks.reshape(sequences, length)
    score_scale = (NOPE + ROPE) ** (-0.5)
    scores = jnp.einsum("bqhd,bkhd->bhqk", queries, keys, preferred_element_type=F32) * score_scale
    allowed = blocks[:, None, None, :] <= blocks[:, None, :, None]
    scores = jnp.where(allowed, scores, -1e30)
    weights = jnp.exp(scores - jnp.max(scores, axis=-1, keepdims=True))
    probs = weights / jnp.sum(weights, axis=-1, keepdims=True)
    shares = probs.astype(BF16)
    attended = jnp.einsum("bhqk,bkhd->bqhd", shares, values, preferred_element_type=F32)
    attended = to_rows(attended.astype(BF16)).reshape(group, heads * VD)
    in_odd = dp_exchange(in_parts, n_dp, dp_index, odd_steps, (in_even, attended))
    in_moved = in_even | in_odd
    in_moved[0] = dp_block(in_parts, dp_index)
    attended = hold(attended, in_even, down_got)
    heads_out = absolute(attended.reshape(n_seq, tokens, heads * VD))
    heads_out = lax.all_to_all(heads_out, "seq", split_axis=0, concat_axis=2, tiled=True)
    heads_out = heads_out.reshape(tokens, H * VD)

    rows = hidden.astype(F32)
    residual = rows + matmul(heads_out, weight_out)
    normed_ffn = (residual * rms_scale(residual) * gain_ffn).astype(BF16)

    slots = jnp.arange(1, capacity + 1, dtype=jnp.int32)
    all_codes = slot_code.reshape(n_dp, group)
    all_here = all_codes[:, :, None] == slots
    slot_gate = jnp.where(all_here, gate_of.reshape(n_dp, group)[:, :, None], 0.0)
    slot_gate = jnp.sum(slot_gate, axis=1)[:, :, None]
    all_placed = lax.optimization_barrier(all_here.astype(BF16))
    cot_rows = cot_all.reshape(n_dp, group, width)
    slot_cot = jnp.stack(
        [
            (lead_dot(all_placed[g], cot_rows[g]) * slot_gate[g]).astype(BF16)
            for g in range(n_dp)
        ]
    )
    down_kept, down_got = hold((down_kept, down_got), normed_ffn)
    weight_back = jnp.concatenate(
        [jnp.where(is_low, down_kept, down_got), jnp.where(is_low, down_got, down_kept)], axis=0
    )
    shared_act_grad = jnp.stack([tail_dot(cot_rows[g], shared_down) for g in range(n_dp)])

    far = hold(normed_ffn, in_odd)
    ffn_chunks = [normed_ffn] + [dp_swap(far, n_dp, step) for step in range(1, n_dp)]
    ffn_chunks = [seq_gather(chunk, n_seq) for chunk in ffn_chunks]
    chunk_places, kept_rows = [], []
    for step in range(n_dp):
        codes = relative(dp_block(slot_code, dp_index ^ step)).reshape(group)
        placed = lax.optimization_barrier((codes[:, None] == slots).astype(BF16))
        if step == 1:
            placed = hold(placed, slot_cot, shared_act_grad)
        chunk_places.append(placed)
        kept_rows.append(lead_dot(placed, ffn_chunks[step]).astype(BF16))

    in_moved = hold([in_moved[step] for step in range(n_dp)], ffn_chunks[0])
    weight_in = in_order(in_moved, n_dp, dp_index).reshape(width, -1)
    weight_shared_in = weight_in[:, 2 * ff_part :]
    weight_in = weight_in[:, : 2 * ff_part]
    shared_in_back = weight_shared_in.T
    grad_shared_in = 0.0
    kept_cots, kept_acts, kept_grads = [], [], []
    kept_shared, shared_acts, spreads = [], [], []
    for step in range(n_dp):
        ffn_rows = ffn_chunks[step]
        shared_in = matmul(ffn_rows, weight_shared_in)
        shared_gate, shared_up = shared_in[:, :units], shared_in[:, units:]
        act_grad = dp_block(shared_act_grad, dp_index ^ step)
        act_grad = relative(act_grad.reshape(n_seq, tokens, units)).reshape(group, units)
        shared_in_grad = jnp.concatenate(
            swiglu_back(shared_gate, shared_up, act_grad), axis=1
        ).astype(BF16)
        kept_shared.append(shared_in_grad)
        shared_acts.append(swiglu(shared_gate, shared_up).astype(BF16))

        spreads.append((chunk_places[step], shared_in_grad))

    for step in range(n_dp):
        expert_in = matmul(kept_rows[step], weight_in)
        expert_gate, expert_up = expert_in[:, :ff_part], expert_in[:, ff_part:]
        chunk_cot = dp_block(slot_cot, dp_index ^ step)
        expert_in_grad = jnp.concatenate(
            swiglu_back(expert_gate, expert_up, tail_dot(chunk_cot, weight_back)), axis=1
        ).astype(BF16)
        slot_grad = tail_dot(expert_in_grad, weight_in).astype(BF16)
        spreads[step] += (slot_grad,)
        kept_cots.append(chunk_cot)
        kept_acts.append(swiglu(expert_gate, expert_up).astype(BF16))
        kept_grads.append(expert_in_grad)

    planes, sums = [], []
    for step in list(range(1, n_dp)) + [0]:
        placed, shared_in_grad, slot_grad = spreads[step]
        for age in range(1, min(len(planes), 3) + 1):
            placed = hold(placed, planes[-age][age - 1])
        left_side = jnp.concatenate([placed, shared_in_grad], axis=1)
        right_side = jnp.concatenate([slot_grad, shared_in_back], axis=0)
        planes.append(seq_scatter(lambda part: matmul(half_of(left_side, part), right_side), n_seq))
        if step:
            sums.append(dp_swap(planes[-1][-1].astype(BF16), n_dp, step).astype(F32))
        else:
            sums.append(planes[-1][-1])
    ffn_grad = sum(sums[1:], sums[0])

    from_norm, gain_ffn_grad = rms_back(residual, gain_ffn, ffn_grad)
    residual_grad = cotangent.astype(F32) + from_norm
    residual_low = residual_grad.astype(BF16)
    heads_grad = tail_dot(residual_low, weight_out).astype(BF16)
    heads_grad = heads_grad.reshape(tokens, n_seq, heads * VD)
    heads_grad = lax.all_to_all(heads_grad, "seq", split_axis=1, concat_axis=0, tiled=True)

    out_acts, shared_acts = hold((kept_acts, shared_acts), planes[-1][0])
    kept_rows, kept_cots, kept_acts, kept_grads, ffn_chunks = hold(
        (kept_rows, kept_cots, kept_acts, kept_grads, ffn_chunks), heads_grad
    )
    grad_in = lead_dot(jnp.concatenate(kept_rows), jnp.concatenate(kept_grads)).astype(BF16)
    back_parts = grad_in.reshape(n_dp, expert_rows, 2 * ff_part)
    back_even = dp_exchange(back_parts, n_dp, dp_index, even_steps, ffn_grad)
    expert_act = in_order(out_acts, n_dp, dp_index)
    grad_back = lead_dot(jnp.concatenate(kept_acts), jnp.concatenate(kept_cots))
    half = expert_down.shape[0]
    low_half, high_half = grad_back[:half], grad_back[half:]
    grad_kept = jnp.where(is_low, low_half, high_half)
    grad_sent = jnp.where(is_low, high_half, low_half).astype(BF16)
    grad_got = dp_swap(hold(grad_sent, ffn_grad), n_dp, 1)
    shared_act = in_order(
        [absolute(act.reshape(n_seq, tokens, units)) for act in shared_acts], n_dp, dp_index
    ).reshape(n_dp, group, units)
    expert_out = (contract(expert_act, weight_back, 2, 0) * slot_gate).astype(BF16)
    out_part = jnp.einsum(
        "gtk,gkd->gtd",
        jnp.concatenate([all_placed, shared_act], axis=2),
        jnp.concatenate(
            [expert_out, jnp.broadcast_to(shared_down, (n_dp, units, width))], axis=1
        ),
        preferred_element_type=F32,
    ).astype(BF16)
    out_sum = lax.psum_scatter(
        hold(out_part.reshape(n_all * tokens, width), ffn_grad),
        BOTH,
        scatter_dimension=0,
        tiled=True,
    )
    output = (residual + out_sum.astype(F32)).astype(BF16)
    shared_late = hold(shared_act, heads_grad).reshape(n_all * tokens, units)
    grad_shared_down = lead_dot(shared_late, cot_all)
    for step in range(n_dp):
        grad_shared_in = grad_shared_in + lead_dot(ffn_chunks[step], kept_shared[step])

    residual_group = seq_gather(hold(residual_low, heads_grad), n_seq)
    grad_shared_in = hold(grad_shared_in.astype(BF16), heads_grad)
    shared_back = lax.all_to_all(
        grad_shared_in.reshape(n_all, -1, 2 * units), BOTH, split_axis=0, concat_axis=0, tiled=True
    )
    heads_grad = relative(heads_grad.reshape(n_seq, tokens, heads * VD))
    grad_out_heads = lead_dot(attended, residual_group)
    out_shard = dp_scatter(grad_out_heads, n_dp, dp_index)
    home = [
        (d * n_seq + s, s * n_dp + d) for d in range(n_dp) for s in range(n_seq)
    ]
    grad_out_weight = lax.ppermute(out_shard, BOTH, home)

    grad_o = to_sequence(heads_grad.reshape(group, heads, VD))
    prob_grad = jnp.einsum("bqhd,bkhd->bhqk", grad_o, values, preferred_element_type=F32)
    centre = jnp.sum(probs * prob_grad, axis=-1, keepdims=True)
    score_grad = (probs * (prob_grad - centre)).astype(BF16)
    query_grad = jnp.einsum("bhqk,bkhd->bqhd", score_grad, keys, preferred_element_type=F32)
    key_grad = jnp.einsum("bhqk,bqhd->bkhd", score_grad, queries, preferred_element_type=F32)
    value_grad = jnp.einsum("bhqk,bqhd->bkhd", shares, grad_o, preferred_element_type=F32)
    query_grad = to_rows((query_grad * score_scale).astype(BF16)).astype(F32)
    key_grad = to_rows((key_grad * score_scale).astype(BF16)).astype(F32)
    value_grad = to_rows(value_grad.astype(BF16))
    query_low = jnp.concatenate(
        [
            query_grad[..., :NOPE],
            rotate_back(query_grad[..., NOPE:], cosine[:, None], sine[:, None]),
        ],
        axis=-1,
    ).astype(BF16).reshape(group, q_width)
    rope_grad = rotate_back(jnp.sum(key_grad[..., NOPE:], axis=1), cosine, sine)
    expand_low = jnp.concatenate(
        [key_grad[..., :NOPE].astype(BF16), value_grad], axis=-1
    ).reshape(group, e_width)

    latent_sum = seq_scatter(
        lambda part: jnp.concatenate(
            [tail_dot(half_of(expand_low, part), weight_up), half_of(rope_grad, part)], axis=1
        ),
        n_seq,
    )[-1]
    normed_low = [tail_dot(half_of(query_low, part), weight_q).astype(BF16) for part in (0, 1)]
    normed_sum = seq_scatter(lambda part: normed_low[part], n_seq)[-1]
    unit_rows = rows_group * rms_scale(rows_group)
    gain_attn_grad = sum(
        jnp.sum(normed_low[part].astype(F32) * half_of(unit_rows, part), axis=0) for part in (0, 1)
    )
    grad_q = lead_dot(normed_group, query_low)
    grad_up = lead_dot(latent, expand_low).reshape(width, -1)
    grad_joined = hold(jnp.concatenate([grad_q, grad_up], axis=1), back_even, grad_got)
    grad_joined = dp_scatter(grad_joined, n_dp, dp_index)
    back_odd = dp_exchange(back_parts, n_dp, dp_index, odd_steps, grad_joined)
    grad_joined = grad_joined.reshape(n_seq, down_rows, joined_width)
    grad_joined = hold(grad_joined, shared_back)
    grad_joined = lax.all_to_all(grad_joined, "seq", split_axis=0, concat_axis=0, tiled=True)
    grad_q = jnp.swapaxes(grad_joined[..., :q_width], 0, 1).reshape(q_weight.shape)
    grad_up = grad_joined[..., q_width:].reshape(n_seq, kv_up.shape[0], e_width)
    grad_up = jnp.swapaxes(grad_up, 0, 1).reshape(kv_up.shape)

    latent_grad, gain_kv_grad = rms_back(latent_raw[:tokens], gain_kv, latent_sum[:, :KV_RANK])
    down_low = jnp.concatenate([latent_grad, latent_sum[:, KV_RANK:]], axis=1).astype(BF16)
    down_group = seq_gather(down_low, n_seq)
    normed_cols = normed_group.reshape(group, n_dp, n_seq, down_rows)
    normed_cols = lax.dynamic_index_in_dim(normed_cols, seq_index, 2, keepdims=False)
    grad_down = lead_dot(normed_cols.reshape(group, n_dp * down_rows), down_group)
    grad_down = dp_scatter(grad_down, n_dp, dp_index)

    in_back = back_even | back_odd
    in_back[0] = dp_block(back_parts, dp_index)
    in_back, grad_got, shared_back = hold((in_back, grad_got, shared_back), down_low)
    in_back = [in_back[step] for step in range(n_dp)]
    grad_expert_in = assemble(in_back, dp_index, expert_gate_up.shape)
    grad_got = grad_got.astype(F32)
    grad_expert_down = jnp.stack(
        [jnp.where(is_low, grad_kept, grad_got), jnp.where(is_low, grad_got, grad_kept)], axis=1
    )
    shared_back = shared_back.reshape(n_all, -1, 2, units).astype(F32)
    grad_shared_gate_up = jnp.transpose(shared_back, (1, 2, 0, 3)).reshape(shared_gate_up.shape)

    down_grad = tail_dot(down_low, weight_down)
    rows_from_norm, _ = rms_back(rows, gain_attn, normed_sum + down_grad)
    input_grad = residual_grad + rows_from_norm

    gain_attn_grad = gain_attn_grad + jnp.sum(down_grad * rows * rms_scale(rows), axis=0)
    gain_grads = jnp.concatenate(
        [
            gain_attn_grad.reshape(n_all, -1),
            gain_ffn_grad.reshape(n_all, -1),
            gain_kv_grad.reshape(n_all, -1),
        ],
        axis=1,
    )
    gain_grads = lax.all_to_all(gain_grads, BOTH, split_axis=0, concat_axis=0, tiled=True)
    gain_grads = jnp.sum(gain_grads, axis=0)
    attn_end = attn_gain.shape[0]
    ffn_end = attn_end + ffn_gain.shape[0]

    return (
        output,
        input_grad,
        gain_grads[:attn_end],
        grad_q,
        grad_down,
        gain_grads[ffn_end:],
        grad_up,
        grad_out_weight,
        gain_grads[attn_end:ffn_end],
        grad_shared_gate_up,
        grad_shared_down,
        grad_expert_in,
        grad_expert_down,
    )


def solution(mesh):
    rows = P(BOTH, None)
    return jax.shard_map(
        body,
        mesh=mesh,
        in_specs=(
            rows,
            rows,
            P(BOTH),
            rows,
            rows,
            P(BOTH),
            rows,
            rows,
            P(BOTH),
            rows,
            rows,
            P("dp", "seq", None),
            P("dp", "seq", None),
            P("dp", None),
            rows,
            P("dp", None),
        ),
        out_specs=(
            rows,
            rows,
            P(BOTH),
            rows,
            rows,
            P(BOTH),
            rows,
            rows,
            P(BOTH),
            rows,
            rows,
            P("dp", "seq", None),
            P("dp", "seq", None),
        ),
        check_vma=False,
    )
```

```python
import jax
import jax.numpy as jnp
import numpy as np
from jax import lax
from jax.experimental import pallas as pl
from jax.experimental.pallas import tpu as pltpu
from jax.sharding import PartitionSpec as P

H = 16
NOPE = 128
ROPE = 64
VD = 128
KV_RANK = 512
TOP = 6

EPS = 1e-06
THETA = 10000.0
GATE_UNIT = 16384.0

BOTH = ("dp", "seq")
F32 = jnp.float32
BF16 = jnp.bfloat16


def contract(left_side, right_side, left_dim, right_dim):
    return lax.dot_general(
        left_side,
        right_side,
        (((left_dim,), (right_dim,)), ((), ())),
        preferred_element_type=F32,
    )


def matmul(left_side, right_side):
    return contract(left_side, right_side, left_side.ndim - 1, 0)


def lead_dot(left_side, right_side):
    return contract(left_side, right_side, 0, 0)


def tail_dot(left_side, right_side):
    return contract(left_side, right_side, 1, 1)


def rms_scale(values):
    return lax.rsqrt(jnp.mean(values * values, axis=-1, keepdims=True) + EPS)


def rms_back(values, gain, grad):
    scale = rms_scale(values)
    unit = values * scale
    weighted = grad * gain
    centre = jnp.mean(weighted * unit, axis=-1, keepdims=True)
    return scale * (weighted - unit * centre), jnp.sum(grad * unit, axis=0)


def swiglu(gate, up):
    return jax.nn.silu(gate) * up


def swiglu_back(gate, up, grad):
    sig = jax.nn.sigmoid(gate)
    return grad * up * sig * (1.0 + gate * (1.0 - sig)), grad * (gate * sig)


def rotary_tables(positions):
    half_width = ROPE // 2
    frequency = THETA ** (-jnp.arange(half_width, dtype=F32) * 2.0 / ROPE)
    angles = positions.astype(F32)[:, None] * frequency[None, :]
    return jnp.cos(angles), jnp.sin(angles)


def rotate(values, cosine, sine):
    half_width = values.shape[-1] // 2
    lead = values[..., :half_width]
    trail = values[..., half_width:]
    return jnp.concatenate([lead * cosine - trail * sine, trail * cosine + lead * sine], axis=-1)


def rotate_back(grads, cosine, sine):
    return rotate(grads, cosine, -sine)


def link_orders(n_seq):
    bits = [1 << j for j in range(1, n_seq.bit_length() - 1)]
    return bits, bits[::-1]


def block_table(n_seq):
    orders = link_orders(n_seq)
    steps = len(orders[0])
    table = np.zeros((n_seq, n_seq), np.int32)
    for s in range(n_seq):
        for m in range(n_seq):
            core = (s & 1) ^ (m >> steps)
            other = (s & ~1) | core
            for j in range(steps):
                if m >> j & 1:
                    other ^= orders[core][j]
            table[s, m] = other
    return table


def seq_step(values, n_seq, step):
    orders = link_orders(n_seq)
    return lax.ppermute(values, "seq", [(s, s ^ orders[s & 1][step]) for s in range(n_seq)])


def core_swap(values, n_seq):
    return lax.ppermute(values, "seq", [(s, s ^ 1) for s in range(n_seq)])


def seq_gather(values, n_seq, first=None):
    current = values if first is None else first
    for step in range(0 if first is None else 1, len(link_orders(n_seq)[0])):
        current = jnp.concatenate([current, seq_step(current, n_seq, step)], axis=0)
    return jnp.concatenate([current, core_swap(current, n_seq)], axis=0)


def seq_scatter(make_half, n_seq):
    sent = core_swap(make_half(1).astype(BF16), n_seq)
    kept = make_half(0)
    stages = []
    for step in reversed(range(len(link_orders(n_seq)[0]))):
        half = sent.shape[0] // 2
        onward = (kept[half:].astype(F32) + sent[half:].astype(F32)).astype(BF16)
        kept = kept[:half].astype(F32) + sent[:half].astype(F32)
        stages.append(kept)
        sent = seq_step(onward, n_seq, step)
    stages.append(kept + sent.astype(F32))
    return stages


def half_of(values, part):
    half = values.shape[0] // 2
    return values[part * half : (part + 1) * half]


def hold(value, *until):
    return lax.optimization_barrier((value,) + until)[0]


def dp_swap(values, n_dp, step):
    return lax.ppermute(values, "dp", [(d, d ^ step) for d in range(n_dp)])


def dp_block(blocks, index):
    return lax.dynamic_index_in_dim(blocks, index, 0, keepdims=False)


def dp_exchange(blocks, n_dp, dp_index, steps, until):
    blocks = hold(blocks, until)
    return {
        step: dp_swap(dp_block(blocks, dp_index ^ step), n_dp, step) for step in steps
    }


def in_order(moved, n_dp, dp_index):
    result = jnp.zeros((n_dp,) + moved[0].shape, moved[0].dtype)
    for step in range(n_dp):
        result = lax.dynamic_update_index_in_dim(result, moved[step], dp_index ^ step, 0)
    return result


def dp_scatter(values, n_dp, dp_index):
    blocks = values.reshape((n_dp, -1) + values.shape[1:])
    low = blocks.astype(BF16)
    total = dp_block(blocks, dp_index).astype(F32)
    for step in range(1, n_dp):
        total = total + dp_swap(dp_block(low, dp_index ^ step), n_dp, step).astype(F32)
    return total


def assemble_kernel(index_ref, *refs):
    pieces, out_ref = refs[:-1], refs[-1]
    count = len(pieces)
    per_device = out_ref.shape[1]
    part = pieces[0].shape[1] // 2
    values = [piece[...].astype(F32) for piece in pieces]
    for expert in range(per_device):
        gates, ups = [], []
        for ff in range(count // per_device):
            step = index_ref[0] ^ (ff * per_device + expert)
            chosen = values[0]
            for j in range(1, count):
                chosen = jnp.where(step == j, values[j], chosen)
            gates.append(chosen[:, :part])
            ups.append(chosen[:, part:])
        out_ref[:, expert, :] = jnp.concatenate(gates + ups, axis=1)


def assemble(pieces, dp_index, out_shape):
    rows, piece_width = pieces[0].shape
    step_rows = 64
    return pl.pallas_call(
        assemble_kernel,
        out_shape=jax.ShapeDtypeStruct(out_shape, F32),
        grid_spec=pltpu.PrefetchScalarGridSpec(
            num_scalar_prefetch=1,
            grid=(rows // step_rows,),
            in_specs=[pl.BlockSpec((step_rows, piece_width), lambda i, index: (i, 0))] * len(pieces),
            out_specs=pl.BlockSpec((step_rows,) + out_shape[1:], lambda i, index: (i, 0, 0)),
        ),
        compiler_params=pltpu.CompilerParams(vmem_limit_bytes=48 * 2**20),
        name="assemble",
    )(jnp.reshape(dp_index, (1,)).astype(jnp.int32), *pieces)


def lay_out_kernel(index_ref, *refs):
    count = (len(refs) - 2)
    pieces, out_ref, sems = refs[:count], refs[count], refs[count + 1]
    rows = pieces[0].shape[0]
    copies = [
        pltpu.make_async_copy(
            pieces[step], out_ref.at[pl.ds((index_ref[0] ^ step) * rows, rows)], sems.at[step]
        )
        for step in range(count)
    ]
    for copy in copies:
        copy.start()
    for copy in copies:
        copy.wait()


def lay_out(pieces, dp_index):
    rows, cols = pieces[0].shape
    count = len(pieces)
    return pl.pallas_call(
        lay_out_kernel,
        out_shape=jax.ShapeDtypeStruct((count * rows, cols), pieces[0].dtype),
        grid_spec=pltpu.PrefetchScalarGridSpec(
            num_scalar_prefetch=1,
            grid=(1,),
            in_specs=[pl.BlockSpec(memory_space=pl.ANY)] * count,
            out_specs=pl.BlockSpec(memory_space=pl.ANY),
            scratch_shapes=[pltpu.SemaphoreType.DMA((count,))],
        ),
        name="lay_out",
    )(jnp.reshape(dp_index, (1,)).astype(jnp.int32), *pieces)


def body(
    hidden,
    cotangent,
    attn_gain,
    q_weight,
    kv_down,
    kv_gain,
    kv_up,
    out_weight,
    ffn_gain,
    shared_gate_up,
    shared_down,
    expert_gate_up,
    expert_down,
    expert_ids,
    gate_fix,
    block_ids,
):
    n_dp = lax.axis_size("dp")
    n_seq = lax.axis_size("seq")
    n_all = n_dp * n_seq
    dp_index = lax.axis_index("dp")
    seq_index = lax.axis_index("seq")
    tokens, width = hidden.shape
    sequences, length = block_ids.shape
    part = length // n_seq
    group = n_seq * tokens
    heads = H // n_seq
    per_device = expert_gate_up.shape[1]
    experts = per_device * n_seq
    capacity = TOP * tokens // per_device
    ff_parts = n_dp // per_device
    expert_bit = dp_index % per_device
    down_rows = kv_down.shape[0]
    down_width = kv_down.shape[1]
    q_width = heads * (NOPE + ROPE)
    e_width = heads * (NOPE + VD)
    block_at = dp_block(jnp.asarray(block_table(n_seq)), seq_index)
    block_of = dp_block(jnp.asarray(np.argsort(block_table(n_seq), axis=1)), seq_index)

    def relative(values):
        return jnp.take(values, block_at, axis=0, mode="clip")

    def absolute(values):
        return jnp.take(values, block_of, axis=0, mode="clip")

    ff_width = expert_gate_up.shape[2] // 2
    ff_part = ff_width // ff_parts
    expert_rows = expert_gate_up.shape[0]
    in_parts = expert_gate_up.reshape(expert_rows, per_device, 2, ff_parts, ff_part)
    in_parts = jnp.transpose(in_parts, (3, 1, 0, 2, 4)).reshape(n_dp, expert_rows, 2 * ff_part)
    down_kept = lax.dynamic_index_in_dim(expert_down, expert_bit, 1, keepdims=False)
    down_sent = lax.dynamic_index_in_dim(expert_down, 1 - expert_bit, 1, keepdims=False)
    is_low = expert_bit == 0

    units = shared_down.shape[0]
    shared_cols = shared_gate_up.reshape(down_rows, 2, n_dp, n_seq, units)
    shared_cols = jnp.transpose(shared_cols, (0, 3, 2, 1, 4)).reshape(down_rows, n_seq, -1)

    out_far = [out_weight] + [dp_swap(out_weight, n_dp, step) for step in range(1, n_dp)]
    out_rows = jnp.concatenate(out_far, axis=0)
    late_cot = hold(cotangent, out_far)
    cot_far = [late_cot] + [dp_swap(late_cot, n_dp, step) for step in range(1, n_dp)]

    up_rows = kv_up.reshape(kv_up.shape[0], n_seq, -1, kv_up.shape[0] * e_width // down_rows)
    up_rows = jnp.swapaxes(up_rows, 1, 2).reshape(down_rows, n_seq, -1)
    joined_width = q_width + up_rows.shape[2]
    joined = jnp.concatenate(
        [q_weight.reshape(down_rows, n_seq, q_width), up_rows, shared_cols], axis=2
    )
    joined = lax.all_to_all(joined, "seq", split_axis=1, concat_axis=0, tiled=True)
    joined = joined.reshape(n_seq * down_rows, -1)
    shared_parts = joined[:, joined_width:].reshape(-1, n_dp, 2 * units)
    shared_parts = jnp.swapaxes(shared_parts, 0, 1)
    joined = joined[:, :joined_width]
    joined = [joined] + [dp_swap(joined, n_dp, step) for step in range(1, n_dp)]
    joined = hold(joined, in_parts, down_kept, down_sent, cot_far)
    joined = in_order(joined, n_dp, dp_index).reshape(-1, joined_width)
    weight_q = joined[:, :q_width]
    weight_up = joined[:, q_width:].reshape(KV_RANK, e_width)

    hidden_group = seq_gather(hidden, n_seq)
    out_rows = seq_gather(hold(out_rows, joined), n_seq).reshape(n_seq, n_dp * down_rows, width)
    ready = joined
    in_parts = jnp.concatenate([in_parts, shared_parts], axis=2)
    even_steps, odd_steps = range(2, n_dp, 2), range(1, n_dp, 2)
    in_even = dp_exchange(in_parts, n_dp, dp_index, even_steps, ready)
    down_got = dp_swap(hold(down_sent, ready), n_dp, 1)

    labels = jnp.arange(experts, dtype=jnp.int32)
    hits = jnp.sum((expert_ids[:, :, None] == labels).astype(jnp.int32), axis=1)
    earlier = jnp.arange(group, dtype=jnp.int32)[:, None] < seq_index * tokens
    before_own = jnp.sum(jnp.where(earlier, hits, 0), axis=0)
    own_hits = lax.dynamic_slice_in_dim(hits, seq_index * tokens, tokens, 0)
    own_picks = lax.dynamic_slice_in_dim(expert_ids, seq_index * tokens, tokens, 0)
    own_slot = before_own[None, :] + jnp.cumsum(own_hits, axis=0) - own_hits
    code = jnp.where((own_hits > 0) & (own_slot < capacity), own_slot + 1, 0)
    gates = jnp.sum(
        gate_fix[:, :, None] * (own_picks[:, :, None] == labels).astype(jnp.int32), axis=1
    )
    pieces = jnp.stack([code // 16, code % 16, gates // 128, gates % 128], axis=0)
    pieces = jnp.transpose(pieces, (2, 0, 1)).reshape(experts, 4 * tokens).astype(BF16)

    def wide_row(vector):
        return jnp.pad(vector, (0, down_width - 4 * tokens - vector.shape[0]))[None]

    extras = jnp.concatenate([wide_row(attn_gain), wide_row(ffn_gain), wide_row(kv_gain)], axis=0)
    extras = jnp.pad(extras, ((0, experts - 3), (0, 0)))
    message = jnp.concatenate(
        [kv_down, jnp.concatenate([pieces, extras], axis=1)], axis=0
    )
    spread = lax.all_gather(message, BOTH, axis=0, tiled=False)
    weight_down = spread[:, :down_rows].reshape(-1, down_width)
    spread_tail = spread[:, down_rows:]
    first = 4 * tokens
    gain_attn = spread_tail[:, 0, first : first + attn_gain.shape[0]].reshape(-1).astype(F32)
    gain_ffn = spread_tail[:, 1, first : first + ffn_gain.shape[0]].reshape(-1).astype(F32)
    gain_kv = spread_tail[:, 2, first : first + kv_gain.shape[0]].reshape(-1).astype(F32)
    own_expert = per_device * seq_index + expert_bit
    routing = lax.dynamic_index_in_dim(spread_tail, own_expert, axis=1, keepdims=False)
    routing = routing[:, :first].reshape(n_dp, n_seq, 4, tokens).astype(jnp.int32)
    slot_code = routing[:, :, 0] * 16 + routing[:, :, 1]
    gate_of = (routing[:, :, 2] * 128 + routing[:, :, 3]).astype(F32) / GATE_UNIT

    out_rows = absolute(out_rows).reshape(n_seq, n_dp, down_rows, width)
    dp_order = jnp.arange(n_dp, dtype=jnp.int32) ^ dp_index
    weight_out = jnp.swapaxes(jnp.take(out_rows, dp_order, axis=1, mode="clip"), 0, 1)
    weight_out = weight_out.reshape(H * VD, width)

    rows_group = hidden_group.astype(F32)
    normed_group = (rows_group * rms_scale(rows_group) * gain_attn).astype(BF16)
    in_part = jnp.arange(tokens, dtype=jnp.int32) % part
    positions = (block_at[:, None] * part + in_part[None, :]).reshape(group)
    cosine, sine = rotary_tables(positions)

    def to_sequence(values):
        split = values.reshape((n_seq, sequences, part) + values.shape[1:])
        return jnp.swapaxes(split, 0, 1).reshape((sequences, length) + values.shape[1:])

    def to_rows(values):
        split = values.reshape((sequences, n_seq, part) + values.shape[2:])
        return jnp.swapaxes(split, 0, 1).reshape((group,) + values.shape[2:])

    query_raw = matmul(normed_group, weight_q).reshape(group, heads, NOPE + ROPE)
    latent_in = matmul(normed_group, weight_down)
    latent_raw = latent_in[:, :KV_RANK]
    latent = (latent_raw * rms_scale(latent_raw) * gain_kv).astype(BF16)
    cot_chunks = [seq_gather(chunk, n_seq) for chunk in hold(cot_far[:2], latent)]
    expanded = matmul(latent, weight_up).reshape(group, heads, NOPE + VD)
    rope_query = rotate(query_raw[..., NOPE:], cosine[:, None], sine[:, None])
    rope_key = rotate(latent_in[:, KV_RANK:], cosine, sine)
    rope_key = jnp.broadcast_to(rope_key[:, None], (group, heads, ROPE))
    queries = to_sequence(
        jnp.concatenate([query_raw[..., :NOPE], rope_query], axis=-1).astype(BF16)
    )
    keys = to_sequence(
        jnp.concatenate([expanded[..., :NOPE], rope_key], axis=-1).astype(BF16)
    )
    values = to_sequence(expanded[..., NOPE:].astype(BF16))
    blocks = jnp.take(block_ids.reshape(sequences, n_seq, part), block_at, axis=1, mode="clip")
    blocks = blocks.reshape(sequences, length)
    score_scale = (NOPE + ROPE) ** (-0.5)
    scores = jnp.einsum("bqhd,bkhd->bhqk", queries, keys, preferred_element_type=F32) * score_scale
    allowed = blocks[:, None, None, :] <= blocks[:, None, :, None]
    scores = jnp.where(allowed, scores, -1e30)
    weights = jnp.exp(scores - jnp.max(scores, axis=-1, keepdims=True))
    probs = weights / jnp.sum(weights, axis=-1, keepdims=True)
    shares = probs.astype(BF16)
    attended = jnp.einsum("bhqk,bkhd->bqhd", shares, values, preferred_element_type=F32)
    attended = to_rows(attended.astype(BF16)).reshape(group, heads * VD)
    in_odd = dp_exchange(in_parts, n_dp, dp_index, odd_steps, (in_even, attended))
    in_moved = in_even | in_odd
    in_moved[0] = dp_block(in_parts, dp_index)
    attended = hold(attended, in_even, down_got)
    heads_out = absolute(attended.reshape(n_seq, tokens, heads * VD))
    heads_out = lax.all_to_all(heads_out, "seq", split_axis=0, concat_axis=2, tiled=True)
    heads_out = hold(heads_out.reshape(tokens, H * VD), cot_chunks)

    rows = hidden.astype(F32)
    residual = rows + matmul(heads_out, weight_out)
    normed_ffn = (residual * rms_scale(residual) * gain_ffn).astype(BF16)

    slots = jnp.arange(1, capacity + 1, dtype=jnp.int32)
    down_kept, down_got = hold((down_kept, down_got), normed_ffn)
    weight_back = jnp.concatenate(
        [jnp.where(is_low, down_kept, down_got), jnp.where(is_low, down_got, down_kept)], axis=0
    )

    far = hold(normed_ffn, in_odd)
    cot_chunks += [seq_gather(chunk, n_seq) for chunk in hold(cot_far[2:], far)]
    near = jnp.concatenate([normed_ffn, seq_step(normed_ffn, n_seq, 0)], axis=0)
    ffn_chunks = [seq_gather(normed_ffn, n_seq, near)]
    for step in range(1, n_dp):
        ffn_chunks.append(seq_gather(dp_swap(far, n_dp, step), n_seq))
    in_moved = hold([in_moved[step] for step in range(n_dp)], near)
    weight_in = lay_out(in_moved, dp_index)
    weight_shared_in = weight_in[:, 2 * ff_part :]
    weight_in = weight_in[:, : 2 * ff_part]
    chunk_places, chunk_gates, kept_rows, kept_cots = [], [], [], []
    for step in range(n_dp):
        codes = relative(dp_block(slot_code, dp_index ^ step)).reshape(group)
        gates_here = relative(dp_block(gate_of, dp_index ^ step)).reshape(group)
        here = codes[:, None] == slots
        placed = lax.optimization_barrier(here.astype(BF16))
        slot_gate = jnp.sum(jnp.where(here, gates_here[:, None], 0.0), axis=0)[:, None]
        chunk_places.append(placed)
        chunk_gates.append(slot_gate)
        kept_cots.append((lead_dot(placed, cot_chunks[step]) * slot_gate).astype(BF16))
        kept_rows.append(lead_dot(placed, ffn_chunks[step]).astype(BF16))
    shared_in_back = weight_shared_in.T
    grad_shared_in = 0.0
    kept_acts, kept_grads = [], []
    kept_shared, shared_acts, spreads = [], [], []
    for step in range(n_dp):
        ffn_rows = ffn_chunks[step]
        shared_in = matmul(ffn_rows, weight_shared_in)
        shared_gate, shared_up = shared_in[:, :units], shared_in[:, units:]
        act_grad = tail_dot(cot_chunks[step], shared_down)
        shared_in_grad = jnp.concatenate(
            swiglu_back(shared_gate, shared_up, act_grad), axis=1
        ).astype(BF16)
        kept_shared.append(shared_in_grad)
        shared_acts.append(swiglu(shared_gate, shared_up).astype(BF16))

        spreads.append((chunk_places[step], shared_in_grad))

    for step in range(n_dp):
        expert_in = matmul(kept_rows[step], weight_in)
        expert_gate, expert_up = expert_in[:, :ff_part], expert_in[:, ff_part:]
        expert_in_grad = jnp.concatenate(
            swiglu_back(expert_gate, expert_up, tail_dot(kept_cots[step], weight_back)), axis=1
        ).astype(BF16)
        slot_grad = tail_dot(expert_in_grad, weight_in).astype(BF16)
        spreads[step] += (slot_grad,)
        kept_acts.append(swiglu(expert_gate, expert_up).astype(BF16))
        kept_grads.append(expert_in_grad)

    planes, sums = [], []
    for step in list(range(1, n_dp)) + [0]:
        placed, shared_in_grad, slot_grad = spreads[step]
        for age in range(1, min(len(planes), 3) + 1):
            placed = hold(placed, planes[-age][age - 1])
        left_side = jnp.concatenate([placed, shared_in_grad], axis=1)
        right_side = jnp.concatenate([slot_grad, shared_in_back], axis=0)
        planes.append(seq_scatter(lambda part: matmul(half_of(left_side, part), right_side), n_seq))
        if step:
            sums.append(dp_swap(planes[-1][-1].astype(BF16), n_dp, step).astype(F32))
        else:
            sums.append(planes[-1][-1])
    ffn_grad = sum(sums[1:], sums[0])

    from_norm, gain_ffn_grad = rms_back(residual, gain_ffn, ffn_grad)
    residual_grad = cotangent.astype(F32) + from_norm
    residual_low = residual_grad.astype(BF16)
    heads_grad = tail_dot(residual_low, weight_out).astype(BF16)
    heads_grad = heads_grad.reshape(tokens, n_seq, heads * VD)
    heads_grad = lax.all_to_all(heads_grad, "seq", split_axis=1, concat_axis=0, tiled=True)

    late_acts, late_cots, late_rows = hold((shared_acts, cot_chunks, ffn_chunks), planes[-1][0])
    grad_shared_down = 0.0
    for step in range(n_dp):
        grad_shared_down = grad_shared_down + lead_dot(late_acts[step], late_cots[step])
        grad_shared_in = grad_shared_in + lead_dot(late_rows[step], kept_shared[step])
    out_acts, shared_acts = hold(
        (kept_acts, shared_acts), planes[-1][0], grad_shared_down, grad_shared_in
    )
    out_halves = []
    for step in range(n_dp):
        expert_out = (matmul(out_acts[step], weight_back) * chunk_gates[step]).astype(BF16)
        left_side = jnp.concatenate([chunk_places[step], shared_acts[step]], axis=1)
        right_side = jnp.concatenate([expert_out, shared_down], axis=0)
        out_halves.append(
            [matmul(half_of(left_side, part), right_side).astype(BF16) for part in (0, 1)]
        )
    kept_rows, kept_cots, kept_acts, kept_grads = hold(
        (kept_rows, kept_cots, kept_acts, kept_grads), heads_grad
    )
    grad_in = lead_dot(jnp.concatenate(kept_rows), jnp.concatenate(kept_grads)).astype(BF16)
    back_parts = grad_in.reshape(n_dp, expert_rows, 2 * ff_part)
    back_even = dp_exchange(back_parts, n_dp, dp_index, even_steps, ffn_grad)
    grad_back = lead_dot(jnp.concatenate(kept_acts), jnp.concatenate(kept_cots))
    half = expert_down.shape[0]
    low_half, high_half = grad_back[:half], grad_back[half:]
    grad_kept = jnp.where(is_low, low_half, high_half)
    grad_sent = jnp.where(is_low, high_half, low_half).astype(BF16)
    grad_got = dp_swap(hold(grad_sent, ffn_grad), n_dp, 1)
    out_halves = hold(out_halves, ffn_grad)
    output = residual
    for step in list(range(1, n_dp)) + [0]:
        plane_sum = seq_scatter(lambda part: out_halves[step][part], n_seq)[-1]
        if step:
            plane_sum = dp_swap(plane_sum.astype(BF16), n_dp, step).astype(F32)
        output = output + plane_sum
    output = output.astype(BF16)

    residual_group = seq_gather(hold(residual_low, heads_grad), n_seq)
    grad_shared_in = hold(grad_shared_in.astype(BF16), heads_grad)
    shared_back = lax.all_to_all(
        grad_shared_in.reshape(n_all, -1, 2 * units), BOTH, split_axis=0, concat_axis=0, tiled=True
    )
    heads_grad = relative(heads_grad.reshape(n_seq, tokens, heads * VD))
    grad_out_heads = lead_dot(attended, residual_group)
    out_shard = dp_scatter(grad_out_heads, n_dp, dp_index)
    home = [
        (d * n_seq + s, s * n_dp + d) for d in range(n_dp) for s in range(n_seq)
    ]
    grad_out_weight = lax.ppermute(out_shard, BOTH, home)

    grad_o = to_sequence(heads_grad.reshape(group, heads, VD))
    prob_grad = jnp.einsum("bqhd,bkhd->bhqk", grad_o, values, preferred_element_type=F32)
    centre = jnp.sum(probs * prob_grad, axis=-1, keepdims=True)
    score_grad = (probs * (prob_grad - centre)).astype(BF16)
    query_grad = jnp.einsum("bhqk,bkhd->bqhd", score_grad, keys, preferred_element_type=F32)
    key_grad = jnp.einsum("bhqk,bqhd->bkhd", score_grad, queries, preferred_element_type=F32)
    value_grad = jnp.einsum("bhqk,bqhd->bkhd", shares, grad_o, preferred_element_type=F32)
    query_grad = to_rows((query_grad * score_scale).astype(BF16)).astype(F32)
    key_grad = to_rows((key_grad * score_scale).astype(BF16)).astype(F32)
    value_grad = to_rows(value_grad.astype(BF16))
    query_low = jnp.concatenate(
        [
            query_grad[..., :NOPE],
            rotate_back(query_grad[..., NOPE:], cosine[:, None], sine[:, None]),
        ],
        axis=-1,
    ).astype(BF16).reshape(group, q_width)
    rope_grad = rotate_back(jnp.sum(key_grad[..., NOPE:], axis=1), cosine, sine)
    expand_low = jnp.concatenate(
        [key_grad[..., :NOPE].astype(BF16), value_grad], axis=-1
    ).reshape(group, e_width)

    latent_sum = seq_scatter(
        lambda part: jnp.concatenate(
            [tail_dot(half_of(expand_low, part), weight_up), half_of(rope_grad, part)], axis=1
        ),
        n_seq,
    )[-1]
    normed_low = [tail_dot(half_of(query_low, part), weight_q).astype(BF16) for part in (0, 1)]
    normed_sum = seq_scatter(lambda part: normed_low[part], n_seq)[-1]
    unit_rows = rows_group * rms_scale(rows_group)
    gain_attn_grad = sum(
        jnp.sum(normed_low[part].astype(F32) * half_of(unit_rows, part), axis=0) for part in (0, 1)
    )
    grad_q = lead_dot(normed_group, query_low)
    grad_up = lead_dot(latent, expand_low).reshape(width, -1)
    grad_joined = hold(jnp.concatenate([grad_q, grad_up], axis=1), back_even, grad_got)
    grad_joined = dp_scatter(grad_joined, n_dp, dp_index)
    back_odd = dp_exchange(back_parts, n_dp, dp_index, odd_steps, grad_joined)
    grad_joined = grad_joined.reshape(n_seq, down_rows, joined_width)
    grad_joined = hold(grad_joined, shared_back)
    grad_joined = lax.all_to_all(grad_joined, "seq", split_axis=0, concat_axis=0, tiled=True)
    grad_q = jnp.swapaxes(grad_joined[..., :q_width], 0, 1).reshape(q_weight.shape)
    grad_up = grad_joined[..., q_width:].reshape(n_seq, kv_up.shape[0], e_width)
    grad_up = jnp.swapaxes(grad_up, 0, 1).reshape(kv_up.shape)

    latent_grad, gain_kv_grad = rms_back(latent_raw[:tokens], gain_kv, latent_sum[:, :KV_RANK])
    down_low = jnp.concatenate([latent_grad, latent_sum[:, KV_RANK:]], axis=1).astype(BF16)
    down_group = seq_gather(down_low, n_seq)
    normed_cols = normed_group.reshape(group, n_dp, n_seq, down_rows)
    normed_cols = lax.dynamic_index_in_dim(normed_cols, seq_index, 2, keepdims=False)
    grad_down = lead_dot(normed_cols.reshape(group, n_dp * down_rows), down_group)
    grad_down = dp_scatter(grad_down, n_dp, dp_index)

    in_back = back_even | back_odd
    in_back[0] = dp_block(back_parts, dp_index)
    in_back, grad_got, shared_back = hold((in_back, grad_got, shared_back), down_low)
    in_back = [in_back[step] for step in range(n_dp)]
    grad_expert_in = assemble(in_back, dp_index, expert_gate_up.shape)
    grad_got = grad_got.astype(F32)
    grad_expert_down = jnp.stack(
        [jnp.where(is_low, grad_kept, grad_got), jnp.where(is_low, grad_got, grad_kept)], axis=1
    )
    shared_back = shared_back.reshape(n_all, -1, 2, units).astype(F32)
    grad_shared_gate_up = jnp.transpose(shared_back, (1, 2, 0, 3)).reshape(shared_gate_up.shape)

    down_grad = tail_dot(down_low, weight_down)
    rows_from_norm, _ = rms_back(rows, gain_attn, normed_sum + down_grad)
    input_grad = residual_grad + rows_from_norm

    gain_attn_grad = gain_attn_grad + jnp.sum(down_grad * rows * rms_scale(rows), axis=0)
    gain_grads = jnp.concatenate(
        [
            gain_attn_grad.reshape(n_all, -1),
            gain_ffn_grad.reshape(n_all, -1),
            gain_kv_grad.reshape(n_all, -1),
        ],
        axis=1,
    )
    gain_grads = lax.all_to_all(gain_grads, BOTH, split_axis=0, concat_axis=0, tiled=True)
    gain_grads = jnp.sum(gain_grads, axis=0)
    attn_end = attn_gain.shape[0]
    ffn_end = attn_end + ffn_gain.shape[0]

    return (
        output,
        input_grad,
        gain_grads[:attn_end],
        grad_q,
        grad_down,
        gain_grads[ffn_end:],
        grad_up,
        grad_out_weight,
        gain_grads[attn_end:ffn_end],
        grad_shared_gate_up,
        grad_shared_down,
        grad_expert_in,
        grad_expert_down,
    )


def solution(mesh):
    rows = P(BOTH, None)
    return jax.shard_map(
        body,
        mesh=mesh,
        in_specs=(
            rows,
            rows,
            P(BOTH),
            rows,
            rows,
            P(BOTH),
            rows,
            rows,
            P(BOTH),
            rows,
            rows,
            P("dp", "seq", None),
            P("dp", "seq", None),
            P("dp", None),
            rows,
            P("dp", None),
        ),
        out_specs=(
            rows,
            rows,
            P(BOTH),
            rows,
            rows,
            P(BOTH),
            rows,
            rows,
            P(BOTH),
            rows,
            rows,
            P("dp", "seq", None),
            P("dp", "seq", None),
        ),
        check_vma=False,
    )
```
